256 devices in a mesh: gx: 16 (over z, core), gy: 4 (over x), gz: 4 (over y).
Axes of the slice: x: 4, y: 4, z: 8, core: 2. Of those that a mesh axis runs over, the one named last changes fastest.
Arguments:
- field: float32 [128, 1024, 2048], P('gz', 'gx', 'gy'), may hold values from -6 to 6
Outputs:
- coeffs: float32 [128, 1024, 2048], P('gz', 'gx', 'gy')
The draws below stay inside these ranges and needn't reach their ends.
All inputs are finite; a program needn't handle non-finite values.
Results may differ from the reference program's by a relative error of at most 0.000075.
Values sent between devices are 32-bit elements; how exact they have to be, the bound alone decides.
A program may use at most 128 MiB of HBM per device.

```python
import jax
import jax.numpy as jnp
from jax import lax

NZ = 128
NX = 1024
NY = 2048


def block_scale(stream_key, extent, split, smallest, top_value):
    def one(position, parts):
        heights = jax.random.uniform(jax.random.fold_in(jax.random.fold_in(stream_key, 6), position), (parts,), jnp.float32, smallest / len(split), top_value / len(split))
        return jnp.repeat(jnp.exp(heights), extent[position] // parts).reshape((-1,) + (1,) * (len(extent) - position - 1))

    loudness = one(*split[0])
    for cut in split[1:]:
        loudness = loudness * one(*cut)
    return loudness


def scatter_about(own_key, shape, width, limit, pieces=(), kind=jnp.bfloat16):
    level = block_scale(own_key, shape, pieces, -0.22, 0.18) if pieces else 1.0
    result = jax.random.normal(own_key, shape, jnp.float32) * width * level
    return jnp.minimum(jnp.maximum(result, -limit), limit).astype(kind)


def setup_inputs(seed: int = 0) -> dict:
    streams_of = jax.random.split(jax.random.key(seed), 2)
    field = scatter_about(streams_of[0], (NZ, NX, NY), 1.0, 6.0, ((0, 4), (1, 16), (2, 4)), jnp.float32)
    return dict(field=field)


lift_alpha = -1.586134342
lift_beta = -0.05298011854
lift_gamma = 0.8829110762
lift_delta = 0.4435068522
lift_zeta = 1.149604398


def cut_range(values, first_index, last_index, which_dim):
    return lax.slice_in_dim(values, first_index, last_index, axis=which_dim)


def lift_pairs(even_part, odd_part, which_dim):
    pair_count = even_part.shape[which_dim]
    first_odd = cut_range(odd_part, 0, pair_count - 1, which_dim) + lift_alpha * (cut_range(even_part, 0, pair_count - 1, which_dim) + cut_range(even_part, 1, pair_count, which_dim))
    first_even = cut_range(even_part, 1, pair_count - 1, which_dim) + lift_beta * (cut_range(first_odd, 0, pair_count - 2, which_dim) + cut_range(first_odd, 1, pair_count - 1, which_dim))
    second_odd = cut_range(first_odd, 1, pair_count - 2, which_dim) + lift_gamma * (cut_range(first_even, 0, pair_count - 3, which_dim) + cut_range(first_even, 1, pair_count - 2, which_dim))
    second_even = cut_range(first_even, 1, pair_count - 3, which_dim) + lift_delta * (cut_range(second_odd, 0, pair_count - 4, which_dim) + cut_range(second_odd, 1, pair_count - 3, which_dim))
    return second_even * lift_zeta, cut_range(second_odd, 1, pair_count - 3, which_dim) / lift_zeta


def lift_along(volume, which_dim):
    length = volume.shape[which_dim]
    extended = jnp.concatenate([cut_range(volume, length - 4, length, which_dim), volume, cut_range(volume, 0, 4, which_dim)], axis=which_dim)
    even_part = lax.slice_in_dim(extended, 0, length + 8, stride=2, axis=which_dim)
    odd_part = lax.slice_in_dim(extended, 1, length + 8, stride=2, axis=which_dim)
    low_part, high_part = lift_pairs(even_part, odd_part, which_dim)
    return jnp.stack([low_part, high_part], axis=which_dim + 1).reshape(volume.shape)


def one_level(volume):
    volume = lift_along(volume, 1)
    volume = lift_along(volume, 2)
    return lift_along(volume, 0)


def reference(field):
    level_one = one_level(field)
    level_two = one_level(level_one[::2, ::2, ::2])
    level_three = one_level(level_two[::2, ::2, ::2])
    level_two = level_two.at[::2, ::2, ::2].set(level_three)
    return level_one.at[::2, ::2, ::2].set(level_two)
```

```python
import functools

import jax
import jax.numpy as jnp
from jax import lax
from jax.experimental import pallas as pl
from jax.experimental.pallas import tpu as pltpu
from jax.sharding import PartitionSpec as P

lift_alpha = -1.586134342
lift_beta = -0.05298011854
lift_gamma = 0.8829110762
lift_delta = 0.4435068522
lift_zeta = 1.149604398
STEPS = (lift_alpha, lift_beta, lift_gamma, lift_delta)
MESH = pl.DeviceIdType.MESH
LANES = 128


def lift_lanes(values, step, masks):
    width = values.shape[1]
    odd, even, scale = masks
    for number, weight in enumerate(STEPS):
        near = pltpu.roll(values, step, 1) + pltpu.roll(values, width - step, 1)
        values = values + near * ((odd if number % 2 == 0 else even) * weight)
    return values * scale


def kernel(shape, field_ref, out_ref, two_ref, three_ref, *scratch):
    depth, rows, lanes = shape
    tiles = lanes // LANES
    refs = list(scratch)
    y_send, y_recv, x_send, x_recv, z_send, z_recv = [[refs.pop(0) for _ in range(3)] for _ in range(6)]
    load_sem, send_sem, recv_sem = refs

    here = {name: lax.axis_index(name) for name in ("gx", "gy", "gz")}
    count = {name: lax.axis_size(name) for name in ("gx", "gy", "gz")}

    def beside(name, by):
        return {name: lax.rem(here[name] + by + count[name], count[name])}

    for tile in range(tiles):
        pltpu.make_async_copy(
            field_ref.at[:, :, pl.ds(tile * LANES, LANES)], out_ref.at[:, tile], load_sem.at[tile]
        ).start()

    barrier = pltpu.get_barrier_semaphore()
    for name in ("gx", "gy", "gz"):
        for by in (-1, 1):
            pl.semaphore_signal(barrier, inc=1, device_id=beside(name, by), device_id_type=MESH)
    pl.semaphore_wait(barrier, 6)

    for tile in range(tiles):
        pltpu.make_async_copy(
            field_ref.at[:, :, pl.ds(tile * LANES, LANES)], out_ref.at[:, tile], load_sem.at[tile]
        ).wait()

    def exchange(name, index, send_ref, recv_ref):
        copies = []
        for side, by in ((0, 1), (1, -1)):
            copies.append(
                pltpu.make_async_remote_copy(
                    src_ref=send_ref.at[side],
                    dst_ref=recv_ref.at[side],
                    send_sem=send_sem.at[index, side],
                    recv_sem=recv_sem.at[index, side],
                    device_id=beside(name, by),
                    device_id_type=MESH,
                )
            )
            copies[-1].start()
        for copy in copies:
            copy.wait()

    a, b, g, e = STEPS
    for level in range(3):
        step = 2**level
        planes, height = depth // step, rows // step
        body = (out_ref, two_ref, three_ref)[level]
        flat = body.reshape(planes * tiles * height, LANES)

        window = 4 * step
        lane = lax.broadcasted_iota(jnp.int32, (height, LANES), 1)

        def pack(plane, held):
            to_right, to_left = held
            mine = lane // window == plane
            tail = pltpu.roll(body[plane, tiles - 1], lax.rem(plane * window + window, LANES), 1)
            head = pltpu.roll(body[plane, 0], plane * window, 1)
            return jnp.where(mine, tail, to_right), jnp.where(mine, head, to_left)

        nothing = jnp.zeros((height, LANES), jnp.float32)
        to_right, to_left = lax.fori_loop(0, planes, pack, (nothing, nothing))
        y_send[level][0] = to_right
        y_send[level][1] = to_left
        exchange("gy", 3 * level, y_send[level], y_recv[level])

        wide = lax.broadcasted_iota(jnp.int32, (8, lanes + LANES), 1)
        phase = wide % (2 * step)
        odd = (phase == step).astype(jnp.float32)
        even = (phase == 0).astype(jnp.float32)
        scale = jnp.where(phase == 0, lift_zeta, jnp.where(phase == step, 1.0 / lift_zeta, 1.0))
        first_half = lax.broadcasted_iota(jnp.int32, (8, LANES), 1) >= LANES // 2

        def along_y(plane, _):
            for top in range(0, height, 8):
                part = pl.ds(top, 8)
                left = pltpu.roll(y_recv[level][0, part, :], lax.rem(2 * LANES - window - plane * window, LANES), 1)
                right = pltpu.roll(y_recv[level][1, part, :], lax.rem(LANES - plane * window, LANES), 1)
                halo = jnp.where(first_half, left, right)
                values = jnp.concatenate([body[plane, tile, part, :] for tile in range(tiles)] + [halo], axis=1)
                values = lift_lanes(values, step, (odd, even, scale))
                for tile in range(tiles):
                    body[plane, tile, part, :] = values[:, tile * LANES : (tile + 1) * LANES]
            return 0

        lax.fori_loop(0, planes, along_y, 0)

        def row(tile, number):
            return flat[pl.ds(tile * height + number, planes, stride=tiles * height), :]

        for tile in range(tiles):
            s2, d2, s1, d1 = [row(tile, height - 4 + number) for number in range(4)]
            x_send[level][0, 0, tile] = d1 + a * s1
            x_send[level][0, 1, tile] = s1 + b * (d2 + a * (s2 + s1))
            s0, d0, s1 = [row(tile, number) for number in range(3)]
            x_send[level][1, 0, tile] = s0
            x_send[level][1, 1, tile] = s0 + b * (d0 + a * (s0 + s1))
        exchange("gx", 3 * level + 1, x_send[level], x_recv[level])

        half = height // 2
        pair = lax.broadcasted_iota(jnp.int32, (half, LANES), 0)

        def along_x(plane, _):
            for tile in range(tiles):
                start = (plane * tiles + tile) * height
                s = flat[pl.ds(start, half, stride=2), :]
                d = flat[pl.ds(start + 1, half, stride=2), :]
                left_a = x_recv[level][0, 0, tile, pl.ds(plane, 1), :]
                left_b = x_recv[level][0, 1, tile, pl.ds(plane, 1), :]
                right_c = x_recv[level][1, 0, tile, pl.ds(plane, 1), :]
                right_e = x_recv[level][1, 1, tile, pl.ds(plane, 1), :]

                def after(values, last):
                    return jnp.where(pair == half - 1, last, pltpu.roll(values, half - 1, 0))

                def before(values, first):
                    return jnp.where(pair == 0, first, pltpu.roll(values, 1, 0))

                d_before = left_a + a * s[:1]
                d = d + a * (s + after(s, right_c))
                s_after = right_e + b * d[half - 1 :]
                s_before = left_b + b * d_before
                s = s + b * (before(d, d_before) + d)
                d_before = d_before + g * (s_before + s[:1])
                d = d + g * (s + after(s, s_after))
                s = s + e * (before(d, d_before) + d)
                flat[pl.ds(start, half, stride=2), :] = s * lift_zeta
                flat[pl.ds(start + 1, half, stride=2), :] = d * (1.0 / lift_zeta)
            return 0

        lax.fori_loop(0, planes, along_x, 0)

        for tile in range(tiles):
            s2, d2, s1, d1 = [body[planes - 4 + number, tile] for number in range(4)]
            z_send[level][0, 0, tile] = d1 + a * s1
            z_send[level][0, 1, tile] = s1 + b * (d2 + a * (s2 + s1))
            s0, d0, s1 = [body[number, tile] for number in range(3)]
            z_send[level][1, 0, tile] = s0
            z_send[level][1, 1, tile] = s0 + b * (d0 + a * (s0 + s1))
        exchange("gz", 3 * level + 2, z_send[level], z_recv[level])

        def along_z(block, _):
            tile = block // (height // 8)
            part = pl.ds(pl.multiple_of((block % (height // 8)) * 8, 8), 8)
            pairs = planes // 2
            s = [body[2 * number, tile, part, :] for number in range(pairs)]
            d = [body[2 * number + 1, tile, part, :] for number in range(pairs)]
            left_a = z_recv[level][0, 0, tile, part, :]
            left_b = z_recv[level][0, 1, tile, part, :]
            right_c = z_recv[level][1, 0, tile, part, :]
            right_e = z_recv[level][1, 1, tile, part, :]
            d_before = left_a + a * s[0]
            s_before = left_b + b * d_before
            around = s + [right_c]
            d = [d[i] + a * (around[i] + around[i + 1]) for i in range(pairs)]
            s_after = right_e + b * d[-1]
            around = [d_before] + d
            s = [s[i] + b * (around[i] + around[i + 1]) for i in range(pairs)]
            d_before = d_before + g * (s_before + s[0])
            around = s + [s_after]
            d = [d[i] + g * (around[i] + around[i + 1]) for i in range(pairs)]
            around = [d_before] + d
            s = [s[i] + e * (around[i] + around[i + 1]) for i in range(pairs)]
            for number in range(pairs):
                body[2 * number, tile, part, :] = s[number] * lift_zeta
                body[2 * number + 1, tile, part, :] = d[number] * (1.0 / lift_zeta)
            return 0

        lax.fori_loop(0, tiles * height // 8, along_z, 0)

        if level < 2:
            inner = (two_ref, three_ref)[level]

            def pick(plane, _):
                for tile in range(tiles):
                    start = (2 * plane * tiles + tile) * height
                    inner[plane, tile] = flat[pl.ds(start, half, stride=2), :]
                return 0

            lax.fori_loop(0, planes // 2, pick, 0)

    for level in (1, 0):
        step = 2**level
        planes, height = depth // step, rows // step
        half = height // 2
        body = (out_ref, two_ref)[level]
        inner = (two_ref, three_ref)[level]
        flat = body.reshape(planes * tiles * height, LANES)
        keep = lax.broadcasted_iota(jnp.int32, (half, LANES), 1) % (2 * step) == 0

        def place(plane, _):
            for tile in range(tiles):
                start = (2 * plane * tiles + tile) * height
                where = pl.ds(start, half, stride=2)
                flat[where, :] = jnp.where(keep, inner[plane, tile], flat[where, :])
            return 0

        lax.fori_loop(0, planes // 2, place, 0)


def write_out(held_ref, out_ref, sem):
    tiles = held_ref.shape[1]
    copies = [
        pltpu.make_async_copy(held_ref.at[:, tile], out_ref.at[:, :, pl.ds(tile * LANES, LANES)], sem.at[tile])
        for tile in range(tiles)
    ]
    for copy in copies:
        copy.start()
    for copy in copies:
        copy.wait()


def local(field):
    depth, rows, lanes = field.shape
    tiles = lanes // LANES
    sizes = [(depth >> level, rows >> level) for level in range(3)]
    f32 = jnp.float32
    scratch = []
    for _ in range(2):
        scratch += [pltpu.VMEM((2, height, LANES), f32) for _, height in sizes]
    for _ in range(2):
        scratch += [pltpu.VMEM((2, 2, tiles, planes, LANES), f32) for planes, _ in sizes]
    for _ in range(2):
        scratch += [pltpu.VMEM((2, 2, tiles, height, LANES), f32) for _, height in sizes]
    held = pl.pallas_call(
        functools.partial(kernel, field.shape),
        out_shape=jax.ShapeDtypeStruct((depth, tiles, rows, LANES), f32),
        in_specs=[pl.BlockSpec(memory_space=pl.ANY)],
        out_specs=pl.BlockSpec(memory_space=pltpu.VMEM),
        scratch_shapes=[
            pltpu.VMEM((sizes[1][0], tiles, sizes[1][1], LANES), f32),
            pltpu.VMEM((sizes[2][0], tiles, sizes[2][1], LANES), f32),
            *scratch,
            pltpu.SemaphoreType.DMA((tiles,)),
            pltpu.SemaphoreType.DMA((9, 2)),
            pltpu.SemaphoreType.DMA((9, 2)),
        ],
        compiler_params=pltpu.CompilerParams(
            collective_id=0, has_side_effects=True, vmem_limit_bytes=32 * 2**20
        ),
        name="lift",
    )(field)
    return pl.pallas_call(
        write_out,
        out_shape=jax.ShapeDtypeStruct(field.shape, f32),
        in_specs=[pl.BlockSpec(memory_space=pltpu.VMEM)],
        out_specs=pl.BlockSpec(memory_space=pl.ANY),
        scratch_shapes=[pltpu.SemaphoreType.DMA((tiles,))],
        name="write_out",
    )(held)


def solution(mesh):
    placed = (P("gz", "gx", "gy"),)
    return jax.shard_map(
        local, mesh=mesh, in_specs=placed, out_specs=P("gz", "gx", "gy"), check_vma=False
    )
```

```python
import functools

import jax
import jax.numpy as jnp
import numpy as np
from jax import lax
from jax.experimental import pallas as pl
from jax.experimental.pallas import tpu as pltpu
from jax.sharding import PartitionSpec as P

A = -1.586134342
B = -0.05298011854
G = 0.8829110762
E = 0.4435068522
Z = 1.149604398
MESH = pl.DeviceIdType.MESH
LANES = 128
TILES = 4
LEVELS = 3
SIDES = (0, 1)
f32, bf16 = jnp.float32, jnp.bfloat16


def filter_taps():
    u = np.eye(64)
    s, d = u[0::2].copy(), u[1::2].copy()
    d += A * (s + np.roll(s, -1, 0))
    s += B * (np.roll(d, 1, 0) + d)
    d += G * (s + np.roll(s, -1, 0))
    s += E * (np.roll(d, 1, 0) + d)
    low, high = s[16] * Z, d[16] / Z
    return [float(low[32 + o]) for o in range(5)], [float(high[33 + o]) for o in range(5)]


LOW, HIGH = filter_taps()

FROM_LEFT = {
    0: (Z * (B + E * (1 + 3 * G * B)), Z * E * G),
    1: (G * B / Z, 0.0),
    2: (Z * E * G * B, 0.0),
}
FROM_RIGHT = {
    -4: (Z * E * G * B * A, 0.0),
    -3: (G * B * A / Z, 0.0),
    -2: (Z * (B * A + E * (G * B * A + A * (1 + 2 * G * B))), Z * E * G),
    -1: (A * (1 + 2 * G * B) / Z, G / Z),
}


def tap_weights(position, target, step):
    apart = jnp.abs(position - target)
    phase = target % (2 * step)
    low = jnp.zeros(position.shape, f32)
    high = jnp.zeros(position.shape, f32)
    for o in range(5):
        low = jnp.where(apart == o * step, LOW[o], low)
        if o < 4:
            high = jnp.where(apart == o * step, HIGH[o], high)
    rest = jnp.where(apart == 0, 1.0, 0.0) if step > 1 else high
    return jnp.where(phase == 0, low, jnp.where(phase == step, high, rest))


def parts_of(values):
    top = values.astype(bf16)
    return top, (values - top.astype(f32)).astype(bf16)


def encode_end(s2, d2, s1, d1):
    return d1 + A * s1, s1 + B * (d2 + A * (s2 + s1))


def encode_start(s0, d0, s1):
    return s0, s0 + B * (d0 + A * (s0 + s1))


def lift_list(u, halo=None):
    s, d = list(u[0::2]), list(u[1::2])
    count = len(s)
    d_before = A * s[0]
    if halo is not None:
        d_before = d_before + halo[0]
    s_before = B * d_before
    if halo is not None:
        s_before = s_before + halo[1]
    for i in range(count - 1):
        d[i] = d[i] + A * (s[i] + s[i + 1])
    last = s[-1] if halo is None else s[-1] + halo[2]
    d[-1] = d[-1] + A * last
    s_after = B * d[-1]
    if halo is not None:
        s_after = s_after + halo[3]
    around = [d_before] + d
    s = [s[i] + B * (around[i] + around[i + 1]) for i in range(count)]
    d_before = d_before + G * (s_before + s[0])
    around = s + [s_after]
    d = [d[i] + G * (around[i] + around[i + 1]) for i in range(count)]
    around = [d_before] + d
    s = [s[i] + E * (around[i] + around[i + 1]) for i in range(count)]
    out = []
    for i in range(count):
        out += [s[i] * Z, d[i] * (1.0 / Z)]
    return out


def lift_rows(flat, start, height):
    half = height // 2
    pair = lax.broadcasted_iota(jnp.int32, (half, LANES), 0)
    even, odd = pl.ds(start, half, stride=2), pl.ds(start + 1, half, stride=2)
    s, d = flat[even, :], flat[odd, :]

    def after(values, last):
        return jnp.where(pair == half - 1, last, pltpu.roll(values, half - 1, 0))

    def before(values, first):
        return jnp.where(pair == 0, first, pltpu.roll(values, 1, 0))

    d_before = A * s[:1]
    d = d + A * (s + after(s, 0.0))
    s_after = B * d[half - 1 :]
    s_before = B * d_before
    s = s + B * (before(d, d_before) + d)
    d_before = d_before + G * (s_before + s[:1])
    d = d + G * (s + after(s, s_after))
    s = s + E * (before(d, d_before) + d)
    flat[even, :] = s * Z
    flat[odd, :] = d * (1.0 / Z)


def lift_lanes(tiles, ext, weights):
    first = lax.broadcasted_iota(jnp.int32, tiles[0].shape, 1) < LANES // 2
    out = []
    for block in range(2):
        main = jnp.concatenate([tiles[2 * block], tiles[2 * block + 1]], axis=1)
        beside = jnp.where(first, tiles[2], ext) if block == 0 else jnp.where(first, ext, tiles[1])
        main_top, main_low = parts_of(main)
        side_top, side_low = parts_of(beside)
        stacked = jnp.concatenate([main_top, main_low, main_top, side_top, side_low, side_top], axis=1)
        result = jnp.dot(stacked, weights[...], preferred_element_type=f32)
        out += [result[:, :LANES], result[:, LANES:]]
    return out


def sizes_of(shape, level):
    return shape[0] >> level, shape[1] >> level


def kernel(shape, field_ref, out_ref, *scratch):
    depth, rows, _ = shape
    refs = list(scratch)
    take = lambda: refs.pop(0)
    bodies = [out_ref, take(), take()]
    load_sem, send_sem, recv_sem = take(), take(), take()
    y_weights, far_weights, z_weights = [[take() for _ in range(LEVELS)] for _ in range(3)]
    per_level = [{} for _ in range(LEVELS)]
    for level in range(LEVELS):
        for name in ("zs", "zr", "ze", "xs", "xr", "xe", "xl", "es", "er", "ys", "yr", "zys", "zyr", "xys", "xyr", "cr"):
            per_level[level][name] = take()

    here = {name: lax.axis_index(name) for name in ("gx", "gy", "gz")}
    count = {name: lax.axis_size(name) for name in ("gx", "gy", "gz")}

    def beside(**by):
        return {name: lax.rem(here[name] + way + count[name], count[name]) for name, way in by.items()}

    loads = [
        pltpu.make_async_copy(
            field_ref.at[:, :, pl.ds(tile * LANES, LANES)], out_ref.at[:, tile], load_sem.at[tile]
        )
        for tile in range(TILES)
    ]
    for load in loads:
        load.start()

    barrier = pltpu.get_barrier_semaphore()
    for x in (-1, 0, 1):
        for y in (-1, 0, 1):
            for z in (-1, 0, 1):
                if (x, y, z) != (0, 0, 0):
                    pl.semaphore_signal(barrier, inc=1, device_id=beside(gx=x, gy=y, gz=z), device_id_type=MESH)

    def make_weights(level):
        step = 2**level
        window = 4 * step
        row = lax.broadcasted_iota(jnp.int32, (2 * LANES, 2 * LANES), 0)
        col = lax.broadcasted_iota(jnp.int32, (2 * LANES, 2 * LANES), 1)
        near, low = parts_of(tap_weights(row, col, step))
        weights = y_weights[level]
        weights[0 : 2 * LANES] = near
        weights[2 * LANES : 4 * LANES] = near
        weights[4 * LANES : 6 * LANES] = low
        side = row[:LANES]
        position = jnp.where(side < LANES // 2, 2 * LANES + side, side - LANES)
        near, low = parts_of(tap_weights(position, col[:LANES], step))
        weights[6 * LANES : 7 * LANES] = near
        weights[7 * LANES : 8 * LANES] = near
        weights[8 * LANES : 9 * LANES] = low
        left = row < LANES
        position = jnp.where(left, row % window - window, LANES + row % window)
        taps = tap_weights(position, col % LANES, step)
        near, low = parts_of(jnp.where(left == (col < LANES), taps, 0.0))
        weights = far_weights[level]
        weights[0 : 2 * LANES] = near
        weights[2 * LANES : 4 * LANES] = near
        weights[4 * LANES : 6 * LANES] = low
        row, col = row[:LANES, :LANES], col[:LANES, :LANES]
        taps = tap_weights(row // window, col // window, 1)
        near, low = parts_of(jnp.where(row % window == col % window, taps, 0.0))
        weights = z_weights[level]
        weights[0:LANES] = near
        weights[LANES : 2 * LANES] = near
        weights[2 * LANES : 3 * LANES] = low

    make_weights(0)
    for load in loads:
        load.wait()

    sends = []
    sub = lax.broadcasted_iota(jnp.int32, (8, LANES), 0)
    lane8 = lax.broadcasted_iota(jnp.int32, (8, LANES), 1)

    def per_row(table, layer):
        values = jnp.zeros((8, LANES), f32)
        for number, weights in table.items():
            if weights[layer] != 0.0:
                values = jnp.where(sub == number % 8, weights[layer], values)
        return values

    for level in range(LEVELS):
        step = 2**level
        window = 4 * step
        planes, height = depth // step, rows // step
        body = bodies[level]
        flat = body.reshape(planes * TILES * height, LANES)
        r = per_level[level]
        arrivals = {}

        def send(key, number, source, target, **by):
            copy = pltpu.make_async_remote_copy(
                src_ref=source,
                dst_ref=target,
                send_sem=send_sem.at[level, number],
                recv_sem=recv_sem.at[level, number],
                device_id=beside(**by),
                device_id_type=MESH,
            )
            if level == 0 and number == 0:
                pl.semaphore_wait(barrier, 26)
            copy.start()
            sends.append(copy)
            arrivals.setdefault(key, []).append(copy)

        way = (1, -1)
        zs, xs, es = r["zs"], r["xs"], r["es"]
        def encode_z(tile, _):
            end = encode_end(*[body[planes - 4 + number, tile] for number in range(4)])
            start = encode_start(*[body[number, tile] for number in range(3)])
            for k in range(2):
                zs[0, k, tile] = end[k]
                zs[1, k, tile] = start[k]
            return 0

        lax.fori_loop(0, TILES, encode_z, 0)
        for side in SIDES:
            send("z", side, zs.at[side], r["zr"].at[side], gz=way[side])

        xs_flat = xs.reshape(2 * planes * 8, LANES)
        for tile in range(TILES):
            def at(number):
                return flat[pl.ds(tile * height + number, planes, stride=TILES * height), :]

            end = encode_end(*[at(height - 4 + number) for number in range(4)])
            start = encode_start(*[at(number) for number in range(3)])
            for k in range(2):
                xs_flat[pl.ds(k * TILES + tile, planes, stride=8), :] = end[k]
                xs_flat[pl.ds(planes * 8 + k * TILES + tile, planes, stride=8), :] = start[k]
        for side in SIDES:
            send("x", 2 + side, xs.at[side], r["xr"].at[side], gx=way[side])

        for side in SIDES:
            end = encode_end(*[xs[side, planes - 4 + number] for number in range(4)])
            start = encode_start(*[xs[side, number] for number in range(3)])
            for k in range(2):
                es[side, 0, k] = end[k]
                es[side, 1, k] = start[k]
        for sx in SIDES:
            for sz in SIDES:
                send("e", 4 + 2 * sx + sz, es.at[sx, sz], r["er"].at[sx, sz], gx=way[sx], gz=way[sz])
                for sy in SIDES:
                    send(
                        "c",
                        8 + 4 * sx + 2 * sz + sy,
                        es.at[sx, sz],
                        r["cr"].at[sx, sz, sy],
                        gx=way[sx],
                        gz=way[sz],
                        gy=way[sy],
                    )

        lane = lax.broadcasted_iota(jnp.int32, (height, LANES), 1)

        def pack(plane, held):
            to_right, to_left, x_right, x_left = held
            tail_by = lax.rem(plane * window + window, LANES)
            head_by = plane * window
            mine = lane // window == plane
            to_right = jnp.where(mine, pltpu.roll(body[plane, TILES - 1], tail_by, 1), to_right)
            to_left = jnp.where(mine, pltpu.roll(body[plane, 0], head_by, 1), to_left)
            mine = lane8 // window == plane
            x_right = tuple(jnp.where(mine, pltpu.roll(xs[sx, plane], tail_by, 1), x_right[sx]) for sx in SIDES)
            x_left = tuple(jnp.where(mine, pltpu.roll(xs[sx, plane], head_by, 1), x_left[sx]) for sx in SIDES)
            return to_right, to_left, x_right, x_left

        none = jnp.zeros((height, LANES), f32)
        none8 = jnp.zeros((8, LANES), f32)
        to_right, to_left, x_right, x_left = lax.fori_loop(
            0, planes, pack, (none, none, (none8, none8), (none8, none8))
        )
        r["ys"][0], r["ys"][1] = to_right, to_left
        for sx in SIDES:
            r["xys"][0, sx], r["xys"][1, sx] = x_right[sx], x_left[sx]
        groups = height // 8
        for sz in SIDES:
            tail = head = none8
            for k in range(2):
                for group in range(groups):
                    slot = k * groups + group
                    mine = lane8 // window == slot
                    part = pl.ds(group * 8, 8)
                    by = (slot * window + window) % LANES
                    tail = jnp.where(mine, pltpu.roll(zs[sz, k, TILES - 1, part, :], by, 1), tail)
                    head = jnp.where(mine, pltpu.roll(zs[sz, k, 0, part, :], slot * window, 1), head)
            r["zys"][0, sz], r["zys"][1, sz] = tail, head
        for sy in SIDES:
            send("y", 16 + sy, r["ys"].at[sy], r["yr"].at[sy], gy=way[sy])
            for s in SIDES:
                send("xy", 18 + 2 * sy + s, r["xys"].at[sy, s], r["xyr"].at[sy, s], gy=way[sy], gx=way[s])
                send("zy", 22 + 2 * sy + s, r["zys"].at[sy, s], r["zyr"].at[sy, s], gy=way[sy], gz=way[s])

        if level == 0:
            for other in range(1, LEVELS):
                make_weights(other)

        def own_x(plane, _):
            for tile in range(TILES):
                lift_rows(flat, (plane * TILES + tile) * height, height)
            return 0

        lax.fori_loop(0, planes, own_x, 0)

        def own_z(block, _):
            tile = block // groups
            part = pl.ds(pl.multiple_of((block % groups) * 8, 8), 8)
            lifted = lift_list([body[plane, tile, part, :] for plane in range(planes)])
            for plane in range(planes):
                body[plane, tile, part, :] = lifted[plane]
            return 0

        lax.fori_loop(0, TILES * groups, own_z, 0)

        chunk = min(planes, 512 // height)
        weights = y_weights[level]

        def own_y(number, _):
            where = pl.ds(number * chunk, chunk)
            tiles = [body[where, tile].reshape(chunk * height, LANES) for tile in range(TILES)]
            lifted = lift_lanes(tiles, jnp.zeros((chunk * height, LANES), f32), weights)
            for tile in range(TILES):
                body[where, tile] = lifted[tile].reshape(chunk, height, LANES)
            return 0

        lax.fori_loop(0, planes // chunk, own_y, 0)

        for copy in arrivals["y"]:
            copy.wait_recv()
        packed = []
        for sy in SIDES:
            held = r["yr"].at[sy]
            lift_rows(held, 0, height)
            top, low = parts_of(held[...])
            stacked = jnp.concatenate([top, low, top], axis=1)
            packed.append(jnp.dot(stacked, z_weights[level][...], preferred_element_type=f32))
        packed = [part for values in packed for part in (values,)]
        tops = [values.astype(bf16).astype(f32) for values in packed]
        lows = [values - top for values, top in zip(packed, tops)]
        far = far_weights[level]
        r["ys"]

        def far_y(number, _):
            stacks = []
            for inner in range(chunk):
                mine = lane // window == number * chunk + inner
                top = [jnp.where(mine, values, 0.0).astype(bf16) for values in tops]
                low = [jnp.where(mine, values, 0.0).astype(bf16) for values in lows]
                stacks.append(jnp.concatenate(top + low + top, axis=1))
            added = jnp.dot(jnp.concatenate(stacks, axis=0), far[...], preferred_element_type=f32)
            where = pl.ds(number * chunk, chunk)
            body[where, 0] = body[where, 0] + added[:, :LANES].reshape(chunk, height, LANES)
            body[where, TILES - 1] = body[where, TILES - 1] + added[:, LANES:].reshape(chunk, height, LANES)
            return 0

        lax.fori_loop(0, planes // chunk, far_y, 0)

        for key in ("x", "e", "c", "xy"):
            for copy in arrivals[key]:
                copy.wait_recv()
        xr, xe, xl = r["xr"], r["xe"], r["xl"]
        last_half = lane8 >= LANES // 2

        def unpack_x(plane, _):
            left_by = lax.rem(2 * LANES - window - plane * window, LANES)
            right_by = lax.rem(LANES - plane * window, LANES)
            for sx in SIDES:
                left = pltpu.roll(pltpu.roll(r["xyr"][0, sx], 5, 0), left_by, 1)
                right = pltpu.roll(r["xyr"][1, sx], right_by, 1)
                xe[sx, plane] = jnp.where(last_half, left, right)
            return 0

        lax.fori_loop(0, planes, unpack_x, 0)
        for sx in SIDES:
            halo = [r["er"][sx, sz, k] for sz in SIDES for k in range(2)]
            lifted = lift_list([xr[sx, plane] for plane in range(planes)], halo)
            for plane in range(planes):
                xr[sx, plane] = lifted[plane]
            halo = [
                jnp.where(last_half, pltpu.roll(r["cr"][sx, sz, 0, k], 5, 0), r["cr"][sx, sz, 1, k])
                for sz in SIDES
                for k in range(2)
            ]
            lifted = lift_list([xe[sx, plane] for plane in range(planes)], halo)
            for plane in range(planes):
                xe[sx, plane] = lifted[plane]
        xr_flat = xr.reshape(2 * planes * 8, LANES)
        xe_flat = xe.reshape(2 * planes * 8, LANES)
        for k in range(2):
            tiles = [xr_flat[pl.ds(k * TILES + tile, 2 * planes, stride=8), :] for tile in range(TILES)]
            ext = xe_flat[pl.ds(k * TILES, 2 * planes, stride=8), :]
            lifted = lift_lanes(tiles, ext, weights)
            for tile in range(TILES):
                xl[k, tile] = lifted[tile]
        left_rows = [per_row(FROM_LEFT, layer) for layer in range(2)]
        right_rows = [per_row(FROM_RIGHT, layer) for layer in range(2)]

        def far_x(plane, _):
            for tile in range(TILES):
                for side, weigh, top in ((0, left_rows, 0), (1, right_rows, height - 8)):
                    part = pl.ds(top, 8)
                    at = pl.ds(side * planes + plane, 1)
                    added = weigh[0] * xl[0, tile, at, :] + weigh[1] * xl[1, tile, at, :]
                    body[plane, tile, part, :] = body[plane, tile, part, :] + added
            return 0

        lax.fori_loop(0, planes, far_x, 0)

        for key in ("zy", "z"):
            for copy in arrivals[key]:
                copy.wait_recv()
        zr, ze = r["zr"], r["ze"]
        zr_flat = zr.reshape(4 * TILES * height, LANES)
        ze_flat = ze.reshape(4 * height, LANES)
        for sz in SIDES:
            for k in range(2):
                for group in range(groups):
                    slot = k * groups + group
                    left = pltpu.roll(r["zyr"][0, sz], (2 * LANES - window - slot * window) % LANES, 1)
                    right = pltpu.roll(r["zyr"][1, sz], (LANES - slot * window) % LANES, 1)
                    ze[sz, k, pl.ds(group * 8, 8), :] = jnp.where(last_half, left, right)

        def far_z_rows(layer, _):
            for tile in range(TILES):
                lift_rows(zr_flat, (layer * TILES + tile) * height, height)
            lift_rows(ze_flat, layer * height, height)
            return 0

        lax.fori_loop(0, 4, far_z_rows, 0)
        tiles = [zr[:, :, tile].reshape(4 * height, LANES) for tile in range(TILES)]
        lifted = lift_lanes(tiles, ze[...].reshape(4 * height, LANES), weights)
        for tile in range(TILES):
            layers = [lifted[tile][k * height : (k + 1) * height] for k in range(4)]
            for first, table in ((0, FROM_LEFT), (2, FROM_RIGHT)):
                for number, (one, two) in table.items():
                    plane = number % planes
                    added = one * layers[first]
                    if two != 0.0:
                        added = added + two * layers[first + 1]
                    body[plane, tile] = body[plane, tile] + added

        if level < LEVELS - 1:
            inner = bodies[level + 1]

            def pick(plane, _):
                for tile in range(TILES):
                    start = (2 * plane * TILES + tile) * height
                    inner[plane, tile] = flat[pl.ds(start, height // 2, stride=2), :]
                return 0

            lax.fori_loop(0, planes // 2, pick, 0)

    for level in (1, 0):
        step = 2**level
        planes, height = depth // step, rows // step
        half = height // 2
        inner = bodies[level + 1]
        flat = bodies[level].reshape(planes * TILES * height, LANES)
        keep = lax.broadcasted_iota(jnp.int32, (half, LANES), 1) % (2 * step) == 0

        def place(plane, _):
            for tile in range(TILES):
                start = (2 * plane * TILES + tile) * height
                where = pl.ds(start, half, stride=2)
                flat[where, :] = jnp.where(keep, inner[plane, tile], flat[where, :])
            return 0

        lax.fori_loop(0, planes // 2, place, 0)

    for copy in sends:
        copy.wait_send()


def write_out(held_ref, out_ref, sem):
    copies = [
        pltpu.make_async_copy(held_ref.at[:, tile], out_ref.at[:, :, pl.ds(tile * LANES, LANES)], sem.at[tile])
        for tile in range(TILES)
    ]
    for copy in copies:
        copy.start()
    for copy in copies:
        copy.wait()


def local(field):
    depth, rows, lanes = field.shape
    vmem = pltpu.VMEM
    sizes = [(depth >> level, rows >> level) for level in range(LEVELS)]
    scratch = [vmem((planes, TILES, height, LANES), f32) for planes, height in sizes[1:]]
    scratch += [
        pltpu.SemaphoreType.DMA((TILES,)),
        pltpu.SemaphoreType.DMA((LEVELS, 26)),
        pltpu.SemaphoreType.DMA((LEVELS, 26)),
    ]
    for shape in ((9 * LANES, 2 * LANES), (6 * LANES, 2 * LANES), (3 * LANES, LANES)):
        scratch += [vmem(shape, bf16)] * LEVELS
    for planes, height in sizes:
        shapes = [(2, 2, TILES, height)] * 2 + [(2, 2, height)]
        shapes += [(2, planes, 8)] * 3 + [(2, TILES, 2 * planes)]
        shapes += [(2, 2, 2, 8)] * 2 + [(2, height)] * 2 + [(2, 2, 8)] * 4 + [(2, 2, 2, 2, 8)]
        scratch += [vmem((*shape, LANES), f32) for shape in shapes]
    held = pl.pallas_call(
        functools.partial(kernel, field.shape),
        out_shape=jax.ShapeDtypeStruct((depth, TILES, rows, LANES), f32),
        in_specs=[pl.BlockSpec(memory_space=pltpu.HBM)],
        out_specs=pl.BlockSpec(memory_space=pltpu.VMEM),
        scratch_shapes=scratch,
        compiler_params=pltpu.CompilerParams(
            collective_id=0, has_side_effects=True, vmem_limit_bytes=40 * 2**20
        ),
        name="lift",
    )(field)
    return pl.pallas_call(
        write_out,
        out_shape=jax.ShapeDtypeStruct(field.shape, f32),
        in_specs=[pl.BlockSpec(memory_space=pltpu.VMEM)],
        out_specs=pl.BlockSpec(memory_space=pltpu.HBM),
        scratch_shapes=[pltpu.SemaphoreType.DMA((TILES,))],
        compiler_params=pltpu.CompilerParams(vmem_limit_bytes=8 * 2**20),
        name="write_out",
    )(held)


def solution(mesh):
    placed = (P("gz", "gx", "gy"),)
    return jax.shard_map(
        local, mesh=mesh, in_specs=placed, out_specs=P("gz", "gx", "gy"), check_vma=False
    )
```

```python
import functools

import jax
import jax.numpy as jnp
import numpy as np
from jax import lax
from jax.experimental import pallas as pl
from jax.experimental.pallas import tpu as pltpu
from jax.sharding import PartitionSpec as P

A = -1.586134342
B = -0.05298011854
G = 0.8829110762
E = 0.4435068522
Z = 1.149604398
MESH = pl.DeviceIdType.MESH
LANES = 128
TILES = 4
LEVELS = 3
SIDES = (0, 1)
f32, bf16 = jnp.float32, jnp.bfloat16


def filter_taps():
    u = np.eye(64)
    s, d = u[0::2].copy(), u[1::2].copy()
    d += A * (s + np.roll(s, -1, 0))
    s += B * (np.roll(d, 1, 0) + d)
    d += G * (s + np.roll(s, -1, 0))
    s += E * (np.roll(d, 1, 0) + d)
    low, high = s[16] * Z, d[16] / Z
    return [float(low[32 + o]) for o in range(5)], [float(high[33 + o]) for o in range(5)]


LOW, HIGH = filter_taps()

FROM_LEFT = {
    0: (Z * (B + E * (1 + 3 * G * B)), Z * E * G),
    1: (G * B / Z, 0.0),
    2: (Z * E * G * B, 0.0),
}
FROM_RIGHT = {
    -4: (Z * E * G * B * A, 0.0),
    -3: (G * B * A / Z, 0.0),
    -2: (Z * (B * A + E * (G * B * A + A * (1 + 2 * G * B))), Z * E * G),
    -1: (A * (1 + 2 * G * B) / Z, G / Z),
}


def cell_of(level, tile, lane):
    if level == 0:
        return tile * LANES + lane
    if level == 1:
        turn = lane & 1
        return ((tile + 2 * turn) * LANES + lane - turn) >> 1
    turn = lane & 3
    return (((turn >> 1) + 2 * (turn & 1)) * LANES + lane - turn) >> 2


def tap_weights(position, target):
    apart = jnp.abs(position - target)
    low = jnp.zeros(position.shape, f32)
    high = jnp.zeros(position.shape, f32)
    for o in range(5):
        low = jnp.where(apart == o, LOW[o], low)
        if o < 4:
            high = jnp.where(apart == o, HIGH[o], high)
    return jnp.where((target & 1) == 0, low, high)


def parts_of(values):
    top = values.astype(bf16)
    return top, (values - top.astype(f32)).astype(bf16)


def encode_end(s2, d2, s1, d1):
    return d1 + A * s1, s1 + B * (d2 + A * (s2 + s1))


def encode_start(s0, d0, s1):
    return s0, s0 + B * (d0 + A * (s0 + s1))


def lift_list(u, halo=None):
    s, d = list(u[0::2]), list(u[1::2])
    count = len(s)
    d_before = A * s[0]
    if halo is not None:
        d_before = d_before + halo[0]
    s_before = B * d_before
    if halo is not None:
        s_before = s_before + halo[1]
    for i in range(count - 1):
        d[i] = d[i] + A * (s[i] + s[i + 1])
    last = s[-1] if halo is None else s[-1] + halo[2]
    d[-1] = d[-1] + A * last
    s_after = B * d[-1]
    if halo is not None:
        s_after = s_after + halo[3]
    around = [d_before] + d
    s = [s[i] + B * (around[i] + around[i + 1]) for i in range(count)]
    d_before = d_before + G * (s_before + s[0])
    around = s + [s_after]
    d = [d[i] + G * (around[i] + around[i + 1]) for i in range(count)]
    around = [d_before] + d
    s = [s[i] + E * (around[i] + around[i + 1]) for i in range(count)]
    out = []
    for i in range(count):
        out += [s[i] * Z, d[i] * (1.0 / Z)]
    return out


def lift_rows(flat, start, height):
    half = height // 2
    pair = lax.broadcasted_iota(jnp.int32, (half, LANES), 0)
    even, odd = pl.ds(start, half, stride=2), pl.ds(start + 1, half, stride=2)
    s, d = flat[even, :], flat[odd, :]

    def after(values, last):
        return jnp.where(pair == half - 1, last, pltpu.roll(values, half - 1, 0))

    def before(values, first):
        return jnp.where(pair == 0, first, pltpu.roll(values, 1, 0))

    d_before = A * s[:1]
    d = d + A * (s + after(s, 0.0))
    s_after = B * d[half - 1 :]
    s_before = B * d_before
    s = s + B * (before(d, d_before) + d)
    d_before = d_before + G * (s_before + s[:1])
    d = d + G * (s + after(s, s_after))
    s = s + E * (before(d, d_before) + d)
    flat[even, :] = s * Z
    flat[odd, :] = d * (1.0 / Z)


def pack_tiles(level, tiles):
    lane = lax.broadcasted_iota(jnp.int32, tiles[0].shape, 1)
    step = 2**level
    keep = lane & (2 * step - 1) < step
    half = len(tiles) // 2
    return [jnp.where(keep, tiles[i], pltpu.roll(tiles[i + half], step, 1)) for i in range(half)]


def unpack_tiles(level, tiles, inner):
    lane = lax.broadcasted_iota(jnp.int32, tiles[0].shape, 1)
    step = 2**level
    keep = lane & (2 * step - 1) < step
    inner = list(inner) + [pltpu.roll(tile, LANES - step, 1) for tile in inner]
    return [jnp.where(keep, new, old) for new, old in zip(inner, tiles)]


def lift_lanes(tiles, ext, weights):
    first = lax.broadcasted_iota(jnp.int32, tiles[0].shape, 1) < LANES // 2
    blocks = [(tiles, ext)]
    if len(tiles) == 4:
        blocks = [(tiles[:2], jnp.where(first, tiles[2], ext)), (tiles[2:], jnp.where(first, ext, tiles[1]))]
    out = []
    for main, beside in blocks:
        main_top, main_low = parts_of(jnp.concatenate(main, axis=1))
        side_top, side_low = parts_of(beside)
        stacked = jnp.concatenate([main_top, main_low, main_top, side_top, side_low, side_top], axis=1)
        result = jnp.dot(stacked, weights[...], preferred_element_type=f32)
        out += [result[:, i * LANES : (i + 1) * LANES] for i in range(len(main))]
    return out


NAMES = ("zs", "zr", "ze", "xs", "xr", "xe", "xl", "es", "er", "ys", "yr", "yp", "zys", "zyr", "xys", "xyr", "cr")


def kernel(shape, field_ref, out_ref, *scratch):
    depth, rows, _ = shape
    refs = list(scratch)
    take = lambda: refs.pop(0)
    bodies = [out_ref, take(), take()]
    load_sem, send_sem, recv_sem = take(), take(), take()
    y_weights, far_weights, z_weights = [[take() for _ in range(LEVELS)] for _ in range(3)]
    held = [{name: take() for name in NAMES} for _ in range(LEVELS)]

    here = {name: lax.axis_index(name) for name in ("gx", "gy", "gz")}
    count = {name: lax.axis_size(name) for name in ("gx", "gy", "gz")}

    def beside(**by):
        return {name: lax.rem(here[name] + way + count[name], count[name]) for name, way in by.items()}

    barrier = pltpu.get_barrier_semaphore()
    for x in (-1, 0, 1):
        for y in (-1, 0, 1):
            for z in (-1, 0, 1):
                if (x, y, z) != (0, 0, 0):
                    pl.semaphore_signal(barrier, inc=1, device_id=beside(gx=x, gy=y, gz=z), device_id_type=MESH)

    loads = [
        pltpu.make_async_copy(
            field_ref.at[:, :, pl.ds(tile * LANES, LANES)], out_ref.at[:, tile], load_sem.at[tile]
        )
        for tile in range(TILES)
    ]
    for load in loads:
        load.start()

    def fill(ref, blocks):
        start = 0
        for values in blocks:
            top, low = parts_of(values)
            size = values.shape[0]
            for part in (top, top, low):
                ref[start : start + size] = part
                start += size

    def make_weights(level):
        window = 4 << level
        tiles = TILES >> level
        cells = (TILES * LANES) >> level
        width = min(tiles, 2) * LANES
        row = lax.broadcasted_iota(jnp.int32, (2 * LANES, width), 0)
        col = lax.broadcasted_iota(jnp.int32, (2 * LANES, width), 1)
        target = cell_of(level, col >> 7, col & 127)
        main = row[:width]
        side = row[:LANES]
        after, before = (2 * LANES, -LANES) if level == 0 else (cells, -cells)
        right = cell_of(level, 0, side) + after
        left = cell_of(level, 0 if level == 0 else tiles - 1, side) + before
        position = jnp.where(side < LANES // 2, right, left)
        fill(
            y_weights[level],
            [
                tap_weights(cell_of(level, main >> 7, main & 127), target[:width]),
                tap_weights(position, target[:LANES]),
            ],
        )
        inside = row & (window - 1)
        left = cell_of(level, tiles - 1, LANES - window + inside) - cells
        right = cell_of(level, 0, inside) + cells
        position = jnp.where(row < LANES, left, right)
        last = cell_of(level, tiles - 1, col & 127)
        target = jnp.where(col < LANES, cell_of(level, 0, col & 127), last)
        fill(far_weights[level], [tap_weights(position, target)])
        shift = 2 + level
        row, col = row[:LANES, :LANES], col[:LANES, :LANES]
        taps = tap_weights(row >> shift, col >> shift)
        fill(z_weights[level], [jnp.where((row & (window - 1)) == (col & (window - 1)), taps, 0.0)])

    make_weights(0)
    for load in loads:
        load.wait()

    sends = []
    arrivals = [{} for _ in range(LEVELS)]
    way = (1, -1)
    sub = lax.broadcasted_iota(jnp.int32, (8, LANES), 0)
    lane8 = lax.broadcasted_iota(jnp.int32, (8, LANES), 1)
    last_half = lane8 >= LANES // 2
    none8 = jnp.zeros((8, LANES), f32)

    def extent(level):
        return depth >> level, TILES >> level, rows >> level, 4 << level

    def flat_of(ref):
        size = 1
        for extent_of_dim in ref.shape[:-1]:
            size *= extent_of_dim
        return ref.reshape(size, LANES)

    def wait_for(level, *keys):
        for key in keys:
            for copy in arrivals[level][key]:
                copy.wait_recv()

    def start(level):
        planes, tiles, height, window = extent(level)
        body, flat, r = bodies[level], flat_of(bodies[level]), held[level]
        shift = 2 + level

        def send(key, number, source, target, **by):
            copy = pltpu.make_async_remote_copy(
                src_ref=source,
                dst_ref=target,
                send_sem=send_sem.at[level, number],
                recv_sem=recv_sem.at[level, number],
                device_id=beside(**by),
                device_id_type=MESH,
            )
            if level == 0 and number == 0:
                pl.semaphore_wait(barrier, 26)
            copy.start()
            sends.append(copy)
            arrivals[level].setdefault(key, []).append(copy)

        zs, xs, es = r["zs"], r["xs"], r["es"]
        for tile in range(tiles):
            end = encode_end(*[body[planes - 4 + number, tile] for number in range(4)])
            begin = encode_start(*[body[number, tile] for number in range(3)])
            for k in range(2):
                zs[0, k, tile] = end[k]
                zs[1, k, tile] = begin[k]
        for side in SIDES:
            send("z", side, zs.at[side], r["zr"].at[side], gz=way[side])

        xs_flat = flat_of(xs)
        for tile in range(tiles):
            def at(number):
                return flat[pl.ds(tile * height + number, planes, stride=tiles * height), :]

            end = encode_end(*[at(height - 4 + number) for number in range(4)])
            begin = encode_start(*[at(number) for number in range(3)])
            for k in range(2):
                xs_flat[pl.ds(k * tiles + tile, planes, stride=8), :] = end[k]
                xs_flat[pl.ds(planes * 8 + k * tiles + tile, planes, stride=8), :] = begin[k]
        for side in SIDES:
            send("x", 2 + side, xs.at[side], r["xr"].at[side], gx=way[side])

        for side in SIDES:
            end = encode_end(*[xs[side, planes - 4 + number] for number in range(4)])
            begin = encode_start(*[xs[side, number] for number in range(3)])
            for k in range(2):
                es[side, 0, k] = end[k]
                es[side, 1, k] = begin[k]
        for sx in SIDES:
            for sz in SIDES:
                number = 4 + 2 * sx + sz
                send("e", number, es.at[sx, sz], r["er"].at[sx, sz], gx=way[sx], gz=way[sz])
                for sy in SIDES:
                    number = 8 + 4 * sx + 2 * sz + sy
                    send("c", number, es.at[sx, sz], r["cr"].at[sx, sz, sy], gx=way[sx], gz=way[sz], gy=way[sy])

        lane = lax.broadcasted_iota(jnp.int32, (height, LANES), 1)

        def pack(plane, carried):
            to_right, to_left, x_right, x_left = carried
            tail_by = lax.rem(plane * window + window, LANES)
            head_by = plane * window
            mine = lane >> shift == plane
            to_right = jnp.where(mine, pltpu.roll(body[plane, tiles - 1], tail_by, 1), to_right)
            to_left = jnp.where(mine, pltpu.roll(body[plane, 0], head_by, 1), to_left)
            mine = lane8 >> shift == plane
            x_right = tuple(jnp.where(mine, pltpu.roll(xs[sx, plane], tail_by, 1), x_right[sx]) for sx in SIDES)
            x_left = tuple(jnp.where(mine, pltpu.roll(xs[sx, plane], head_by, 1), x_left[sx]) for sx in SIDES)
            return to_right, to_left, x_right, x_left

        none = jnp.zeros((height, LANES), f32)
        to_right, to_left, x_right, x_left = lax.fori_loop(
            0, planes, pack, (none, none, (none8, none8), (none8, none8))
        )
        r["ys"][0], r["ys"][1] = to_right, to_left
        for sx in SIDES:
            r["xys"][0, sx], r["xys"][1, sx] = x_right[sx], x_left[sx]
        groups = height // 8
        for sz in SIDES:
            tail = head = none8
            for k in range(2):
                for group in range(groups):
                    slot = k * groups + group
                    mine = lane8 >> shift == slot
                    part = pl.ds(group * 8, 8)
                    by = (slot * window + window) % LANES
                    tail = jnp.where(mine, pltpu.roll(zs[sz, k, tiles - 1, part, :], by, 1), tail)
                    head = jnp.where(mine, pltpu.roll(zs[sz, k, 0, part, :], slot * window, 1), head)
            r["zys"][0, sz], r["zys"][1, sz] = tail, head
        for sy in SIDES:
            send("y", 16 + sy, r["ys"].at[sy], r["yr"].at[sy], gy=way[sy])
            for s in SIDES:
                send("xy", 18 + 2 * sy + s, r["xys"].at[sy, s], r["xyr"].at[sy, s], gy=way[sy], gx=way[s])
                send("zy", 22 + 2 * sy + s, r["zys"].at[sy, s], r["zyr"].at[sy, s], gy=way[sy], gz=way[s])

    def own_xz(level):
        planes, tiles, height, _ = extent(level)
        body, flat = bodies[level], flat_of(bodies[level])
        groups = height // 8

        def along_x(plane, _):
            for tile in range(tiles):
                lift_rows(flat, (plane * tiles + tile) * height, height)
            return 0

        lax.fori_loop(0, planes, along_x, 0)

        def along_z(block, _):
            tile = block // groups
            part = pl.ds(pl.multiple_of((block % groups) * 8, 8), 8)
            lifted = lift_list([body[plane, tile, part, :] for plane in range(planes)])
            for plane in range(planes):
                body[plane, tile, part, :] = lifted[plane]
            return 0

        lax.fori_loop(0, tiles * groups, along_z, 0)

    def own_y(level):
        planes, tiles, height, _ = extent(level)
        body = bodies[level]
        chunk = min(planes, 512 // height)

        def along_y(number, _):
            where = pl.ds(number * chunk, chunk)
            values = [body[where, tile].reshape(chunk * height, LANES) for tile in range(tiles)]
            lifted = lift_lanes(values, jnp.zeros((chunk * height, LANES), f32), y_weights[level])
            for tile in range(tiles):
                body[where, tile] = lifted[tile].reshape(chunk, height, LANES)
            return 0

        lax.fori_loop(0, planes // chunk, along_y, 0)

    def prepare_y(level):
        height = extent(level)[2]
        r = held[level]
        for sy in SIDES:
            lift_rows(r["yr"].at[sy], 0, height)
            top, low = parts_of(r["yr"][sy])
            stacked = jnp.concatenate([top, low, top], axis=1)
            values = jnp.dot(stacked, z_weights[level][...], preferred_element_type=f32)
            top = values.astype(bf16).astype(f32)
            r["yp"][0, sy] = top
            r["yp"][1, sy] = values - top

    def spread_y(level, planes, pick):
        height = extent(level)[2]
        shift = 2 + level
        yp = held[level]["yp"]
        parts = [[pick(yp.at[part, sy]) for sy in SIDES] for part in range(2)]
        lane = lax.broadcasted_iota(jnp.int32, parts[0][0].shape, 1)
        stacks = []
        for plane in planes:
            mine = lane >> shift == plane
            top, low = [[jnp.where(mine, values, 0.0).astype(bf16) for values in part] for part in parts]
            stacks.append(jnp.concatenate(top + low + top, axis=1))
        return jnp.dot(jnp.concatenate(stacks, axis=0), far_weights[level][...], preferred_element_type=f32)

    def prepare_x(level):
        planes, tiles, height, window = extent(level)
        r = held[level]
        xr, xe, xl = r["xr"], r["xe"], r["xl"]

        def aligned(values):
            return pltpu.roll(values, 9 - tiles, 0) if tiles > 1 else values

        lefts = [aligned(r["xyr"][0, sx]) for sx in SIDES]
        rights = [r["xyr"][1, sx] for sx in SIDES]

        def unpack(plane, _):
            left_by = lax.rem(2 * LANES - window - plane * window, LANES)
            right_by = lax.rem(LANES - plane * window, LANES)
            for sx in SIDES:
                xe[sx, plane] = jnp.where(
                    last_half, pltpu.roll(lefts[sx], left_by, 1), pltpu.roll(rights[sx], right_by, 1)
                )
            return 0

        lax.fori_loop(0, planes, unpack, 0)
        for sx in SIDES:
            halo = [r["er"][sx, sz, k] for sz in SIDES for k in range(2)]
            lifted = lift_list([xr[sx, plane] for plane in range(planes)], halo)
            for plane in range(planes):
                xr[sx, plane] = lifted[plane]
            halo = [
                jnp.where(last_half, aligned(r["cr"][sx, sz, 0, k]), r["cr"][sx, sz, 1, k])
                for sz in SIDES
                for k in range(2)
            ]
            lifted = lift_list([xe[sx, plane] for plane in range(planes)], halo)
            for plane in range(planes):
                xe[sx, plane] = lifted[plane]
        xr_flat, xe_flat = flat_of(xr), flat_of(xe)

        def strip(ref, start):
            return ref[pl.ds(start, 2 * planes, stride=8), :]

        values = [
            jnp.concatenate([strip(xr_flat, k * tiles + tile) for k in range(2)], axis=0) for tile in range(tiles)
        ]
        ext = jnp.concatenate([strip(xe_flat, k * tiles) for k in range(2)], axis=0)
        lifted = lift_lanes(values, ext, y_weights[level])
        for tile in range(tiles):
            xl[tile] = lifted[tile]

    def prepare_z(level):
        planes, tiles, height, window = extent(level)
        r = held[level]
        zr, ze = r["zr"], r["ze"]
        zr_flat, ze_flat = flat_of(zr), flat_of(ze)
        groups = height // 8
        wait_for(level, "zy")
        for sz in SIDES:
            for k in range(2):
                for group in range(groups):
                    slot = k * groups + group
                    left = pltpu.roll(r["zyr"][0, sz], (2 * LANES - window - slot * window) % LANES, 1)
                    right = pltpu.roll(r["zyr"][1, sz], (LANES - slot * window) % LANES, 1)
                    ze[sz, k, pl.ds(group * 8, 8), :] = jnp.where(last_half, left, right)
        wait_for(level, "z")

        def along_x(layer, _):
            for tile in range(tiles):
                lift_rows(zr_flat, (layer * tiles + tile) * height, height)
            lift_rows(ze_flat, layer * height, height)
            return 0

        lax.fori_loop(0, 4, along_x, 0)
        values = [zr[:, :, tile].reshape(4 * height, LANES) for tile in range(tiles)]
        lifted = lift_lanes(values, ze[...].reshape(4 * height, LANES), y_weights[level])
        for tile in range(tiles):
            zr[:, :, tile] = lifted[tile].reshape(2, 2, height, LANES)

    def row_weights(table, layer, at):
        values = none8
        for number, weights in table.items():
            place = at(number)
            if place is not None and weights[layer] != 0.0:
                values = jnp.where(sub == place, weights[layer], values)
        return values

    def add_y(level):
        planes, tiles, height, _ = extent(level)
        body = bodies[level]
        chunk = min(planes, 512 // height)

        def add(number, _):
            where = pl.ds(number * chunk, chunk)
            added = spread_y(level, [number * chunk + inner for inner in range(chunk)], lambda ref: ref[...])
            body[where, 0] = body[where, 0] + added[:, :LANES].reshape(chunk, height, LANES)
            if tiles > 1:
                body[where, tiles - 1] = body[where, tiles - 1] + added[:, LANES:].reshape(chunk, height, LANES)
            return 0

        lax.fori_loop(0, planes // chunk, add, 0)

    def add_x_rows(body, planes, every, height, strips, at):
        tables = ((FROM_LEFT, 0), (FROM_RIGHT, height - 8))
        weigh = [[row_weights(table, layer, at) for layer in range(2)] for table, _ in tables]

        def add(number, _):
            for tile in range(body.shape[1]):
                strip = strips(tile)
                for side in SIDES:
                    part = pl.ds(tables[side][1], 8)
                    first = side * planes + number * every
                    added = weigh[side][0] * strip[pl.ds(first, 1), :]
                    added = added + weigh[side][1] * strip[pl.ds(2 * planes + first, 1), :]
                    body[number, tile, part, :] = body[number, tile, part, :] + added
            return 0

        lax.fori_loop(0, planes // every, add, 0)

    def add_x(level):
        planes, _, height, _ = extent(level)
        xl = held[level]["xl"]
        add_x_rows(bodies[level], planes, 1, height, lambda tile: xl.at[tile], lambda number: number % 8)

    def add_z(level):
        planes, tiles, _, _ = extent(level)
        body, zr = bodies[level], held[level]["zr"]
        for side, table in ((0, FROM_LEFT), (1, FROM_RIGHT)):
            for number, (one, two) in table.items():
                plane = number % planes
                for tile in range(tiles):
                    added = one * zr[side, 0, tile]
                    if two != 0.0:
                        added = added + two * zr[side, 1, tile]
                    body[plane, tile] = body[plane, tile] + added

    start(0)
    for level in range(1, LEVELS):
        make_weights(level)
    own_xz(0)
    planes, tiles, height, _ = extent(0)
    half, deep = height // 2, planes // 2
    inner, inner_tiles = bodies[1], tiles // 2
    flat = flat_of(bodies[0])
    tops = list(range(0, planes, 2))

    def low_rows(ref_flat, start_of):
        return ref_flat[pl.ds(start_of, half, stride=2), :]

    values = [
        jnp.concatenate([low_rows(flat, (plane * tiles + tile) * height) for plane in tops], axis=0)
        for tile in range(tiles)
    ]
    lifted = lift_lanes(values, jnp.zeros((deep * half, LANES), f32), y_weights[0])
    for tile, packed in enumerate(pack_tiles(0, lifted)):
        inner[:, tile] = packed.reshape(deep, half, LANES)

    wait_for(0, "y")
    prepare_y(0)
    added = spread_y(0, tops, lambda ref: ref[pl.ds(0, half, stride=2), :])
    keep = (lax.broadcasted_iota(jnp.int32, (deep * half, LANES), 1) & 1) == 0
    first = jnp.where(keep, added[:, :LANES], 0.0)
    last = jnp.where(keep, 0.0, pltpu.roll(added[:, LANES:], 1, 1))
    inner[:, 0] = inner[:, 0] + first.reshape(deep, half, LANES)
    inner[:, inner_tiles - 1] = inner[:, inner_tiles - 1] + last.reshape(deep, half, LANES)

    wait_for(0, "x", "e", "c", "xy")
    prepare_x(0)
    xl, xp = held[0]["xl"], take()
    for tile, packed in enumerate(pack_tiles(0, [xl[tile] for tile in range(tiles)])):
        xp[tile] = packed

    def even_row(number):
        return (number % 16) // 2 % 8 if number % 2 == 0 else None

    add_x_rows(inner, planes, 2, half, lambda tile: xp.at[tile], even_row)
    prepare_z(0)
    zr_flat = flat_of(held[0]["zr"])
    for side, table in ((0, FROM_LEFT), (1, FROM_RIGHT)):
        packed = [
            pack_tiles(0, [low_rows(zr_flat, ((2 * side + k) * tiles + tile) * height) for tile in range(tiles)])
            for k in range(2)
        ]
        for number, (one, two) in table.items():
            if number % 2 == 0:
                plane = (number % planes) // 2
                for tile in range(inner_tiles):
                    added = one * packed[0][tile]
                    if two != 0.0:
                        added = added + two * packed[1][tile]
                    inner[plane, tile] = inner[plane, tile] + added

    start(1)
    own_xz(1)
    own_y(1)
    own_y(0)
    wait_for(1, "y")
    prepare_y(1)
    add_y(1)
    wait_for(1, "x", "e", "c", "xy")
    prepare_x(1)
    add_x(1)
    prepare_z(1)
    add_z(1)
    planes, tiles, height, _ = extent(1)
    half = height // 2
    flat = flat_of(bodies[1])

    def pick(plane, _):
        values = [flat[pl.ds((2 * plane * tiles + tile) * height, half, stride=2), :] for tile in range(tiles)]
        for tile, packed in enumerate(pack_tiles(1, values)):
            bodies[2][plane, tile] = packed
        return 0

    lax.fori_loop(0, planes // 2, pick, 0)

    start(2)
    own_xz(2)
    own_y(2)
    add_y(0)
    add_x(0)
    add_z(0)
    wait_for(2, "y")
    prepare_y(2)
    add_y(2)
    wait_for(2, "x", "e", "c", "xy")
    prepare_x(2)
    add_x(2)
    prepare_z(2)
    add_z(2)

    for level in (1, 0):
        planes, tiles, height, _ = extent(level)
        half = height // 2
        flat = flat_of(bodies[level])

        def place(plane, _):
            where = [pl.ds((2 * plane * tiles + tile) * height, half, stride=2) for tile in range(tiles)]
            inner = [bodies[level + 1][plane, tile] for tile in range(tiles // 2)]
            for at, values in zip(where, unpack_tiles(level, [flat[at, :] for at in where], inner)):
                flat[at, :] = values
            return 0

        lax.fori_loop(0, planes // 2, place, 0)

    for copy in sends:
        copy.wait_send()


def write_out(held_ref, out_ref, sem):
    copies = [
        pltpu.make_async_copy(held_ref.at[:, tile], out_ref.at[:, :, pl.ds(tile * LANES, LANES)], sem.at[tile])
        for tile in range(TILES)
    ]
    for copy in copies:
        copy.start()
    for copy in copies:
        copy.wait()


def local(field):
    depth, rows, lanes = field.shape
    vmem = pltpu.VMEM
    sizes = [(depth >> level, TILES >> level, rows >> level) for level in range(LEVELS)]
    scratch = [vmem((planes, tiles, height, LANES), f32) for planes, tiles, height in sizes[1:]]
    scratch += [
        pltpu.SemaphoreType.DMA((TILES,)),
        pltpu.SemaphoreType.DMA((LEVELS, 26)),
        pltpu.SemaphoreType.DMA((LEVELS, 26)),
    ]
    widths = [min(tiles, 2) * LANES for _, tiles, _ in sizes]
    scratch += [vmem((3 * (width + LANES), width), bf16) for width in widths]
    scratch += [vmem((6 * LANES, width), bf16) for width in widths]
    scratch += [vmem((3 * LANES, LANES), bf16) for _ in sizes]
    for planes, tiles, height in sizes:
        shapes = [(2, 2, tiles, height)] * 2 + [(2, 2, height)]
        shapes += [(2, planes, 8)] * 3 + [(tiles, 4 * planes)]
        shapes += [(2, 2, 2, 8)] * 2 + [(2, height)] * 2 + [(2, 2, height)]
        shapes += [(2, 2, 8)] * 4 + [(2, 2, 2, 2, 8)]
        scratch += [vmem((*shape, LANES), f32) for shape in shapes]
    scratch += [vmem((TILES // 2, 4 * depth, LANES), f32)]
    lifted = pl.pallas_call(
        functools.partial(kernel, field.shape),
        out_shape=jax.ShapeDtypeStruct((depth, TILES, rows, LANES), f32),
        in_specs=[pl.BlockSpec(memory_space=pltpu.HBM)],
        out_specs=pl.BlockSpec(memory_space=pltpu.VMEM),
        scratch_shapes=scratch,
        compiler_params=pltpu.CompilerParams(
            collective_id=0, has_side_effects=True, vmem_limit_bytes=48 * 2**20
        ),
        name="lift",
    )(field)
    return pl.pallas_call(
        write_out,
        out_shape=jax.ShapeDtypeStruct(field.shape, f32),
        in_specs=[pl.BlockSpec(memory_space=pltpu.VMEM)],
        out_specs=pl.BlockSpec(memory_space=pltpu.HBM),
        scratch_shapes=[pltpu.SemaphoreType.DMA((TILES,))],
        compiler_params=pltpu.CompilerParams(vmem_limit_bytes=8 * 2**20),
        name="write_out",
    )(lifted)


def solution(mesh):
    placed = (P("gz", "gx", "gy"),)
    return jax.shard_map(
        local, mesh=mesh, in_specs=placed, out_specs=P("gz", "gx", "gy"), check_vma=False
    )
```

```python
import functools

import jax
import jax.numpy as jnp
import numpy as np
from jax import lax
from jax.experimental import pallas as pl
from jax.experimental.pallas import tpu as pltpu
from jax.sharding import PartitionSpec as P

A = -1.586134342
B = -0.05298011854
G = 0.8829110762
E = 0.4435068522
Z = 1.149604398
MESH = pl.DeviceIdType.MESH
LANES = 128
TILES = 4
LEVELS = 3
SIDES = (0, 1)
f32, bf16 = jnp.float32, jnp.bfloat16


def filter_taps():
    u = np.eye(64)
    s, d = u[0::2].copy(), u[1::2].copy()
    d += A * (s + np.roll(s, -1, 0))
    s += B * (np.roll(d, 1, 0) + d)
    d += G * (s + np.roll(s, -1, 0))
    s += E * (np.roll(d, 1, 0) + d)
    low, high = s[16] * Z, d[16] / Z
    return [float(low[32 + o]) for o in range(5)], [float(high[33 + o]) for o in range(5)]


LOW, HIGH = filter_taps()

FROM_LEFT = {
    0: (Z * (B + E * (1 + 3 * G * B)), Z * E * G),
    1: (G * B / Z, 0.0),
    2: (Z * E * G * B, 0.0),
}
FROM_RIGHT = {
    -4: (Z * E * G * B * A, 0.0),
    -3: (G * B * A / Z, 0.0),
    -2: (Z * (B * A + E * (G * B * A + A * (1 + 2 * G * B))), Z * E * G),
    -1: (A * (1 + 2 * G * B) / Z, G / Z),
}


def cell_of(level, tile, lane):
    if level == 0:
        return tile * LANES + lane
    if level == 1:
        turn = lane & 1
        return ((tile + 2 * turn) * LANES + lane - turn) >> 1
    turn = lane & 3
    return (((turn >> 1) + 2 * (turn & 1)) * LANES + lane - turn) >> 2


def tap_weights(position, target):
    apart = jnp.abs(position - target)
    low = jnp.zeros(position.shape, f32)
    high = jnp.zeros(position.shape, f32)
    for o in range(5):
        low = jnp.where(apart == o, LOW[o], low)
        if o < 4:
            high = jnp.where(apart == o, HIGH[o], high)
    return jnp.where((target & 1) == 0, low, high)


def parts_of(values):
    top = values.astype(bf16)
    return top, (values - top.astype(f32)).astype(bf16)


def encode_end(s2, d2, s1, d1):
    return d1 + A * s1, s1 + B * (d2 + A * (s2 + s1))


def encode_start(s0, d0, s1):
    return s0, s0 + B * (d0 + A * (s0 + s1))


def lift_list(u, halo=None):
    s, d = list(u[0::2]), list(u[1::2])
    count = len(s)
    d_before = A * s[0]
    if halo is not None:
        d_before = d_before + halo[0]
    s_before = B * d_before
    if halo is not None:
        s_before = s_before + halo[1]
    for i in range(count - 1):
        d[i] = d[i] + A * (s[i] + s[i + 1])
    last = s[-1] if halo is None else s[-1] + halo[2]
    d[-1] = d[-1] + A * last
    s_after = B * d[-1]
    if halo is not None:
        s_after = s_after + halo[3]
    around = [d_before] + d
    s = [s[i] + B * (around[i] + around[i + 1]) for i in range(count)]
    d_before = d_before + G * (s_before + s[0])
    around = s + [s_after]
    d = [d[i] + G * (around[i] + around[i + 1]) for i in range(count)]
    around = [d_before] + d
    s = [s[i] + E * (around[i] + around[i + 1]) for i in range(count)]
    out = []
    for i in range(count):
        out += [s[i] * Z, d[i] * (1.0 / Z)]
    return out


def lift_rows(flat, start, height):
    half = height // 2
    pair = lax.broadcasted_iota(jnp.int32, (half, LANES), 0)
    even, odd = pl.ds(start, half, stride=2), pl.ds(start + 1, half, stride=2)
    s, d = flat[even, :], flat[odd, :]

    def after(values, last):
        return jnp.where(pair == half - 1, last, pltpu.roll(values, half - 1, 0))

    def before(values, first):
        return jnp.where(pair == 0, first, pltpu.roll(values, 1, 0))

    d_before = A * s[:1]
    d = d + A * (s + after(s, 0.0))
    s_after = B * d[half - 1 :]
    s_before = B * d_before
    s = s + B * (before(d, d_before) + d)
    d_before = d_before + G * (s_before + s[:1])
    d = d + G * (s + after(s, s_after))
    s = s + E * (before(d, d_before) + d)
    flat[even, :] = s * Z
    flat[odd, :] = d * (1.0 / Z)


def pack_tiles(level, tiles):
    lane = lax.broadcasted_iota(jnp.int32, tiles[0].shape, 1)
    step = 2**level
    keep = lane & (2 * step - 1) < step
    half = len(tiles) // 2
    return [jnp.where(keep, tiles[i], pltpu.roll(tiles[i + half], step, 1)) for i in range(half)]


def unpack_tiles(level, tiles, inner):
    lane = lax.broadcasted_iota(jnp.int32, tiles[0].shape, 1)
    step = 2**level
    keep = lane & (2 * step - 1) < step
    inner = list(inner) + [pltpu.roll(tile, LANES - step, 1) for tile in inner]
    return [jnp.where(keep, new, old) for new, old in zip(inner, tiles)]


def lift_lanes(tiles, ext, weights):
    first = lax.broadcasted_iota(jnp.int32, tiles[0].shape, 1) < LANES // 2
    blocks = [(tiles, ext)]
    if len(tiles) == 4:
        blocks = [(tiles[:2], jnp.where(first, tiles[2], ext)), (tiles[2:], jnp.where(first, ext, tiles[1]))]
    out = []
    for main, beside in blocks:
        main_top, main_low = parts_of(jnp.concatenate(main, axis=1))
        side_top, side_low = parts_of(beside)
        stacked = jnp.concatenate([main_top, main_low, main_top, side_top, side_low, side_top], axis=1)
        result = jnp.dot(stacked, weights[...], preferred_element_type=f32)
        out += [result[:, i * LANES : (i + 1) * LANES] for i in range(len(main))]
    return out


def loop(count, unroll, body, carry=0):
    unroll = min(unroll, count)

    def turns(number, carried):
        for inner in range(unroll):
            carried = body(number * unroll + inner, carried)
        return carried

    return lax.fori_loop(0, count // unroll, turns, carry)


NAMES = ("zs", "zr", "ze", "xs", "xr", "xe", "xl", "es", "er", "ys", "yr", "yp", "zys", "zyr", "xys", "xyr", "cr")


def kernel(shape, field_ref, out_ref, inner_ref, *scratch):
    depth, rows, _ = shape
    refs = list(scratch)
    take = lambda: refs.pop(0)
    bodies = [out_ref, inner_ref, take()]
    load_sem, send_sem, recv_sem = take(), take(), take()
    y_weights, far_weights, z_weights = [[take() for _ in range(LEVELS)] for _ in range(3)]
    held = [{name: take() for name in NAMES} for _ in range(LEVELS)]

    here = {name: lax.axis_index(name) for name in ("gx", "gy", "gz")}
    count = {name: lax.axis_size(name) for name in ("gx", "gy", "gz")}

    near = {
        name: {-1: lax.rem(at + count[name] - 1, count[name]), 0: at, 1: lax.rem(at + 1, count[name])}
        for name, at in here.items()
    }

    def beside(**by):
        return {name: near[name][way] for name, way in by.items()}

    barrier = pltpu.get_barrier_semaphore()
    for x in (-1, 0, 1):
        for y in (-1, 0, 1):
            for z in (-1, 0, 1):
                if (x, y, z) != (0, 0, 0):
                    pl.semaphore_signal(barrier, inc=1, device_id=beside(gx=x, gy=y, gz=z), device_id_type=MESH)

    loads = [
        pltpu.make_async_copy(
            field_ref.at[:, :, pl.ds(tile * LANES, LANES)], out_ref.at[:, tile], load_sem.at[tile]
        )
        for tile in range(TILES)
    ]
    for load in loads:
        load.start()

    def fill(ref, blocks):
        start = 0
        for values in blocks:
            top, low = parts_of(values)
            size = values.shape[0]
            for part in (top, top, low):
                ref[start : start + size] = part
                start += size

    def make_weights(level):
        window = 4 << level
        tiles = TILES >> level
        cells = (TILES * LANES) >> level
        width = min(tiles, 2) * LANES
        row = lax.broadcasted_iota(jnp.int32, (2 * LANES, width), 0)
        col = lax.broadcasted_iota(jnp.int32, (2 * LANES, width), 1)
        target = cell_of(level, col >> 7, col & 127)
        main = row[:width]
        side = row[:LANES]
        after, before = (2 * LANES, -LANES) if level == 0 else (cells, -cells)
        right = cell_of(level, 0, side) + after
        left = cell_of(level, 0 if level == 0 else tiles - 1, side) + before
        position = jnp.where(side < LANES // 2, right, left)
        fill(
            y_weights[level],
            [
                tap_weights(cell_of(level, main >> 7, main & 127), target[:width]),
                tap_weights(position, target[:LANES]),
            ],
        )
        inside = row & (window - 1)
        left = cell_of(level, tiles - 1, LANES - window + inside) - cells
        right = cell_of(level, 0, inside) + cells
        position = jnp.where(row < LANES, left, right)
        last = cell_of(level, tiles - 1, col & 127)
        target = jnp.where(col < LANES, cell_of(level, 0, col & 127), last)
        fill(far_weights[level], [tap_weights(position, target)])
        shift = 2 + level
        row, col = row[:LANES, :LANES], col[:LANES, :LANES]
        taps = tap_weights(row >> shift, col >> shift)
        fill(z_weights[level], [jnp.where((row & (window - 1)) == (col & (window - 1)), taps, 0.0)])

    make_weights(0)
    for load in loads:
        load.wait()

    sends = []
    arrivals = [{} for _ in range(LEVELS)]
    way = (1, -1)
    sub = lax.broadcasted_iota(jnp.int32, (8, LANES), 0)
    lane8 = lax.broadcasted_iota(jnp.int32, (8, LANES), 1)
    last_half = lane8 >= LANES // 2
    none8 = jnp.zeros((8, LANES), f32)

    def extent(level):
        return depth >> level, TILES >> level, rows >> level, 4 << level

    def flat_of(ref):
        size = 1
        for extent_of_dim in ref.shape[:-1]:
            size *= extent_of_dim
        return ref.reshape(size, LANES)

    def wait_for(level, *keys):
        for key in keys:
            for copy in arrivals[level][key]:
                copy.wait_recv()

    def start(level):
        planes, tiles, height, window = extent(level)
        body, flat, r = bodies[level], flat_of(bodies[level]), held[level]
        shift = 2 + level

        def send(key, number, source, target, **by):
            copy = pltpu.make_async_remote_copy(
                src_ref=source,
                dst_ref=target,
                send_sem=send_sem.at[level, number],
                recv_sem=recv_sem.at[level, number],
                device_id=beside(**by),
                device_id_type=MESH,
            )
            if level == 0 and number == 0:
                pl.semaphore_wait(barrier, 26)
            copy.start()
            sends.append(copy)
            arrivals[level].setdefault(key, []).append(copy)

        zs, xs, es = r["zs"], r["xs"], r["es"]
        for tile in range(tiles):
            end = encode_end(*[body[planes - 4 + number, tile] for number in range(4)])
            begin = encode_start(*[body[number, tile] for number in range(3)])
            for k in range(2):
                zs[0, k, tile] = end[k]
                zs[1, k, tile] = begin[k]
        for side in SIDES:
            send("z", side, zs.at[side], r["zr"].at[side], gz=way[side])

        xs_flat = flat_of(xs)
        for tile in range(tiles):
            def at(number):
                return flat[pl.ds(tile * height + number, planes, stride=tiles * height), :]

            end = encode_end(*[at(height - 4 + number) for number in range(4)])
            begin = encode_start(*[at(number) for number in range(3)])
            for k in range(2):
                xs_flat[pl.ds(k * tiles + tile, planes, stride=8), :] = end[k]
                xs_flat[pl.ds(planes * 8 + k * tiles + tile, planes, stride=8), :] = begin[k]
        for side in SIDES:
            send("x", 2 + side, xs.at[side], r["xr"].at[side], gx=way[side])

        for side in SIDES:
            end = encode_end(*[xs[side, planes - 4 + number] for number in range(4)])
            begin = encode_start(*[xs[side, number] for number in range(3)])
            for k in range(2):
                es[side, 0, k] = end[k]
                es[side, 1, k] = begin[k]
        for sx in SIDES:
            for sz in SIDES:
                number = 4 + 2 * sx + sz
                send("e", number, es.at[sx, sz], r["er"].at[sx, sz], gx=way[sx], gz=way[sz])
                for sy in SIDES:
                    number = 8 + 4 * sx + 2 * sz + sy
                    send("c", number, es.at[sx, sz], r["cr"].at[sx, sz, sy], gx=way[sx], gz=way[sz], gy=way[sy])

        lane = lax.broadcasted_iota(jnp.int32, (height, LANES), 1)

        def pack(plane, carried):
            to_right, to_left, x_right, x_left = carried
            tail_by = lax.rem(plane * window + window, LANES)
            head_by = plane * window
            mine = lane >> shift == plane
            to_right = jnp.where(mine, pltpu.roll(body[plane, tiles - 1], tail_by, 1), to_right)
            to_left = jnp.where(mine, pltpu.roll(body[plane, 0], head_by, 1), to_left)
            mine = lane8 >> shift == plane
            x_right = tuple(jnp.where(mine, pltpu.roll(xs[sx, plane], tail_by, 1), x_right[sx]) for sx in SIDES)
            x_left = tuple(jnp.where(mine, pltpu.roll(xs[sx, plane], head_by, 1), x_left[sx]) for sx in SIDES)
            return to_right, to_left, x_right, x_left

        none = jnp.zeros((height, LANES), f32)
        to_right, to_left, x_right, x_left = loop(
            planes, 4, pack, (none, none, (none8, none8), (none8, none8))
        )
        r["ys"][0], r["ys"][1] = to_right, to_left
        for sx in SIDES:
            r["xys"][0, sx], r["xys"][1, sx] = x_right[sx], x_left[sx]
        groups = height // 8
        for sz in SIDES:
            tail = head = none8
            for k in range(2):
                for group in range(groups):
                    slot = k * groups + group
                    mine = lane8 >> shift == slot
                    part = pl.ds(group * 8, 8)
                    by = (slot * window + window) % LANES
                    tail = jnp.where(mine, pltpu.roll(zs[sz, k, tiles - 1, part, :], by, 1), tail)
                    head = jnp.where(mine, pltpu.roll(zs[sz, k, 0, part, :], slot * window, 1), head)
            r["zys"][0, sz], r["zys"][1, sz] = tail, head
        for sy in SIDES:
            send("y", 16 + sy, r["ys"].at[sy], r["yr"].at[sy], gy=way[sy])
            for s in SIDES:
                send("xy", 18 + 2 * sy + s, r["xys"].at[sy, s], r["xyr"].at[sy, s], gy=way[sy], gx=way[s])
                send("zy", 22 + 2 * sy + s, r["zys"].at[sy, s], r["zyr"].at[sy, s], gy=way[sy], gz=way[s])

    def own_xz(level):
        planes, tiles, height, _ = extent(level)
        body, flat = bodies[level], flat_of(bodies[level])
        groups = height // 8

        def along_x(plane, _):
            for tile in range(tiles):
                lift_rows(flat, (plane * tiles + tile) * height, height)
            return 0

        loop(planes, 2 if level == 0 else 4, along_x)

        def along_z(block, _):
            tile = block // groups
            part = pl.ds(pl.multiple_of((block % groups) * 8, 8), 8)
            lifted = lift_list([body[plane, tile, part, :] for plane in range(planes)])
            for plane in range(planes):
                body[plane, tile, part, :] = lifted[plane]
            return 0

        loop(tiles * groups, 1 if level == 0 else 2, along_z)

    def own_y(level):
        planes, tiles, height, _ = extent(level)
        body = bodies[level]
        chunk = min(planes, 512 // height)

        def along_y(number, _):
            where = pl.ds(number * chunk, chunk)
            values = [body[where, tile].reshape(chunk * height, LANES) for tile in range(tiles)]
            lifted = lift_lanes(values, jnp.zeros((chunk * height, LANES), f32), y_weights[level])
            for tile in range(tiles):
                body[where, tile] = lifted[tile].reshape(chunk, height, LANES)
            return 0

        lax.fori_loop(0, planes // chunk, along_y, 0)

    def prepare_y(level):
        height = extent(level)[2]
        r = held[level]
        for sy in SIDES:
            lift_rows(r["yr"].at[sy], 0, height)
            top, low = parts_of(r["yr"][sy])
            stacked = jnp.concatenate([top, low, top], axis=1)
            values = jnp.dot(stacked, z_weights[level][...], preferred_element_type=f32)
            top = values.astype(bf16).astype(f32)
            r["yp"][0, sy] = top
            r["yp"][1, sy] = values - top

    def spread_y(level, planes, pick):
        height = extent(level)[2]
        shift = 2 + level
        yp = held[level]["yp"]
        parts = [[pick(yp.at[part, sy]) for sy in SIDES] for part in range(2)]
        lane = lax.broadcasted_iota(jnp.int32, parts[0][0].shape, 1)
        stacks = []
        for plane in planes:
            mine = lane >> shift == plane
            top, low = [[jnp.where(mine, values, 0.0).astype(bf16) for values in part] for part in parts]
            stacks.append(jnp.concatenate(top + low + top, axis=1))
        return jnp.dot(jnp.concatenate(stacks, axis=0), far_weights[level][...], preferred_element_type=f32)

    def prepare_x(level):
        planes, tiles, height, window = extent(level)
        r = held[level]
        xr, xe, xl = r["xr"], r["xe"], r["xl"]

        def aligned(values):
            return pltpu.roll(values, 9 - tiles, 0) if tiles > 1 else values

        lefts = [aligned(r["xyr"][0, sx]) for sx in SIDES]
        rights = [r["xyr"][1, sx] for sx in SIDES]

        def unpack(plane, _):
            left_by = lax.rem(2 * LANES - window - plane * window, LANES)
            right_by = lax.rem(LANES - plane * window, LANES)
            for sx in SIDES:
                xe[sx, plane] = jnp.where(
                    last_half, pltpu.roll(lefts[sx], left_by, 1), pltpu.roll(rights[sx], right_by, 1)
                )
            return 0

        loop(planes, 8, unpack)
        for sx in SIDES:
            halo = [r["er"][sx, sz, k] for sz in SIDES for k in range(2)]
            lifted = lift_list([xr[sx, plane] for plane in range(planes)], halo)
            for plane in range(planes):
                xr[sx, plane] = lifted[plane]
            halo = [
                jnp.where(last_half, aligned(r["cr"][sx, sz, 0, k]), r["cr"][sx, sz, 1, k])
                for sz in SIDES
                for k in range(2)
            ]
            lifted = lift_list([xe[sx, plane] for plane in range(planes)], halo)
            for plane in range(planes):
                xe[sx, plane] = lifted[plane]
        xr_flat, xe_flat = flat_of(xr), flat_of(xe)

        def strip(ref, start):
            return ref[pl.ds(start, 2 * planes, stride=8), :]

        values = [
            jnp.concatenate([strip(xr_flat, k * tiles + tile) for k in range(2)], axis=0) for tile in range(tiles)
        ]
        ext = jnp.concatenate([strip(xe_flat, k * tiles) for k in range(2)], axis=0)
        lifted = lift_lanes(values, ext, y_weights[level])
        for tile in range(tiles):
            xl[tile] = lifted[tile]

    def prepare_z(level):
        planes, tiles, height, window = extent(level)
        r = held[level]
        zr, ze = r["zr"], r["ze"]
        zr_flat, ze_flat = flat_of(zr), flat_of(ze)
        groups = height // 8
        wait_for(level, "zy")
        for sz in SIDES:
            for k in range(2):
                for group in range(groups):
                    slot = k * groups + group
                    left = pltpu.roll(r["zyr"][0, sz], (2 * LANES - window - slot * window) % LANES, 1)
                    right = pltpu.roll(r["zyr"][1, sz], (LANES - slot * window) % LANES, 1)
                    ze[sz, k, pl.ds(group * 8, 8), :] = jnp.where(last_half, left, right)
        wait_for(level, "z")

        def along_x(layer, _):
            for tile in range(tiles):
                lift_rows(zr_flat, (layer * tiles + tile) * height, height)
            lift_rows(ze_flat, layer * height, height)
            return 0

        loop(4, 4, along_x)
        values = [zr[:, :, tile].reshape(4 * height, LANES) for tile in range(tiles)]
        lifted = lift_lanes(values, ze[...].reshape(4 * height, LANES), y_weights[level])
        for tile in range(tiles):
            zr[:, :, tile] = lifted[tile].reshape(2, 2, height, LANES)

    def row_weights(table, layer, at):
        values = none8
        for number, weights in table.items():
            place = at(number)
            if place is not None and weights[layer] != 0.0:
                values = jnp.where(sub == place, weights[layer], values)
        return values

    def add_y(level):
        planes, tiles, height, _ = extent(level)
        body = bodies[level]
        chunk = min(planes, 512 // height)

        def add(number, _):
            where = pl.ds(number * chunk, chunk)
            added = spread_y(level, [number * chunk + inner for inner in range(chunk)], lambda ref: ref[...])
            body[where, 0] = body[where, 0] + added[:, :LANES].reshape(chunk, height, LANES)
            if tiles > 1:
                body[where, tiles - 1] = body[where, tiles - 1] + added[:, LANES:].reshape(chunk, height, LANES)
            return 0

        lax.fori_loop(0, planes // chunk, add, 0)

    def add_x_rows(body, planes, every, height, strips, at):
        tables = ((FROM_LEFT, 0), (FROM_RIGHT, height - 8))
        weigh = [[row_weights(table, layer, at) for layer in range(2)] for table, _ in tables]

        def add(number, _):
            for tile in range(body.shape[1]):
                strip = strips(tile)
                for side in SIDES:
                    part = pl.ds(tables[side][1], 8)
                    first = side * planes + number * every
                    added = weigh[side][0] * strip[pl.ds(first, 1), :]
                    added = added + weigh[side][1] * strip[pl.ds(2 * planes + first, 1), :]
                    body[number, tile, part, :] = body[number, tile, part, :] + added
            return 0

        loop(planes // every, 4, add)

    def add_x(level):
        planes, _, height, _ = extent(level)
        xl = held[level]["xl"]
        add_x_rows(bodies[level], planes, 1, height, lambda tile: xl.at[tile], lambda number: number % 8)

    def add_z(level):
        planes, tiles, _, _ = extent(level)
        body, zr = bodies[level], held[level]["zr"]
        for side, table in ((0, FROM_LEFT), (1, FROM_RIGHT)):
            for number, (one, two) in table.items():
                plane = number % planes
                for tile in range(tiles):
                    added = one * zr[side, 0, tile]
                    if two != 0.0:
                        added = added + two * zr[side, 1, tile]
                    body[plane, tile] = body[plane, tile] + added

    start(0)
    for level in range(1, LEVELS):
        make_weights(level)
    own_xz(0)
    planes, tiles, height, _ = extent(0)
    half, deep = height // 2, planes // 2
    inner, inner_tiles = bodies[1], tiles // 2
    flat = flat_of(bodies[0])
    tops = list(range(0, planes, 2))

    def low_rows(ref_flat, start_of):
        return ref_flat[pl.ds(start_of, half, stride=2), :]

    values = [
        jnp.concatenate([low_rows(flat, (plane * tiles + tile) * height) for plane in tops], axis=0)
        for tile in range(tiles)
    ]
    lifted = lift_lanes(values, jnp.zeros((deep * half, LANES), f32), y_weights[0])
    for tile, packed in enumerate(pack_tiles(0, lifted)):
        inner[:, tile] = packed.reshape(deep, half, LANES)

    wait_for(0, "y")
    prepare_y(0)
    added = spread_y(0, tops, lambda ref: ref[pl.ds(0, half, stride=2), :])
    keep = (lax.broadcasted_iota(jnp.int32, (deep * half, LANES), 1) & 1) == 0
    first = jnp.where(keep, added[:, :LANES], 0.0)
    last = jnp.where(keep, 0.0, pltpu.roll(added[:, LANES:], 1, 1))
    inner[:, 0] = inner[:, 0] + first.reshape(deep, half, LANES)
    inner[:, inner_tiles - 1] = inner[:, inner_tiles - 1] + last.reshape(deep, half, LANES)

    wait_for(0, "x", "e", "c", "xy")
    prepare_x(0)
    xl, xp = held[0]["xl"], take()
    for tile, packed in enumerate(pack_tiles(0, [xl[tile] for tile in range(tiles)])):
        xp[tile] = packed

    def even_row(number):
        return (number % 16) // 2 % 8 if number % 2 == 0 else None

    add_x_rows(inner, planes, 2, half, lambda tile: xp.at[tile], even_row)
    prepare_z(0)
    zr_flat = flat_of(held[0]["zr"])
    for side, table in ((0, FROM_LEFT), (1, FROM_RIGHT)):
        packed = [
            pack_tiles(0, [low_rows(zr_flat, ((2 * side + k) * tiles + tile) * height) for tile in range(tiles)])
            for k in range(2)
        ]
        for number, (one, two) in table.items():
            if number % 2 == 0:
                plane = (number % planes) // 2
                for tile in range(inner_tiles):
                    added = one * packed[0][tile]
                    if two != 0.0:
                        added = added + two * packed[1][tile]
                    inner[plane, tile] = inner[plane, tile] + added

    start(1)
    own_xz(1)
    own_y(1)
    own_y(0)
    wait_for(1, "y")
    prepare_y(1)
    add_y(1)
    wait_for(1, "x", "e", "c", "xy")
    prepare_x(1)
    add_x(1)
    prepare_z(1)
    add_z(1)
    planes, tiles, height, _ = extent(1)
    half = height // 2
    flat = flat_of(bodies[1])

    def pick(plane, _):
        values = [flat[pl.ds((2 * plane * tiles + tile) * height, half, stride=2), :] for tile in range(tiles)]
        for tile, packed in enumerate(pack_tiles(1, values)):
            bodies[2][plane, tile] = packed
        return 0

    loop(planes // 2, 4, pick)

    start(2)
    own_xz(2)
    own_y(2)
    add_y(0)
    add_x(0)
    add_z(0)
    wait_for(2, "y")
    prepare_y(2)
    add_y(2)
    wait_for(2, "x", "e", "c", "xy")
    prepare_x(2)
    add_x(2)
    prepare_z(2)
    add_z(2)

    planes, tiles, height, _ = extent(1)
    half = height // 2

    def place(plane, _):
        where = [pl.ds((2 * plane * tiles + tile) * height, half, stride=2) for tile in range(tiles)]
        inner = [bodies[2][plane, tile] for tile in range(tiles // 2)]
        for at, values in zip(where, unpack_tiles(1, [flat[at, :] for at in where], inner)):
            flat[at, :] = values
        return 0

    loop(planes // 2, 4, place)

    for copy in sends:
        copy.wait_send()


def write_out(held_ref, inner_ref, out_ref, merged, sem):
    depth, tiles, rows, _ = held_ref.shape
    planes, half = depth // 2, rows // 2
    pairs = held_ref.reshape(planes, 2, tiles, rows, LANES)
    target = out_ref.reshape(planes, 2, rows, tiles * LANES)
    parts = sem.shape[0] - 1
    size = planes // parts

    def copy(source, odd, tile, slot, where):
        return pltpu.make_async_copy(
            source, target.at[where, odd, :, pl.ds(tile * LANES, LANES)], sem.at[slot, tile]
        )

    copies = [copy(pairs.at[:, 1, tile], 1, tile, parts, pl.ds(0, planes)) for tile in range(tiles)]
    for one in copies:
        one.start()
    held_flat = held_ref.reshape(depth * tiles * rows, LANES)
    merged_flat = merged.reshape(planes * tiles * rows, LANES)

    def place(plane, _):
        source = [2 * plane * tiles * rows + tile * rows for tile in range(tiles)]
        target = [plane * tiles * rows + tile * rows for tile in range(tiles)]
        low = [held_flat[pl.ds(start, half, stride=2), :] for start in source]
        inner = [inner_ref[plane, tile] for tile in range(tiles // 2)]
        for tile, values in enumerate(unpack_tiles(0, low, inner)):
            merged_flat[pl.ds(target[tile], half, stride=2), :] = values
            odd = held_flat[pl.ds(source[tile] + 1, half, stride=2), :]
            merged_flat[pl.ds(target[tile] + 1, half, stride=2), :] = odd
        return 0

    for part in range(parts):
        loop(size, 4, lambda number, _: place(part * size + number, _))
        for tile in range(tiles):
            where = pl.ds(part * size, size)
            copies.append(copy(merged.at[where, tile], 0, tile, part, where))
            copies[-1].start()
    for one in copies:
        one.wait()


def local(field):
    depth, rows, lanes = field.shape
    vmem = pltpu.VMEM
    sizes = [(depth >> level, TILES >> level, rows >> level) for level in range(LEVELS)]
    scratch = [vmem((planes, tiles, height, LANES), f32) for planes, tiles, height in sizes[2:]]
    scratch += [
        pltpu.SemaphoreType.DMA((TILES,)),
        pltpu.SemaphoreType.DMA((LEVELS, 26)),
        pltpu.SemaphoreType.DMA((LEVELS, 26)),
    ]
    widths = [min(tiles, 2) * LANES for _, tiles, _ in sizes]
    scratch += [vmem((3 * (width + LANES), width), bf16) for width in widths]
    scratch += [vmem((6 * LANES, width), bf16) for width in widths]
    scratch += [vmem((3 * LANES, LANES), bf16) for _ in sizes]
    for planes, tiles, height in sizes:
        shapes = [(2, 2, tiles, height)] * 2 + [(2, 2, height)]
        shapes += [(2, planes, 8)] * 3 + [(tiles, 4 * planes)]
        shapes += [(2, 2, 2, 8)] * 2 + [(2, height)] * 2 + [(2, 2, height)]
        shapes += [(2, 2, 8)] * 4 + [(2, 2, 2, 2, 8)]
        scratch += [vmem((*shape, LANES), f32) for shape in shapes]
    scratch += [vmem((TILES // 2, 4 * depth, LANES), f32)]
    lifted = pl.pallas_call(
        functools.partial(kernel, field.shape),
        out_shape=[jax.ShapeDtypeStruct((size[0], size[1], size[2], LANES), f32) for size in sizes[:2]],
        in_specs=[pl.BlockSpec(memory_space=pltpu.HBM)],
        out_specs=[pl.BlockSpec(memory_space=pltpu.VMEM)] * 2,
        scratch_shapes=scratch,
        compiler_params=pltpu.CompilerParams(
            collective_id=0, has_side_effects=True, vmem_limit_bytes=48 * 2**20
        ),
        name="lift",
    )(field)
    return pl.pallas_call(
        write_out,
        out_shape=jax.ShapeDtypeStruct(field.shape, f32),
        in_specs=[pl.BlockSpec(memory_space=pltpu.VMEM)] * 2,
        out_specs=pl.BlockSpec(memory_space=pltpu.HBM),
        scratch_shapes=[
            vmem((depth // 2, TILES, rows, LANES), f32),
            pltpu.SemaphoreType.DMA((3, TILES)),
        ],
        compiler_params=pltpu.CompilerParams(vmem_limit_bytes=8 * 2**20),
        name="write_out",
    )(*lifted)


def solution(mesh):
    placed = (P("gz", "gx", "gy"),)
    return jax.shard_map(
        local, mesh=mesh, in_specs=placed, out_specs=P("gz", "gx", "gy"), check_vma=False
    )
```

```python
import functools

import jax
import jax.numpy as jnp
import numpy as np
from jax import lax
from jax.experimental import pallas as pl
from jax.experimental.pallas import tpu as pltpu
from jax.sharding import PartitionSpec as P

A = -1.586134342
B = -0.05298011854
G = 0.8829110762
E = 0.4435068522
Z = 1.149604398
MESH = pl.DeviceIdType.MESH
LANES = 128
TILES = 4
LEVELS = 3
SIDES = (0, 1)
f32, bf16 = jnp.float32, jnp.bfloat16


def filter_taps():
    u = np.eye(64)
    s, d = u[0::2].copy(), u[1::2].copy()
    d += A * (s + np.roll(s, -1, 0))
    s += B * (np.roll(d, 1, 0) + d)
    d += G * (s + np.roll(s, -1, 0))
    s += E * (np.roll(d, 1, 0) + d)
    low, high = s[16] * Z, d[16] / Z
    return [float(low[32 + o]) for o in range(5)], [float(high[33 + o]) for o in range(5)]


LOW, HIGH = filter_taps()

FROM_LEFT = {
    0: (Z * (B + E * (1 + 3 * G * B)), Z * E * G),
    1: (G * B / Z, 0.0),
    2: (Z * E * G * B, 0.0),
}
FROM_RIGHT = {
    -4: (Z * E * G * B * A, 0.0),
    -3: (G * B * A / Z, 0.0),
    -2: (Z * (B * A + E * (G * B * A + A * (1 + 2 * G * B))), Z * E * G),
    -1: (A * (1 + 2 * G * B) / Z, G / Z),
}


def cell_of(level, tile, lane):
    if level == 0:
        return tile * LANES + lane
    if level == 1:
        turn = lane & 1
        return ((tile + 2 * turn) * LANES + lane - turn) >> 1
    turn = lane & 3
    return (((turn >> 1) + 2 * (turn & 1)) * LANES + lane - turn) >> 2


def tap_weights(position, target):
    apart = jnp.abs(position - target)
    low = jnp.zeros(position.shape, f32)
    high = jnp.zeros(position.shape, f32)
    for o in range(5):
        low = jnp.where(apart == o, LOW[o], low)
        if o < 4:
            high = jnp.where(apart == o, HIGH[o], high)
    return jnp.where((target & 1) == 0, low, high)


def parts_of(values):
    top = values.astype(bf16)
    return top, (values - top.astype(f32)).astype(bf16)


def encode_end(s2, d2, s1, d1):
    return d1 + A * s1, s1 + B * (d2 + A * (s2 + s1))


def encode_start(s0, d0, s1):
    return s0, s0 + B * (d0 + A * (s0 + s1))


def lift_list(u, halo=None):
    s, d = list(u[0::2]), list(u[1::2])
    count = len(s)
    d_before = A * s[0]
    if halo is not None:
        d_before = d_before + halo[0]
    s_before = B * d_before
    if halo is not None:
        s_before = s_before + halo[1]
    for i in range(count - 1):
        d[i] = d[i] + A * (s[i] + s[i + 1])
    last = s[-1] if halo is None else s[-1] + halo[2]
    d[-1] = d[-1] + A * last
    s_after = B * d[-1]
    if halo is not None:
        s_after = s_after + halo[3]
    around = [d_before] + d
    s = [s[i] + B * (around[i] + around[i + 1]) for i in range(count)]
    d_before = d_before + G * (s_before + s[0])
    around = s + [s_after]
    d = [d[i] + G * (around[i] + around[i + 1]) for i in range(count)]
    around = [d_before] + d
    s = [s[i] + E * (around[i] + around[i + 1]) for i in range(count)]
    out = []
    for i in range(count):
        out += [s[i] * Z, d[i] * (1.0 / Z)]
    return out


def lift_rows(flat, start, height):
    half = height // 2
    pair = lax.broadcasted_iota(jnp.int32, (half, LANES), 0)
    even, odd = pl.ds(start, half, stride=2), pl.ds(start + 1, half, stride=2)
    s, d = flat[even, :], flat[odd, :]

    def after(values, last):
        return jnp.where(pair == half - 1, last, pltpu.roll(values, half - 1, 0))

    def before(values, first):
        return jnp.where(pair == 0, first, pltpu.roll(values, 1, 0))

    d_before = A * s[:1]
    d = d + A * (s + after(s, 0.0))
    s_after = B * d[half - 1 :]
    s_before = B * d_before
    s = s + B * (before(d, d_before) + d)
    d_before = d_before + G * (s_before + s[:1])
    d = d + G * (s + after(s, s_after))
    s = s + E * (before(d, d_before) + d)
    flat[even, :] = s * Z
    flat[odd, :] = d * (1.0 / Z)


def pack_tiles(level, tiles):
    lane = lax.broadcasted_iota(jnp.int32, tiles[0].shape, 1)
    step = 2**level
    keep = lane & (2 * step - 1) < step
    half = len(tiles) // 2
    return [jnp.where(keep, tiles[i], pltpu.roll(tiles[i + half], step, 1)) for i in range(half)]


def unpack_tiles(level, tiles, inner):
    lane = lax.broadcasted_iota(jnp.int32, tiles[0].shape, 1)
    step = 2**level
    keep = lane & (2 * step - 1) < step
    inner = list(inner) + [pltpu.roll(tile, LANES - step, 1) for tile in inner]
    return [jnp.where(keep, new, old) for new, old in zip(inner, tiles)]


def lift_lanes(tiles, ext, weights):
    first = lax.broadcasted_iota(jnp.int32, tiles[0].shape, 1) < LANES // 2
    blocks = [(tiles, ext)]
    if len(tiles) == 4:
        blocks = [(tiles[:2], jnp.where(first, tiles[2], ext)), (tiles[2:], jnp.where(first, ext, tiles[1]))]
    out = []
    for main, beside in blocks:
        main_top, main_low = parts_of(jnp.concatenate(main, axis=1))
        side_top, side_low = parts_of(beside)
        stacked = jnp.concatenate([main_top, main_low, main_top, side_top, side_low, side_top], axis=1)
        result = jnp.dot(stacked, weights[...], preferred_element_type=f32)
        out += [result[:, i * LANES : (i + 1) * LANES] for i in range(len(main))]
    return out


def loop(count, unroll, body, carry=0):
    unroll = min(unroll, count)

    def turns(number, carried):
        for inner in range(unroll):
            carried = body(number * unroll + inner, carried)
        return carried

    return lax.fori_loop(0, count // unroll, turns, carry)


NAMES = ("zs", "zr", "ze", "xs", "xr", "xe", "xl", "es", "er", "ys", "yr", "yp", "zys", "zyr", "xys", "xyr", "cr")
FIRST_NAMES = ("zl", "zc", "zlow", "zlowr")


def kernel(shape, field_ref, out_ref, inner_ref, *scratch):
    depth, rows, _ = shape
    refs = list(scratch)
    take = lambda: refs.pop(0)
    bodies = [out_ref, inner_ref, take()]
    load_sem, send_sem, recv_sem = take(), take(), take()
    y_weights, far_weights, z_weights = [[take() for _ in range(LEVELS)] for _ in range(3)]
    held = [{name: take() for name in NAMES} for _ in range(LEVELS)]
    held[0].update({name: take() for name in FIRST_NAMES})

    here = {name: lax.axis_index(name) for name in ("gx", "gy", "gz")}
    count = {name: lax.axis_size(name) for name in ("gx", "gy", "gz")}

    near = {
        name: {-1: lax.rem(at + count[name] - 1, count[name]), 0: at, 1: lax.rem(at + 1, count[name])}
        for name, at in here.items()
    }

    def beside(**by):
        return {name: near[name][way] for name, way in by.items()}

    barrier = pltpu.get_barrier_semaphore()
    for x in (-1, 0, 1):
        for y in (-1, 0, 1):
            for z in (-1, 0, 1):
                if (x, y, z) != (0, 0, 0):
                    pl.semaphore_signal(barrier, inc=1, device_id=beside(gx=x, gy=y, gz=z), device_id_type=MESH)

    loads = [
        [
            pltpu.make_async_copy(
                field_ref.at[pl.ds(first, size), :, pl.ds(tile * LANES, LANES)],
                out_ref.at[pl.ds(first, size), tile],
                load_sem.at[number, tile],
            )
            for tile in range(TILES)
        ]
        for number, (first, size) in enumerate(((0, 4), (depth - 4, 4), (4, depth - 8)))
    ]
    for part in loads:
        for load in part:
            load.start()

    def fill(ref, blocks):
        start = 0
        for values in blocks:
            top, low = parts_of(values)
            size = values.shape[0]
            for part in (top, top, low):
                ref[start : start + size] = part
                start += size

    def make_weights(level):
        window = 4 << level
        tiles = TILES >> level
        cells = (TILES * LANES) >> level
        width = min(tiles, 2) * LANES
        row = lax.broadcasted_iota(jnp.int32, (2 * LANES, width), 0)
        col = lax.broadcasted_iota(jnp.int32, (2 * LANES, width), 1)
        target = cell_of(level, col >> 7, col & 127)
        main = row[:width]
        side = row[:LANES]
        after, before = (2 * LANES, -LANES) if level == 0 else (cells, -cells)
        right = cell_of(level, 0, side) + after
        left = cell_of(level, 0 if level == 0 else tiles - 1, side) + before
        position = jnp.where(side < LANES // 2, right, left)
        fill(
            y_weights[level],
            [
                tap_weights(cell_of(level, main >> 7, main & 127), target[:width]),
                tap_weights(position, target[:LANES]),
            ],
        )
        inside = row & (window - 1)
        left = cell_of(level, tiles - 1, LANES - window + inside) - cells
        right = cell_of(level, 0, inside) + cells
        position = jnp.where(row < LANES, left, right)
        last = cell_of(level, tiles - 1, col & 127)
        target = jnp.where(col < LANES, cell_of(level, 0, col & 127), last)
        fill(far_weights[level], [tap_weights(position, target)])
        shift = 2 + level
        row, col = row[:LANES, :LANES], col[:LANES, :LANES]
        taps = tap_weights(row >> shift, col >> shift)
        fill(z_weights[level], [jnp.where((row & (window - 1)) == (col & (window - 1)), taps, 0.0)])

    make_weights(0)
    for part in loads[:2]:
        for load in part:
            load.wait()

    sends = []
    arrivals = [{} for _ in range(LEVELS)]
    way = (1, -1)
    sub = lax.broadcasted_iota(jnp.int32, (8, LANES), 0)
    lane8 = lax.broadcasted_iota(jnp.int32, (8, LANES), 1)
    last_half = lane8 >= LANES // 2
    none8 = jnp.zeros((8, LANES), f32)

    def extent(level):
        return depth >> level, TILES >> level, rows >> level, 4 << level

    def flat_of(ref):
        size = 1
        for extent_of_dim in ref.shape[:-1]:
            size *= extent_of_dim
        return ref.reshape(size, LANES)

    def wait_for(level, *keys):
        for key in keys:
            for copy in arrivals[level][key]:
                copy.wait_recv()

    def lift_layers(layers, low):
        _, tiles, height, _ = extent(0)
        layers_flat = flat_of(layers)

        def along_x(layer, _):
            for tile in range(tiles):
                lift_rows(layers_flat, (layer * tiles + tile) * height, height)
            return 0

        loop(4, 4, along_x)
        values = [layers[:, :, tile].reshape(4 * height, LANES) for tile in range(tiles)]
        lifted = lift_lanes(values, jnp.zeros((4 * height, LANES), f32), y_weights[0])
        for tile in range(tiles):
            layers[:, :, tile] = lifted[tile].reshape(2, 2, height, LANES)
        for layer in range(4):
            for tile, packed in enumerate(pack_tiles(0, low_tiles(layers_flat, layer))):
                low[layer // 2, layer % 2, tile] = packed

    def low_tiles(layers_flat, layer):
        _, tiles, height, _ = extent(0)
        return [
            layers_flat[pl.ds((layer * tiles + tile) * height, height // 2, stride=2), :] for tile in range(tiles)
        ]

    def start(level):
        planes, tiles, height, window = extent(level)
        body, flat, r = bodies[level], flat_of(bodies[level]), held[level]
        shift = 2 + level

        def send(key, number, source, target, **by):
            copy = pltpu.make_async_remote_copy(
                src_ref=source,
                dst_ref=target,
                send_sem=send_sem.at[level, number],
                recv_sem=recv_sem.at[level, number],
                device_id=beside(**by),
                device_id_type=MESH,
            )
            if not sends:
                pl.semaphore_wait(barrier, 26)
            copy.start()
            sends.append(copy)
            arrivals[level].setdefault(key, []).append(copy)

        zs, xs, es = r["zs"], r["xs"], r["es"]
        for tile in range(tiles):
            end = encode_end(*[body[planes - 4 + number, tile] for number in range(4)])
            begin = encode_start(*[body[number, tile] for number in range(3)])
            for k in range(2):
                zs[0, k, tile] = end[k]
                zs[1, k, tile] = begin[k]
                if level == 0:
                    r["zl"][0, k, tile] = end[k]
                    r["zl"][1, k, tile] = begin[k]
        if level == 0:
            lift_layers(r["zl"], r["zlow"])
            for side in SIDES:
                send("zlow", 26 + side, r["zlow"].at[side], r["zlowr"].at[side], gz=way[side])
            for load in loads[2]:
                load.wait()
        else:
            for side in SIDES:
                send("z", side, zs.at[side], r["zr"].at[side], gz=way[side])

        xs_flat = flat_of(xs)
        for tile in range(tiles):
            def at(number):
                return flat[pl.ds(tile * height + number, planes, stride=tiles * height), :]

            end = encode_end(*[at(height - 4 + number) for number in range(4)])
            begin = encode_start(*[at(number) for number in range(3)])
            for k in range(2):
                xs_flat[pl.ds(k * tiles + tile, planes, stride=8), :] = end[k]
                xs_flat[pl.ds(planes * 8 + k * tiles + tile, planes, stride=8), :] = begin[k]
        for side in SIDES:
            send("x", 2 + side, xs.at[side], r["xr"].at[side], gx=way[side])

        for side in SIDES:
            end = encode_end(*[xs[side, planes - 4 + number] for number in range(4)])
            begin = encode_start(*[xs[side, number] for number in range(3)])
            for k in range(2):
                es[side, 0, k] = end[k]
                es[side, 1, k] = begin[k]
        for sx in SIDES:
            for sz in SIDES:
                number = 4 + 2 * sx + sz
                send("e", number, es.at[sx, sz], r["er"].at[sx, sz], gx=way[sx], gz=way[sz])
                for sy in SIDES:
                    number = 8 + 4 * sx + 2 * sz + sy
                    send("c", number, es.at[sx, sz], r["cr"].at[sx, sz, sy], gx=way[sx], gz=way[sz], gy=way[sy])

        lane = lax.broadcasted_iota(jnp.int32, (height, LANES), 1)

        def pack(plane, carried):
            to_right, to_left, x_right, x_left = carried
            tail_by = lax.rem(plane * window + window, LANES)
            head_by = plane * window
            mine = lane >> shift == plane
            to_right = jnp.where(mine, pltpu.roll(body[plane, tiles - 1], tail_by, 1), to_right)
            to_left = jnp.where(mine, pltpu.roll(body[plane, 0], head_by, 1), to_left)
            mine = lane8 >> shift == plane
            x_right = tuple(jnp.where(mine, pltpu.roll(xs[sx, plane], tail_by, 1), x_right[sx]) for sx in SIDES)
            x_left = tuple(jnp.where(mine, pltpu.roll(xs[sx, plane], head_by, 1), x_left[sx]) for sx in SIDES)
            return to_right, to_left, x_right, x_left

        none = jnp.zeros((height, LANES), f32)
        to_right, to_left, x_right, x_left = loop(
            planes, 4, pack, (none, none, (none8, none8), (none8, none8))
        )
        r["ys"][0], r["ys"][1] = to_right, to_left
        for sx in SIDES:
            r["xys"][0, sx], r["xys"][1, sx] = x_right[sx], x_left[sx]
        groups = height // 8
        for sz in SIDES:
            tail = head = none8
            for k in range(2):
                for group in range(groups):
                    slot = k * groups + group
                    mine = lane8 >> shift == slot
                    part = pl.ds(group * 8, 8)
                    by = (slot * window + window) % LANES
                    tail = jnp.where(mine, pltpu.roll(zs[sz, k, tiles - 1, part, :], by, 1), tail)
                    head = jnp.where(mine, pltpu.roll(zs[sz, k, 0, part, :], slot * window, 1), head)
            r["zys"][0, sz], r["zys"][1, sz] = tail, head
        for sy in SIDES:
            send("y", 16 + sy, r["ys"].at[sy], r["yr"].at[sy], gy=way[sy])
            for s in SIDES:
                send("xy", 18 + 2 * sy + s, r["xys"].at[sy, s], r["xyr"].at[sy, s], gy=way[sy], gx=way[s])
                send("zy", 22 + 2 * sy + s, r["zys"].at[sy, s], r["zyr"].at[sy, s], gy=way[sy], gz=way[s])
        if level == 0:
            for side in SIDES:
                send("z", side, r["zl"].at[side], r["zr"].at[side], gz=way[side])

    def own_x(level):
        planes, tiles, height, _ = extent(level)
        flat = flat_of(bodies[level])

        def along_x(plane, _):
            for tile in range(tiles):
                lift_rows(flat, (plane * tiles + tile) * height, height)
            return 0

        loop(planes, 2 if level == 0 else 4, along_x)

    def own_z(level, parity=None):
        planes, tiles, height, _ = extent(level)
        flat = flat_of(bodies[level])
        every = 1 if parity is None else 2
        groups = height // (8 * every)

        def along_z(block, _):
            tile, group = block // groups, block % groups
            first = tile * height + group * 8 * every
            if parity is None:
                first = pl.multiple_of(first, 8)
                where = [pl.ds(first + plane * tiles * height, 8) for plane in range(planes)]
            else:
                where = [pl.ds(first + parity + plane * tiles * height, 8, stride=2) for plane in range(planes)]
            lifted = lift_list([flat[at, :] for at in where])
            for at, values in zip(where, lifted):
                flat[at, :] = values
            return 0

        loop(tiles * groups, 1 if level == 0 else 2, along_z)

    def own_y(level, start=0, stop=None):
        planes, tiles, height, _ = extent(level)
        body = bodies[level]
        chunk = min(planes, 512 // height)

        def along_y(number, _):
            where = pl.ds(number * chunk, chunk)
            values = [body[where, tile].reshape(chunk * height, LANES) for tile in range(tiles)]
            lifted = lift_lanes(values, jnp.zeros((chunk * height, LANES), f32), y_weights[level])
            for tile in range(tiles):
                body[where, tile] = lifted[tile].reshape(chunk, height, LANES)
            return 0

        lax.fori_loop(start, planes // chunk if stop is None else stop, along_y, 0)

    def prepare_y(level):
        height = extent(level)[2]
        r = held[level]
        for sy in SIDES:
            lift_rows(r["yr"].at[sy], 0, height)
            top, low = parts_of(r["yr"][sy])
            stacked = jnp.concatenate([top, low, top], axis=1)
            values = jnp.dot(stacked, z_weights[level][...], preferred_element_type=f32)
            top = values.astype(bf16).astype(f32)
            r["yp"][0, sy] = top
            r["yp"][1, sy] = values - top

    def spread_y(level, planes, pick):
        height = extent(level)[2]
        shift = 2 + level
        yp = held[level]["yp"]
        parts = [[pick(yp.at[part, sy]) for sy in SIDES] for part in range(2)]
        lane = lax.broadcasted_iota(jnp.int32, parts[0][0].shape, 1)
        stacks = []
        for plane in planes:
            mine = lane >> shift == plane
            top, low = [[jnp.where(mine, values, 0.0).astype(bf16) for values in part] for part in parts]
            stacks.append(jnp.concatenate(top + low + top, axis=1))
        return jnp.dot(jnp.concatenate(stacks, axis=0), far_weights[level][...], preferred_element_type=f32)

    def prepare_x(level):
        planes, tiles, height, window = extent(level)
        r = held[level]
        xr, xe, xl = r["xr"], r["xe"], r["xl"]

        def aligned(values):
            return pltpu.roll(values, 9 - tiles, 0) if tiles > 1 else values

        lefts = [aligned(r["xyr"][0, sx]) for sx in SIDES]
        rights = [r["xyr"][1, sx] for sx in SIDES]

        def unpack(plane, _):
            left_by = lax.rem(2 * LANES - window - plane * window, LANES)
            right_by = lax.rem(LANES - plane * window, LANES)
            for sx in SIDES:
                xe[sx, plane] = jnp.where(
                    last_half, pltpu.roll(lefts[sx], left_by, 1), pltpu.roll(rights[sx], right_by, 1)
                )
            return 0

        loop(planes, 8, unpack)
        for sx in SIDES:
            halo = [r["er"][sx, sz, k] for sz in SIDES for k in range(2)]
            lifted = lift_list([xr[sx, plane] for plane in range(planes)], halo)
            for plane in range(planes):
                xr[sx, plane] = lifted[plane]
            halo = [
                jnp.where(last_half, aligned(r["cr"][sx, sz, 0, k]), r["cr"][sx, sz, 1, k])
                for sz in SIDES
                for k in range(2)
            ]
            lifted = lift_list([xe[sx, plane] for plane in range(planes)], halo)
            for plane in range(planes):
                xe[sx, plane] = lifted[plane]
        xr_flat, xe_flat = flat_of(xr), flat_of(xe)

        def strip(ref, start):
            return ref[pl.ds(start, 2 * planes, stride=8), :]

        values = [
            jnp.concatenate([strip(xr_flat, k * tiles + tile) for k in range(2)], axis=0) for tile in range(tiles)
        ]
        ext = jnp.concatenate([strip(xe_flat, k * tiles) for k in range(2)], axis=0)
        lifted = lift_lanes(values, ext, y_weights[level])
        for tile in range(tiles):
            xl[tile] = lifted[tile]

    def prepare_z(level):
        planes, tiles, height, window = extent(level)
        r = held[level]
        zr, ze = r["zr"], r["ze"]
        zr_flat, ze_flat = flat_of(zr), flat_of(ze)
        groups = height // 8
        wait_for(level, "zy")
        for sz in SIDES:
            for k in range(2):
                for group in range(groups):
                    slot = k * groups + group
                    left = pltpu.roll(r["zyr"][0, sz], (2 * LANES - window - slot * window) % LANES, 1)
                    right = pltpu.roll(r["zyr"][1, sz], (LANES - slot * window) % LANES, 1)
                    ze[sz, k, pl.ds(group * 8, 8), :] = jnp.where(last_half, left, right)
        if level == 0:
            for layer in range(4):
                lift_rows(ze_flat, layer * height, height)
            ext = ze[...].reshape(4 * height, LANES)
            first = lax.broadcasted_iota(jnp.int32, ext.shape, 1) < LANES // 2
            side_weights = y_weights[0][6 * LANES :]
            for block in range(2):
                top, low = parts_of(jnp.where(first, 0.0, ext) if block == 0 else jnp.where(first, ext, 0.0))
                stacked = jnp.concatenate([top, low, top], axis=1)
                added = jnp.dot(stacked, side_weights, preferred_element_type=f32)
                for tile in range(2):
                    part = added[:, tile * LANES : (tile + 1) * LANES]
                    r["zc"][:, :, 2 * block + tile] = part.reshape(2, 2, height, LANES)
            return
        wait_for(level, "z")

        def along_x(layer, _):
            for tile in range(tiles):
                lift_rows(zr_flat, (layer * tiles + tile) * height, height)
            lift_rows(ze_flat, layer * height, height)
            return 0

        loop(4, 4, along_x)
        values = [zr[:, :, tile].reshape(4 * height, LANES) for tile in range(tiles)]
        lifted = lift_lanes(values, ze[...].reshape(4 * height, LANES), y_weights[level])
        for tile in range(tiles):
            zr[:, :, tile] = lifted[tile].reshape(2, 2, height, LANES)

    def row_weights(table, layer, at):
        values = none8
        for number, weights in table.items():
            place = at(number)
            if place is not None and weights[layer] != 0.0:
                values = jnp.where(sub == place, weights[layer], values)
        return values

    def add_y(level):
        planes, tiles, height, _ = extent(level)
        body = bodies[level]
        chunk = min(planes, 512 // height)

        def add(number, _):
            where = pl.ds(number * chunk, chunk)
            added = spread_y(level, [number * chunk + inner for inner in range(chunk)], lambda ref: ref[...])
            body[where, 0] = body[where, 0] + added[:, :LANES].reshape(chunk, height, LANES)
            if tiles > 1:
                body[where, tiles - 1] = body[where, tiles - 1] + added[:, LANES:].reshape(chunk, height, LANES)
            return 0

        lax.fori_loop(0, planes // chunk, add, 0)

    def add_x_rows(body, planes, every, height, strips, at):
        tables = ((FROM_LEFT, 0), (FROM_RIGHT, height - 8))
        weigh = [[row_weights(table, layer, at) for layer in range(2)] for table, _ in tables]

        def add(number, _):
            for tile in range(body.shape[1]):
                strip = strips(tile)
                for side in SIDES:
                    part = pl.ds(tables[side][1], 8)
                    first = side * planes + number * every
                    added = weigh[side][0] * strip[pl.ds(first, 1), :]
                    added = added + weigh[side][1] * strip[pl.ds(2 * planes + first, 1), :]
                    body[number, tile, part, :] = body[number, tile, part, :] + added
            return 0

        loop(planes // every, 4, add)

    def add_x(level):
        planes, _, height, _ = extent(level)
        xl = held[level]["xl"]
        add_x_rows(bodies[level], planes, 1, height, lambda tile: xl.at[tile], lambda number: number % 8)

    def add_z(level):
        planes, tiles, _, _ = extent(level)
        body, zr = bodies[level], held[level]["zr"]
        if level == 0:
            wait_for(0, "z")
            for side in SIDES:
                for k in range(2):
                    for tile in range(tiles):
                        zr[side, k, tile] = zr[side, k, tile] + held[0]["zc"][side, k, tile]
        for side, table in ((0, FROM_LEFT), (1, FROM_RIGHT)):
            for number, (one, two) in table.items():
                plane = number % planes
                for tile in range(tiles):
                    added = one * zr[side, 0, tile]
                    if two != 0.0:
                        added = added + two * zr[side, 1, tile]
                    body[plane, tile] = body[plane, tile] + added

    start(0)
    own_x(0)
    own_z(0, 0)
    planes, tiles, height, _ = extent(0)
    half, deep = height // 2, planes // 2
    inner, inner_tiles = bodies[1], tiles // 2
    flat = flat_of(bodies[0])
    tops = list(range(0, planes, 2))

    def low_rows(ref_flat, start_of):
        return ref_flat[pl.ds(start_of, half, stride=2), :]

    values = [
        jnp.concatenate([low_rows(flat, (plane * tiles + tile) * height) for plane in tops], axis=0)
        for tile in range(tiles)
    ]
    lifted = lift_lanes(values, jnp.zeros((deep * half, LANES), f32), y_weights[0])
    for tile, packed in enumerate(pack_tiles(0, lifted)):
        inner[:, tile] = packed.reshape(deep, half, LANES)

    wait_for(0, "y")
    prepare_y(0)
    added = spread_y(0, tops, lambda ref: ref[pl.ds(0, half, stride=2), :])
    keep = (lax.broadcasted_iota(jnp.int32, (deep * half, LANES), 1) & 1) == 0
    first = jnp.where(keep, added[:, :LANES], 0.0)
    last = jnp.where(keep, 0.0, pltpu.roll(added[:, LANES:], 1, 1))
    inner[:, 0] = inner[:, 0] + first.reshape(deep, half, LANES)
    inner[:, inner_tiles - 1] = inner[:, inner_tiles - 1] + last.reshape(deep, half, LANES)

    wait_for(0, "x", "e", "c", "xy")
    prepare_x(0)
    xl, xp = held[0]["xl"], take()
    for tile, packed in enumerate(pack_tiles(0, [xl[tile] for tile in range(tiles)])):
        xp[tile] = packed

    def even_row(number):
        return (number % 16) // 2 % 8 if number % 2 == 0 else None

    add_x_rows(inner, planes, 2, half, lambda tile: xp.at[tile], even_row)
    prepare_z(0)
    zc_flat = flat_of(held[0]["zc"])
    packed_layers = [pack_tiles(0, low_tiles(zc_flat, layer)) for layer in range(4)]
    wait_for(0, "zlow")
    for side, table in ((0, FROM_LEFT), (1, FROM_RIGHT)):
        packed = [
            [held[0]["zlowr"][side, k, tile] + packed_layers[2 * side + k][tile] for tile in range(inner_tiles)]
            for k in range(2)
        ]
        for number, (one, two) in table.items():
            if number % 2 == 0:
                plane = (number % planes) // 2
                for tile in range(inner_tiles):
                    added = one * packed[0][tile]
                    if two != 0.0:
                        added = added + two * packed[1][tile]
                    inner[plane, tile] = inner[plane, tile] + added

    start(1)
    make_weights(1)
    own_x(1)
    own_z(1)
    own_y(1)
    own_z(0, 1)
    own_y(0, 0, 2)
    wait_for(1, "y")
    prepare_y(1)
    add_y(1)
    wait_for(1, "x", "e", "c", "xy")
    prepare_x(1)
    add_x(1)
    prepare_z(1)
    add_z(1)
    planes, tiles, height, _ = extent(1)
    half = height // 2
    flat = flat_of(bodies[1])

    def pick(plane, _):
        values = [flat[pl.ds((2 * plane * tiles + tile) * height, half, stride=2), :] for tile in range(tiles)]
        for tile, packed in enumerate(pack_tiles(1, values)):
            bodies[2][plane, tile] = packed
        return 0

    loop(planes // 2, 4, pick)

    start(2)
    make_weights(2)
    own_x(2)
    own_z(2)
    own_y(2)
    own_y(0, 2)
    add_y(0)
    add_x(0)
    add_z(0)
    wait_for(2, "y")
    prepare_y(2)
    add_y(2)
    wait_for(2, "x", "e", "c", "xy")
    prepare_x(2)
    add_x(2)
    prepare_z(2)
    add_z(2)

    planes, tiles, height, _ = extent(1)
    half = height // 2

    def place(plane, _):
        where = [pl.ds((2 * plane * tiles + tile) * height, half, stride=2) for tile in range(tiles)]
        inner = [bodies[2][plane, tile] for tile in range(tiles // 2)]
        for at, values in zip(where, unpack_tiles(1, [flat[at, :] for at in where], inner)):
            flat[at, :] = values
        return 0

    loop(planes // 2, 4, place)

    for copy in sends:
        copy.wait_send()


def write_out(held_ref, inner_ref, out_ref, merged, sem):
    depth, tiles, rows, _ = held_ref.shape
    planes, half = depth // 2, rows // 2
    pairs = held_ref.reshape(planes, 2, tiles, rows, LANES)
    target = out_ref.reshape(planes, 2, rows, tiles * LANES)
    parts = sem.shape[0] - 1
    size = planes // parts

    def copy(source, odd, tile, slot, where):
        return pltpu.make_async_copy(
            source, target.at[where, odd, :, pl.ds(tile * LANES, LANES)], sem.at[slot, tile]
        )

    copies = [copy(pairs.at[:, 1, tile], 1, tile, parts, pl.ds(0, planes)) for tile in range(tiles)]
    for one in copies:
        one.start()
    held_flat = held_ref.reshape(depth * tiles * rows, LANES)
    merged_flat = merged.reshape(planes * tiles * rows, LANES)

    def place(plane, _):
        source = [2 * plane * tiles * rows + tile * rows for tile in range(tiles)]
        target = [plane * tiles * rows + tile * rows for tile in range(tiles)]
        low = [held_flat[pl.ds(start, half, stride=2), :] for start in source]
        inner = [inner_ref[plane, tile] for tile in range(tiles // 2)]
        for tile, values in enumerate(unpack_tiles(0, low, inner)):
            merged_flat[pl.ds(target[tile], half, stride=2), :] = values
            odd = held_flat[pl.ds(source[tile] + 1, half, stride=2), :]
            merged_flat[pl.ds(target[tile] + 1, half, stride=2), :] = odd
        return 0

    for part in range(parts):
        loop(size, 4, lambda number, _: place(part * size + number, _))
        for tile in range(tiles):
            where = pl.ds(part * size, size)
            copies.append(copy(merged.at[where, tile], 0, tile, part, where))
            copies[-1].start()
    for one in copies:
        one.wait()


def local(field):
    depth, rows, lanes = field.shape
    vmem = pltpu.VMEM
    sizes = [(depth >> level, TILES >> level, rows >> level) for level in range(LEVELS)]
    scratch = [vmem((planes, tiles, height, LANES), f32) for planes, tiles, height in sizes[2:]]
    scratch += [
        pltpu.SemaphoreType.DMA((3, TILES)),
        pltpu.SemaphoreType.DMA((LEVELS, 28)),
        pltpu.SemaphoreType.DMA((LEVELS, 28)),
    ]
    widths = [min(tiles, 2) * LANES for _, tiles, _ in sizes]
    scratch += [vmem((3 * (width + LANES), width), bf16) for width in widths]
    scratch += [vmem((6 * LANES, width), bf16) for width in widths]
    scratch += [vmem((3 * LANES, LANES), bf16) for _ in sizes]
    for planes, tiles, height in sizes:
        shapes = [(2, 2, tiles, height)] * 2 + [(2, 2, height)]
        shapes += [(2, planes, 8)] * 3 + [(tiles, 4 * planes)]
        shapes += [(2, 2, 2, 8)] * 2 + [(2, height)] * 2 + [(2, 2, height)]
        shapes += [(2, 2, 8)] * 4 + [(2, 2, 2, 2, 8)]
        scratch += [vmem((*shape, LANES), f32) for shape in shapes]
    scratch += [vmem((2, 2, TILES, rows, LANES), f32)] * 2 + [vmem((2, 2, TILES // 2, rows // 2, LANES), f32)] * 2
    scratch += [vmem((TILES // 2, 4 * depth, LANES), f32)]
    lifted = pl.pallas_call(
        functools.partial(kernel, field.shape),
        out_shape=[jax.ShapeDtypeStruct((size[0], size[1], size[2], LANES), f32) for size in sizes[:2]],
        in_specs=[pl.BlockSpec(memory_space=pltpu.HBM)],
        out_specs=[pl.BlockSpec(memory_space=pltpu.VMEM)] * 2,
        scratch_shapes=scratch,
        compiler_params=pltpu.CompilerParams(
            collective_id=0, has_side_effects=True, vmem_limit_bytes=48 * 2**20
        ),
        name="lift",
    )(field)
    return pl.pallas_call(
        write_out,
        out_shape=jax.ShapeDtypeStruct(field.shape, f32),
        in_specs=[pl.BlockSpec(memory_space=pltpu.VMEM)] * 2,
        out_specs=pl.BlockSpec(memory_space=pltpu.HBM),
        scratch_shapes=[
            vmem((depth // 2, TILES, rows, LANES), f32),
            pltpu.SemaphoreType.DMA((3, TILES)),
        ],
        compiler_params=pltpu.CompilerParams(vmem_limit_bytes=8 * 2**20),
        name="write_out",
    )(*lifted)


def solution(mesh):
    placed = (P("gz", "gx", "gy"),)
    return jax.shard_map(
        local, mesh=mesh, in_specs=placed, out_specs=P("gz", "gx", "gy"), check_vma=False
    )
```

```python
import functools

import jax
import jax.numpy as jnp
import numpy as np
from jax import lax
from jax.experimental import pallas as pl
from jax.experimental.pallas import tpu as pltpu
from jax.sharding import PartitionSpec as P

A = -1.586134342
B = -0.05298011854
G = 0.8829110762
E = 0.4435068522
Z = 1.149604398
MESH = pl.DeviceIdType.MESH
LANES = 128
TILES = 4
LEVELS = 3
SIDES = (0, 1)
f32, bf16 = jnp.float32, jnp.bfloat16


def filter_taps():
    u = np.eye(64)
    s, d = u[0::2].copy(), u[1::2].copy()
    d += A * (s + np.roll(s, -1, 0))
    s += B * (np.roll(d, 1, 0) + d)
    d += G * (s + np.roll(s, -1, 0))
    s += E * (np.roll(d, 1, 0) + d)
    low, high = s[16] * Z, d[16] / Z
    return [float(low[32 + o]) for o in range(5)], [float(high[33 + o]) for o in range(5)]


LOW, HIGH = filter_taps()

FROM_LEFT = {
    0: (Z * (B + E * (1 + 3 * G * B)), Z * E * G),
    1: (G * B / Z, 0.0),
    2: (Z * E * G * B, 0.0),
}
FROM_RIGHT = {
    -4: (Z * E * G * B * A, 0.0),
    -3: (G * B * A / Z, 0.0),
    -2: (Z * (B * A + E * (G * B * A + A * (1 + 2 * G * B))), Z * E * G),
    -1: (A * (1 + 2 * G * B) / Z, G / Z),
}


def cell_of(level, tile, lane):
    if level == 0:
        return tile * LANES + lane
    if level == 1:
        turn = lane & 1
        return ((tile + 2 * turn) * LANES + lane - turn) >> 1
    turn = lane & 3
    return (((turn >> 1) + 2 * (turn & 1)) * LANES + lane - turn) >> 2


def tap_weights(position, target):
    apart = jnp.abs(position - target)
    low = jnp.zeros(position.shape, f32)
    high = jnp.zeros(position.shape, f32)
    for o in range(5):
        low = jnp.where(apart == o, LOW[o], low)
        if o < 4:
            high = jnp.where(apart == o, HIGH[o], high)
    return jnp.where((target & 1) == 0, low, high)


def parts_of(values):
    top = values.astype(bf16)
    return top, (values - top.astype(f32)).astype(bf16)


def encode_end(s2, d2, s1, d1):
    return d1 + A * s1, s1 + B * (d2 + A * (s2 + s1))


def encode_start(s0, d0, s1):
    return s0, s0 + B * (d0 + A * (s0 + s1))


def lift_list(u, halo=None):
    s, d = list(u[0::2]), list(u[1::2])
    count = len(s)
    d_before = A * s[0]
    if halo is not None:
        d_before = d_before + halo[0]
    s_before = B * d_before
    if halo is not None:
        s_before = s_before + halo[1]
    for i in range(count - 1):
        d[i] = d[i] + A * (s[i] + s[i + 1])
    last = s[-1] if halo is None else s[-1] + halo[2]
    d[-1] = d[-1] + A * last
    s_after = B * d[-1]
    if halo is not None:
        s_after = s_after + halo[3]
    around = [d_before] + d
    s = [s[i] + B * (around[i] + around[i + 1]) for i in range(count)]
    d_before = d_before + G * (s_before + s[0])
    around = s + [s_after]
    d = [d[i] + G * (around[i] + around[i + 1]) for i in range(count)]
    around = [d_before] + d
    s = [s[i] + E * (around[i] + around[i + 1]) for i in range(count)]
    out = []
    for i in range(count):
        out += [s[i] * Z, d[i] * (1.0 / Z)]
    return out


def lift_rows(flat, start, height):
    half = height // 2
    pair = lax.broadcasted_iota(jnp.int32, (half, LANES), 0)
    even, odd = pl.ds(start, half, stride=2), pl.ds(start + 1, half, stride=2)
    s, d = flat[even, :], flat[odd, :]

    def after(values, last):
        return jnp.where(pair == half - 1, last, pltpu.roll(values, half - 1, 0))

    def before(values, first):
        return jnp.where(pair == 0, first, pltpu.roll(values, 1, 0))

    d_before = A * s[:1]
    d = d + A * (s + after(s, 0.0))
    s_after = B * d[half - 1 :]
    s_before = B * d_before
    s = s + B * (before(d, d_before) + d)
    d_before = d_before + G * (s_before + s[:1])
    d = d + G * (s + after(s, s_after))
    s = s + E * (before(d, d_before) + d)
    flat[even, :] = s * Z
    flat[odd, :] = d * (1.0 / Z)


def pack_tiles(level, tiles):
    lane = lax.broadcasted_iota(jnp.int32, tiles[0].shape, 1)
    step = 2**level
    keep = lane & (2 * step - 1) < step
    half = len(tiles) // 2
    return [jnp.where(keep, tiles[i], pltpu.roll(tiles[i + half], step, 1)) for i in range(half)]


def unpack_tiles(level, tiles, inner):
    lane = lax.broadcasted_iota(jnp.int32, tiles[0].shape, 1)
    step = 2**level
    keep = lane & (2 * step - 1) < step
    inner = list(inner) + [pltpu.roll(tile, LANES - step, 1) for tile in inner]
    return [jnp.where(keep, new, old) for new, old in zip(inner, tiles)]


def lift_lanes(tiles, ext, weights):
    first = lax.broadcasted_iota(jnp.int32, tiles[0].shape, 1) < LANES // 2
    blocks = [(tiles, ext)]
    if len(tiles) == 4:
        blocks = [(tiles[:2], jnp.where(first, tiles[2], ext)), (tiles[2:], jnp.where(first, ext, tiles[1]))]
    out = []
    for main, beside in blocks:
        main_top, main_low = parts_of(jnp.concatenate(main, axis=1))
        side_top, side_low = parts_of(beside)
        stacked = jnp.concatenate([main_top, main_low, main_top, side_top, side_low, side_top], axis=1)
        result = jnp.dot(stacked, weights[...], preferred_element_type=f32)
        out += [result[:, i * LANES : (i + 1) * LANES] for i in range(len(main))]
    return out


def loop(count, unroll, body, carry=0):
    unroll = min(unroll, count)

    def turns(number, carried):
        for inner in range(unroll):
            carried = body(number * unroll + inner, carried)
        return carried

    return lax.fori_loop(0, count // unroll, turns, carry)


NAMES = ("zs", "zr", "ze", "xs", "xr", "xe", "xl", "es", "er", "ys", "yr", "yp", "zys", "zyr", "xys", "xyr", "cr")
GROUPS = {"y": 0, "x": 1, "e": 1, "c": 1, "xy": 1, "zy": 2, "z": 3, "zlow": 4}
FIRST_NAMES = ("zl", "zc", "zlow", "zlowr")


def kernel(shape, field_ref, out_ref, inner_ref, *scratch):
    depth, rows, _ = shape
    refs = list(scratch)
    take = lambda: refs.pop(0)
    bodies = [out_ref, inner_ref, take()]
    load_sem, send_sem, recv_sem = take(), take(), take()
    y_weights, far_weights, z_weights = [[take() for _ in range(LEVELS)] for _ in range(3)]
    held = [{name: take() for name in NAMES} for _ in range(LEVELS)]
    held[0].update({name: take() for name in FIRST_NAMES})

    here = {name: lax.axis_index(name) for name in ("gx", "gy", "gz")}
    count = {name: lax.axis_size(name) for name in ("gx", "gy", "gz")}

    near = {
        name: {-1: lax.rem(at + count[name] - 1, count[name]), 0: at, 1: lax.rem(at + 1, count[name])}
        for name, at in here.items()
    }

    def beside(**by):
        return {name: near[name][way] for name, way in by.items()}

    barrier = pltpu.get_barrier_semaphore()
    for x in (-1, 0, 1):
        for y in (-1, 0, 1):
            for z in (-1, 0, 1):
                if (x, y, z) != (0, 0, 0):
                    pl.semaphore_signal(barrier, inc=1, device_id=beside(gx=x, gy=y, gz=z), device_id_type=MESH)

    loads = [
        [
            pltpu.make_async_copy(
                field_ref.at[pl.ds(first, size), :, pl.ds(tile * LANES, LANES)],
                out_ref.at[pl.ds(first, size), tile],
                load_sem.at[number, tile],
            )
            for tile in range(TILES)
        ]
        for number, (first, size) in enumerate(((0, 4), (depth - 4, 4), (4, depth - 8)))
    ]
    for part in loads:
        for load in part:
            load.start()

    def fill(ref, blocks):
        start = 0
        for values in blocks:
            top, low = parts_of(values)
            size = values.shape[0]
            for part in (top, top, low):
                ref[start : start + size] = part
                start += size

    def make_weights(level):
        window = 4 << level
        tiles = TILES >> level
        cells = (TILES * LANES) >> level
        width = min(tiles, 2) * LANES
        row = lax.broadcasted_iota(jnp.int32, (2 * LANES, width), 0)
        col = lax.broadcasted_iota(jnp.int32, (2 * LANES, width), 1)
        target = cell_of(level, col >> 7, col & 127)
        main = row[:width]
        side = row[:LANES]
        after, before = (2 * LANES, -LANES) if level == 0 else (cells, -cells)
        right = cell_of(level, 0, side) + after
        left = cell_of(level, 0 if level == 0 else tiles - 1, side) + before
        position = jnp.where(side < LANES // 2, right, left)
        fill(
            y_weights[level],
            [
                tap_weights(cell_of(level, main >> 7, main & 127), target[:width]),
                tap_weights(position, target[:LANES]),
            ],
        )
        inside = row & (window - 1)
        left = cell_of(level, tiles - 1, LANES - window + inside) - cells
        right = cell_of(level, 0, inside) + cells
        position = jnp.where(row < LANES, left, right)
        last = cell_of(level, tiles - 1, col & 127)
        target = jnp.where(col < LANES, cell_of(level, 0, col & 127), last)
        fill(far_weights[level], [tap_weights(position, target)])
        shift = 2 + level
        row, col = row[:LANES, :LANES], col[:LANES, :LANES]
        taps = tap_weights(row >> shift, col >> shift)
        fill(z_weights[level], [jnp.where((row & (window - 1)) == (col & (window - 1)), taps, 0.0)])

    make_weights(0)
    for part in loads[:2]:
        for load in part:
            load.wait()

    sent = [0] * LEVELS
    arriving = [[0] * 5 for _ in range(LEVELS)]
    way = (1, -1)
    sub = lax.broadcasted_iota(jnp.int32, (8, LANES), 0)
    lane8 = lax.broadcasted_iota(jnp.int32, (8, LANES), 1)
    last_half = lane8 >= LANES // 2
    none8 = jnp.zeros((8, LANES), f32)

    def extent(level):
        return depth >> level, TILES >> level, rows >> level, 4 << level

    def flat_of(ref):
        size = 1
        for extent_of_dim in ref.shape[:-1]:
            size *= extent_of_dim
        return ref.reshape(size, LANES)

    def wait_rows(sem, count):
        held_rows = flat_of(out_ref).at[pl.ds(0, count)]
        pltpu.make_async_copy(held_rows, held_rows, sem).wait()

    def wait_for(level, key):
        wait_rows(recv_sem.at[level, GROUPS[key]], arriving[level][GROUPS[key]])

    def lift_layers(layers, low):
        _, tiles, height, _ = extent(0)
        layers_flat = flat_of(layers)

        def along_x(layer, _):
            for tile in range(tiles):
                lift_rows(layers_flat, (layer * tiles + tile) * height, height)
            return 0

        loop(4, 4, along_x)
        values = [layers[:, :, tile].reshape(4 * height, LANES) for tile in range(tiles)]
        lifted = lift_lanes(values, jnp.zeros((4 * height, LANES), f32), y_weights[0])
        for tile in range(tiles):
            layers[:, :, tile] = lifted[tile].reshape(2, 2, height, LANES)
        for layer in range(4):
            for tile, packed in enumerate(pack_tiles(0, low_tiles(layers_flat, layer))):
                low[layer // 2, layer % 2, tile] = packed

    def low_tiles(layers_flat, layer):
        _, tiles, height, _ = extent(0)
        return [
            layers_flat[pl.ds((layer * tiles + tile) * height, height // 2, stride=2), :] for tile in range(tiles)
        ]

    def start(level):
        planes, tiles, height, window = extent(level)
        body, flat, r = bodies[level], flat_of(bodies[level]), held[level]
        shift = 2 + level

        def send(key, source, target, **by):
            copy = pltpu.make_async_remote_copy(
                src_ref=source,
                dst_ref=target,
                send_sem=send_sem.at[level],
                recv_sem=recv_sem.at[level, GROUPS[key]],
                device_id=beside(**by),
                device_id_type=MESH,
            )
            if level == 0 and not sent[0]:
                pl.semaphore_wait(barrier, 26)
            copy.start()
            size = 1
            for extent_of_dim in source.shape[:-1]:
                size *= extent_of_dim
            sent[level] += size
            arriving[level][GROUPS[key]] += size

        zs, xs, es = r["zs"], r["xs"], r["es"]
        for tile in range(tiles):
            end = encode_end(*[body[planes - 4 + number, tile] for number in range(4)])
            begin = encode_start(*[body[number, tile] for number in range(3)])
            for k in range(2):
                zs[0, k, tile] = end[k]
                zs[1, k, tile] = begin[k]
                if level == 0:
                    r["zl"][0, k, tile] = end[k]
                    r["zl"][1, k, tile] = begin[k]
        if level == 0:
            lift_layers(r["zl"], r["zlow"])
            for side in SIDES:
                send("zlow", r["zlow"].at[side], r["zlowr"].at[side], gz=way[side])
            for load in loads[2]:
                load.wait()
        else:
            for side in SIDES:
                send("z", zs.at[side], r["zr"].at[side], gz=way[side])

        xs_flat = flat_of(xs)
        for tile in range(tiles):
            def at(number):
                return flat[pl.ds(tile * height + number, planes, stride=tiles * height), :]

            end = encode_end(*[at(height - 4 + number) for number in range(4)])
            begin = encode_start(*[at(number) for number in range(3)])
            for k in range(2):
                xs_flat[pl.ds(k * tiles + tile, planes, stride=8), :] = end[k]
                xs_flat[pl.ds(planes * 8 + k * tiles + tile, planes, stride=8), :] = begin[k]
        for side in SIDES:
            send("x", xs.at[side], r["xr"].at[side], gx=way[side])

        for side in SIDES:
            end = encode_end(*[xs[side, planes - 4 + number] for number in range(4)])
            begin = encode_start(*[xs[side, number] for number in range(3)])
            for k in range(2):
                es[side, 0, k] = end[k]
                es[side, 1, k] = begin[k]
        for sx in SIDES:
            for sz in SIDES:
                send("e", es.at[sx, sz], r["er"].at[sx, sz], gx=way[sx], gz=way[sz])
                for sy in SIDES:
                    send("c", es.at[sx, sz], r["cr"].at[sx, sz, sy], gx=way[sx], gz=way[sz], gy=way[sy])

        lane = lax.broadcasted_iota(jnp.int32, (height, LANES), 1)

        def pack(plane, carried):
            to_right, to_left, x_right, x_left = carried
            tail_by = lax.rem(plane * window + window, LANES)
            head_by = plane * window
            mine = lane >> shift == plane
            to_right = jnp.where(mine, pltpu.roll(body[plane, tiles - 1], tail_by, 1), to_right)
            to_left = jnp.where(mine, pltpu.roll(body[plane, 0], head_by, 1), to_left)
            mine = lane8 >> shift == plane
            x_right = tuple(jnp.where(mine, pltpu.roll(xs[sx, plane], tail_by, 1), x_right[sx]) for sx in SIDES)
            x_left = tuple(jnp.where(mine, pltpu.roll(xs[sx, plane], head_by, 1), x_left[sx]) for sx in SIDES)
            return to_right, to_left, x_right, x_left

        none = jnp.zeros((height, LANES), f32)
        to_right, to_left, x_right, x_left = loop(
            planes, 4, pack, (none, none, (none8, none8), (none8, none8))
        )
        r["ys"][0], r["ys"][1] = to_right, to_left
        for sx in SIDES:
            r["xys"][0, sx], r["xys"][1, sx] = x_right[sx], x_left[sx]
        groups = height // 8
        for sz in SIDES:
            tail = head = none8
            for k in range(2):
                for group in range(groups):
                    slot = k * groups + group
                    mine = lane8 >> shift == slot
                    part = pl.ds(group * 8, 8)
                    by = (slot * window + window) % LANES
                    tail = jnp.where(mine, pltpu.roll(zs[sz, k, tiles - 1, part, :], by, 1), tail)
                    head = jnp.where(mine, pltpu.roll(zs[sz, k, 0, part, :], slot * window, 1), head)
            r["zys"][0, sz], r["zys"][1, sz] = tail, head
        for sy in SIDES:
            send("y", r["ys"].at[sy], r["yr"].at[sy], gy=way[sy])
            for s in SIDES:
                send("xy", r["xys"].at[sy, s], r["xyr"].at[sy, s], gy=way[sy], gx=way[s])
                send("zy", r["zys"].at[sy, s], r["zyr"].at[sy, s], gy=way[sy], gz=way[s])
        if level == 0:
            for side in SIDES:
                send("z", r["zl"].at[side], r["zr"].at[side], gz=way[side])

    def own_x(level):
        planes, tiles, height, _ = extent(level)
        flat = flat_of(bodies[level])

        def along_x(plane, _):
            for tile in range(tiles):
                lift_rows(flat, (plane * tiles + tile) * height, height)
            return 0

        loop(planes, 2 if level == 0 else 4, along_x)

    def own_z(level, parity=None):
        planes, tiles, height, _ = extent(level)
        flat = flat_of(bodies[level])
        every = 1 if parity is None else 2
        groups = height // (8 * every)

        def along_z(block, _):
            tile, group = block // groups, block % groups
            first = tile * height + group * 8 * every
            if parity is None:
                first = pl.multiple_of(first, 8)
                where = [pl.ds(first + plane * tiles * height, 8) for plane in range(planes)]
            else:
                where = [pl.ds(first + parity + plane * tiles * height, 8, stride=2) for plane in range(planes)]
            lifted = lift_list([flat[at, :] for at in where])
            for at, values in zip(where, lifted):
                flat[at, :] = values
            return 0

        loop(tiles * groups, 1 if level == 0 else 2, along_z)

    def own_y(level, start=0, stop=None, with_halos=False):
        planes, tiles, height, _ = extent(level)
        body = bodies[level]
        chunk = min(planes, 512 // height)

        def halos(plane):
            yp = held[level]["yp"]
            window = 4 << level
            left = pltpu.roll(yp[0, 0] + yp[1, 0], lax.rem(2 * LANES - window - plane * window, LANES), 1)
            right = pltpu.roll(yp[0, 1] + yp[1, 1], lax.rem(LANES - plane * window, LANES), 1)
            return jnp.where(lax.broadcasted_iota(jnp.int32, (height, LANES), 1) >= LANES // 2, left, right)

        def along_y(number, _):
            where = pl.ds(number * chunk, chunk)
            values = [body[where, tile].reshape(chunk * height, LANES) for tile in range(tiles)]
            if with_halos:
                ext = jnp.concatenate([halos(number * chunk + inner) for inner in range(chunk)], axis=0)
            else:
                ext = jnp.zeros((chunk * height, LANES), f32)
            lifted = lift_lanes(values, ext, y_weights[level])
            for tile in range(tiles):
                body[where, tile] = lifted[tile].reshape(chunk, height, LANES)
            return 0

        lax.fori_loop(start, planes // chunk if stop is None else stop, along_y, 0)

    def prepare_y(level):
        height = extent(level)[2]
        r = held[level]
        for sy in SIDES:
            lift_rows(r["yr"].at[sy], 0, height)
            top, low = parts_of(r["yr"][sy])
            stacked = jnp.concatenate([top, low, top], axis=1)
            values = jnp.dot(stacked, z_weights[level][...], preferred_element_type=f32)
            top = values.astype(bf16).astype(f32)
            r["yp"][0, sy] = top
            r["yp"][1, sy] = values - top

    def spread_y(level, planes, pick):
        height = extent(level)[2]
        shift = 2 + level
        yp = held[level]["yp"]
        parts = [[pick(yp.at[part, sy]) for sy in SIDES] for part in range(2)]
        lane = lax.broadcasted_iota(jnp.int32, parts[0][0].shape, 1)
        stacks = []
        for plane in planes:
            mine = lane >> shift == plane
            top, low = [[jnp.where(mine, values, 0.0).astype(bf16) for values in part] for part in parts]
            stacks.append(jnp.concatenate(top + low + top, axis=1))
        return jnp.dot(jnp.concatenate(stacks, axis=0), far_weights[level][...], preferred_element_type=f32)

    def prepare_x(level):
        planes, tiles, height, window = extent(level)
        r = held[level]
        xr, xe, xl = r["xr"], r["xe"], r["xl"]

        def aligned(values):
            return pltpu.roll(values, 9 - tiles, 0) if tiles > 1 else values

        lefts = [aligned(r["xyr"][0, sx]) for sx in SIDES]
        rights = [r["xyr"][1, sx] for sx in SIDES]

        def unpack(plane, _):
            left_by = lax.rem(2 * LANES - window - plane * window, LANES)
            right_by = lax.rem(LANES - plane * window, LANES)
            for sx in SIDES:
                xe[sx, plane] = jnp.where(
                    last_half, pltpu.roll(lefts[sx], left_by, 1), pltpu.roll(rights[sx], right_by, 1)
                )
            return 0

        loop(planes, 8, unpack)
        for sx in SIDES:
            halo = [r["er"][sx, sz, k] for sz in SIDES for k in range(2)]
            lifted = lift_list([xr[sx, plane] for plane in range(planes)], halo)
            for plane in range(planes):
                xr[sx, plane] = lifted[plane]
            halo = [
                jnp.where(last_half, aligned(r["cr"][sx, sz, 0, k]), r["cr"][sx, sz, 1, k])
                for sz in SIDES
                for k in range(2)
            ]
            lifted = lift_list([xe[sx, plane] for plane in range(planes)], halo)
            for plane in range(planes):
                xe[sx, plane] = lifted[plane]
        xr_flat, xe_flat = flat_of(xr), flat_of(xe)

        def strip(ref, start):
            return ref[pl.ds(start, 2 * planes, stride=8), :]

        values = [
            jnp.concatenate([strip(xr_flat, k * tiles + tile) for k in range(2)], axis=0) for tile in range(tiles)
        ]
        ext = jnp.concatenate([strip(xe_flat, k * tiles) for k in range(2)], axis=0)
        lifted = lift_lanes(values, ext, y_weights[level])
        for tile in range(tiles):
            xl[tile] = lifted[tile]

    def prepare_z(level):
        planes, tiles, height, window = extent(level)
        r = held[level]
        zr, ze = r["zr"], r["ze"]
        zr_flat, ze_flat = flat_of(zr), flat_of(ze)
        groups = height // 8
        wait_for(level, "zy")
        for sz in SIDES:
            for k in range(2):
                for group in range(groups):
                    slot = k * groups + group
                    left = pltpu.roll(r["zyr"][0, sz], (2 * LANES - window - slot * window) % LANES, 1)
                    right = pltpu.roll(r["zyr"][1, sz], (LANES - slot * window) % LANES, 1)
                    ze[sz, k, pl.ds(group * 8, 8), :] = jnp.where(last_half, left, right)
        if level == 0:
            for layer in range(4):
                lift_rows(ze_flat, layer * height, height)
            ext = ze[...].reshape(4 * height, LANES)
            first = lax.broadcasted_iota(jnp.int32, ext.shape, 1) < LANES // 2
            side_weights = y_weights[0][6 * LANES :]
            for block in range(2):
                top, low = parts_of(jnp.where(first, 0.0, ext) if block == 0 else jnp.where(first, ext, 0.0))
                stacked = jnp.concatenate([top, low, top], axis=1)
                added = jnp.dot(stacked, side_weights, preferred_element_type=f32)
                for tile in range(2):
                    part = added[:, tile * LANES : (tile + 1) * LANES]
                    r["zc"][:, :, 2 * block + tile] = part.reshape(2, 2, height, LANES)
            return
        wait_for(level, "z")

        def along_x(layer, _):
            for tile in range(tiles):
                lift_rows(zr_flat, (layer * tiles + tile) * height, height)
            lift_rows(ze_flat, layer * height, height)
            return 0

        loop(4, 4, along_x)
        values = [zr[:, :, tile].reshape(4 * height, LANES) for tile in range(tiles)]
        lifted = lift_lanes(values, ze[...].reshape(4 * height, LANES), y_weights[level])
        for tile in range(tiles):
            zr[:, :, tile] = lifted[tile].reshape(2, 2, height, LANES)

    def row_weights(table, layer, at):
        values = none8
        for number, weights in table.items():
            place = at(number)
            if place is not None and weights[layer] != 0.0:
                values = jnp.where(sub == place, weights[layer], values)
        return values

    def add_y(level):
        planes, tiles, height, _ = extent(level)
        body = bodies[level]
        chunk = min(planes, 512 // height)

        def add(number, _):
            where = pl.ds(number * chunk, chunk)
            added = spread_y(level, [number * chunk + inner for inner in range(chunk)], lambda ref: ref[...])
            body[where, 0] = body[where, 0] + added[:, :LANES].reshape(chunk, height, LANES)
            if tiles > 1:
                body[where, tiles - 1] = body[where, tiles - 1] + added[:, LANES:].reshape(chunk, height, LANES)
            return 0

        lax.fori_loop(0, planes // chunk, add, 0)

    def add_x_rows(body, planes, every, height, strips, at):
        tables = ((FROM_LEFT, 0), (FROM_RIGHT, height - 8))
        weigh = [[row_weights(table, layer, at) for layer in range(2)] for table, _ in tables]

        def add(number, _):
            for tile in range(body.shape[1]):
                strip = strips(tile)
                for side in SIDES:
                    part = pl.ds(tables[side][1], 8)
                    first = side * planes + number * every
                    added = weigh[side][0] * strip[pl.ds(first, 1), :]
                    added = added + weigh[side][1] * strip[pl.ds(2 * planes + first, 1), :]
                    body[number, tile, part, :] = body[number, tile, part, :] + added
            return 0

        loop(planes // every, 4, add)

    def add_x(level):
        planes, _, height, _ = extent(level)
        xl = held[level]["xl"]
        add_x_rows(bodies[level], planes, 1, height, lambda tile: xl.at[tile], lambda number: number % 8)

    def add_z(level):
        planes, tiles, _, _ = extent(level)
        body, zr = bodies[level], held[level]["zr"]
        if level == 0:
            wait_for(0, "z")
            for side in SIDES:
                for k in range(2):
                    for tile in range(tiles):
                        zr[side, k, tile] = zr[side, k, tile] + held[0]["zc"][side, k, tile]
        for side, table in ((0, FROM_LEFT), (1, FROM_RIGHT)):
            for number, (one, two) in table.items():
                plane = number % planes
                for tile in range(tiles):
                    added = one * zr[side, 0, tile]
                    if two != 0.0:
                        added = added + two * zr[side, 1, tile]
                    body[plane, tile] = body[plane, tile] + added

    start(0)
    own_x(0)
    own_z(0, 0)
    planes, tiles, height, _ = extent(0)
    half, deep = height // 2, planes // 2
    inner, inner_tiles = bodies[1], tiles // 2
    flat = flat_of(bodies[0])
    tops = list(range(0, planes, 2))

    def low_rows(ref_flat, start_of):
        return ref_flat[pl.ds(start_of, half, stride=2), :]

    values = [
        jnp.concatenate([low_rows(flat, (plane * tiles + tile) * height) for plane in tops], axis=0)
        for tile in range(tiles)
    ]
    lifted = lift_lanes(values, jnp.zeros((deep * half, LANES), f32), y_weights[0])
    for tile, packed in enumerate(pack_tiles(0, lifted)):
        inner[:, tile] = packed.reshape(deep, half, LANES)

    wait_for(0, "y")
    prepare_y(0)
    added = spread_y(0, tops, lambda ref: ref[pl.ds(0, half, stride=2), :])
    keep = (lax.broadcasted_iota(jnp.int32, (deep * half, LANES), 1) & 1) == 0
    first = jnp.where(keep, added[:, :LANES], 0.0)
    last = jnp.where(keep, 0.0, pltpu.roll(added[:, LANES:], 1, 1))
    inner[:, 0] = inner[:, 0] + first.reshape(deep, half, LANES)
    inner[:, inner_tiles - 1] = inner[:, inner_tiles - 1] + last.reshape(deep, half, LANES)

    wait_for(0, "x")
    prepare_x(0)
    xl, xp = held[0]["xl"], take()
    for tile, packed in enumerate(pack_tiles(0, [xl[tile] for tile in range(tiles)])):
        xp[tile] = packed

    def even_row(number):
        return (number % 16) // 2 % 8 if number % 2 == 0 else None

    add_x_rows(inner, planes, 2, half, lambda tile: xp.at[tile], even_row)
    prepare_z(0)
    zc_flat = flat_of(held[0]["zc"])
    packed_layers = [pack_tiles(0, low_tiles(zc_flat, layer)) for layer in range(4)]
    wait_for(0, "zlow")
    for side, table in ((0, FROM_LEFT), (1, FROM_RIGHT)):
        packed = [
            [held[0]["zlowr"][side, k, tile] + packed_layers[2 * side + k][tile] for tile in range(inner_tiles)]
            for k in range(2)
        ]
        for number, (one, two) in table.items():
            if number % 2 == 0:
                plane = (number % planes) // 2
                for tile in range(inner_tiles):
                    added = one * packed[0][tile]
                    if two != 0.0:
                        added = added + two * packed[1][tile]
                    inner[plane, tile] = inner[plane, tile] + added

    start(1)
    make_weights(1)
    own_x(1)
    own_z(1)
    own_y(1)
    own_z(0, 1)
    own_y(0, 0, 2, True)
    wait_for(1, "y")
    prepare_y(1)
    add_y(1)
    wait_for(1, "x")
    prepare_x(1)
    add_x(1)
    prepare_z(1)
    add_z(1)
    planes, tiles, height, _ = extent(1)
    half = height // 2
    flat = flat_of(bodies[1])

    def pick(plane, _):
        values = [flat[pl.ds((2 * plane * tiles + tile) * height, half, stride=2), :] for tile in range(tiles)]
        for tile, packed in enumerate(pack_tiles(1, values)):
            bodies[2][plane, tile] = packed
        return 0

    loop(planes // 2, 4, pick)

    start(2)
    make_weights(2)
    own_x(2)
    own_z(2)
    own_y(2)
    own_y(0, 2, None, True)
    add_x(0)
    add_z(0)
    wait_for(2, "y")
    prepare_y(2)
    add_y(2)
    wait_for(2, "x")
    prepare_x(2)
    add_x(2)
    prepare_z(2)
    add_z(2)

    planes, tiles, height, _ = extent(1)
    half = height // 2

    def place(plane, _):
        where = [pl.ds((2 * plane * tiles + tile) * height, half, stride=2) for tile in range(tiles)]
        inner = [bodies[2][plane, tile] for tile in range(tiles // 2)]
        for at, values in zip(where, unpack_tiles(1, [flat[at, :] for at in where], inner)):
            flat[at, :] = values
        return 0

    loop(planes // 2, 4, place)

    for level in range(LEVELS):
        wait_rows(send_sem.at[level], sent[level])


def write_out(held_ref, inner_ref, out_ref, merged, sem):
    depth, tiles, rows, _ = held_ref.shape
    planes, half = depth // 2, rows // 2
    pairs = held_ref.reshape(planes, 2, tiles, rows, LANES)
    target = out_ref.reshape(planes, 2, rows, tiles * LANES)
    parts = sem.shape[0] - 1
    size = planes // parts

    def copy(source, odd, tile, slot, where):
        return pltpu.make_async_copy(
            source, target.at[where, odd, :, pl.ds(tile * LANES, LANES)], sem.at[slot, tile]
        )

    copies = [copy(pairs.at[:, 1, tile], 1, tile, parts, pl.ds(0, planes)) for tile in range(tiles)]
    for one in copies:
        one.start()
    held_flat = held_ref.reshape(depth * tiles * rows, LANES)
    merged_flat = merged.reshape(planes * tiles * rows, LANES)

    def place(plane, _):
        source = [2 * plane * tiles * rows + tile * rows for tile in range(tiles)]
        target = [plane * tiles * rows + tile * rows for tile in range(tiles)]
        low = [held_flat[pl.ds(start, half, stride=2), :] for start in source]
        inner = [inner_ref[plane, tile] for tile in range(tiles // 2)]
        for tile, values in enumerate(unpack_tiles(0, low, inner)):
            merged_flat[pl.ds(target[tile], half, stride=2), :] = values
            odd = held_flat[pl.ds(source[tile] + 1, half, stride=2), :]
            merged_flat[pl.ds(target[tile] + 1, half, stride=2), :] = odd
        return 0

    for part in range(parts):
        loop(size, 4, lambda number, _: place(part * size + number, _))
        for tile in range(tiles):
            where = pl.ds(part * size, size)
            copies.append(copy(merged.at[where, tile], 0, tile, part, where))
            copies[-1].start()
    for one in copies:
        one.wait()


def local(field):
    depth, rows, lanes = field.shape
    vmem = pltpu.VMEM
    sizes = [(depth >> level, TILES >> level, rows >> level) for level in range(LEVELS)]
    scratch = [vmem((planes, tiles, height, LANES), f32) for planes, tiles, height in sizes[2:]]
    scratch += [
        pltpu.SemaphoreType.DMA((3, TILES)),
        pltpu.SemaphoreType.DMA((LEVELS,)),
        pltpu.SemaphoreType.DMA((LEVELS, 5)),
    ]
    widths = [min(tiles, 2) * LANES for _, tiles, _ in sizes]
    scratch += [vmem((3 * (width + LANES), width), bf16) for width in widths]
    scratch += [vmem((6 * LANES, width), bf16) for width in widths]
    scratch += [vmem((3 * LANES, LANES), bf16) for _ in sizes]
    for planes, tiles, height in sizes:
        shapes = [(2, 2, tiles, height)] * 2 + [(2, 2, height)]
        shapes += [(2, planes, 8)] * 3 + [(tiles, 4 * planes)]
        shapes += [(2, 2, 2, 8)] * 2 + [(2, height)] * 2 + [(2, 2, height)]
        shapes += [(2, 2, 8)] * 4 + [(2, 2, 2, 2, 8)]
        scratch += [vmem((*shape, LANES), f32) for shape in shapes]
    scratch += [vmem((2, 2, TILES, rows, LANES), f32)] * 2 + [vmem((2, 2, TILES // 2, rows // 2, LANES), f32)] * 2
    scratch += [vmem((TILES // 2, 4 * depth, LANES), f32)]
    lifted = pl.pallas_call(
        functools.partial(kernel, field.shape),
        out_shape=[jax.ShapeDtypeStruct((size[0], size[1], size[2], LANES), f32) for size in sizes[:2]],
        in_specs=[pl.BlockSpec(memory_space=pltpu.HBM)],
        out_specs=[pl.BlockSpec(memory_space=pltpu.VMEM)] * 2,
        scratch_shapes=scratch,
        compiler_params=pltpu.CompilerParams(
            collective_id=0, has_side_effects=True, vmem_limit_bytes=48 * 2**20
        ),
        name="lift",
    )(field)
    return pl.pallas_call(
        write_out,
        out_shape=jax.ShapeDtypeStruct(field.shape, f32),
        in_specs=[pl.BlockSpec(memory_space=pltpu.VMEM)] * 2,
        out_specs=pl.BlockSpec(memory_space=pltpu.HBM),
        scratch_shapes=[
            vmem((depth // 2, TILES, rows, LANES), f32),
            pltpu.SemaphoreType.DMA((3, TILES)),
        ],
        compiler_params=pltpu.CompilerParams(vmem_limit_bytes=8 * 2**20),
        name="write_out",
    )(*lifted)


def solution(mesh):
    placed = (P("gz", "gx", "gy"),)
    return jax.shard_map(
        local, mesh=mesh, in_specs=placed, out_specs=P("gz", "gx", "gy"), check_vma=False
    )
```

```python
import functools

import jax
import jax.numpy as jnp
import numpy as np
from jax import lax
from jax.experimental import pallas as pl
from jax.experimental.pallas import tpu as pltpu
from jax.sharding import PartitionSpec as P

A = -1.586134342
B = -0.05298011854
G = 0.8829110762
E = 0.4435068522
Z = 1.149604398
MESH = pl.DeviceIdType.MESH
LANES = 128
TILES = 4
LEVELS = 3
SIDES = (0, 1)
f32, bf16 = jnp.float32, jnp.bfloat16


def filter_taps():
    u = np.eye(64)
    s, d = u[0::2].copy(), u[1::2].copy()
    d += A * (s + np.roll(s, -1, 0))
    s += B * (np.roll(d, 1, 0) + d)
    d += G * (s + np.roll(s, -1, 0))
    s += E * (np.roll(d, 1, 0) + d)
    low, high = s[16] * Z, d[16] / Z
    return [float(low[32 + o]) for o in range(5)], [float(high[33 + o]) for o in range(5)]


LOW, HIGH = filter_taps()

FROM_LEFT = {
    0: (Z * (B + E * (1 + 3 * G * B)), Z * E * G),
    1: (G * B / Z, 0.0),
    2: (Z * E * G * B, 0.0),
}
FROM_RIGHT = {
    -4: (Z * E * G * B * A, 0.0),
    -3: (G * B * A / Z, 0.0),
    -2: (Z * (B * A + E * (G * B * A + A * (1 + 2 * G * B))), Z * E * G),
    -1: (A * (1 + 2 * G * B) / Z, G / Z),
}


def cell_of(level, tile, lane):
    if level == 0:
        return tile * LANES + lane
    if level == 1:
        turn = lane & 1
        return ((tile + 2 * turn) * LANES + lane - turn) >> 1
    turn = lane & 3
    return (((turn >> 1) + 2 * (turn & 1)) * LANES + lane - turn) >> 2


def tap_weights(position, target):
    apart = jnp.abs(position - target)
    low = jnp.zeros(position.shape, f32)
    high = jnp.zeros(position.shape, f32)
    for o in range(5):
        low = jnp.where(apart == o, LOW[o], low)
        if o < 4:
            high = jnp.where(apart == o, HIGH[o], high)
    return jnp.where((target & 1) == 0, low, high)


def parts_of(values):
    top = values.astype(bf16)
    return top, (values - top.astype(f32)).astype(bf16)


def encode_end(s2, d2, s1, d1):
    return d1 + A * s1, s1 + B * (d2 + A * (s2 + s1))


def encode_start(s0, d0, s1):
    return s0, s0 + B * (d0 + A * (s0 + s1))


def lift_list(u, halo=None):
    s, d = list(u[0::2]), list(u[1::2])
    count = len(s)
    d_before = A * s[0]
    if halo is not None:
        d_before = d_before + halo[0]
    s_before = B * d_before
    if halo is not None:
        s_before = s_before + halo[1]
    for i in range(count - 1):
        d[i] = d[i] + A * (s[i] + s[i + 1])
    last = s[-1] if halo is None else s[-1] + halo[2]
    d[-1] = d[-1] + A * last
    s_after = B * d[-1]
    if halo is not None:
        s_after = s_after + halo[3]
    around = [d_before] + d
    s = [s[i] + B * (around[i] + around[i + 1]) for i in range(count)]
    d_before = d_before + G * (s_before + s[0])
    around = s + [s_after]
    d = [d[i] + G * (around[i] + around[i + 1]) for i in range(count)]
    around = [d_before] + d
    s = [s[i] + E * (around[i] + around[i + 1]) for i in range(count)]
    out = []
    for i in range(count):
        out += [s[i] * Z, d[i] * (1.0 / Z)]
    return out


def lift_rows(flat, start, height):
    half = height // 2
    pair = lax.broadcasted_iota(jnp.int32, (half, LANES), 0)
    even, odd = pl.ds(start, half, stride=2), pl.ds(start + 1, half, stride=2)
    s, d = flat[even, :], flat[odd, :]

    def after(values, last):
        return jnp.where(pair == half - 1, last, pltpu.roll(values, half - 1, 0))

    def before(values, first):
        return jnp.where(pair == 0, first, pltpu.roll(values, 1, 0))

    d_before = A * s[:1]
    d = d + A * (s + after(s, 0.0))
    s_after = B * d[half - 1 :]
    s_before = B * d_before
    s = s + B * (before(d, d_before) + d)
    d_before = d_before + G * (s_before + s[:1])
    d = d + G * (s + after(s, s_after))
    s = s + E * (before(d, d_before) + d)
    flat[even, :] = s * Z
    flat[odd, :] = d * (1.0 / Z)


def pack_tiles(level, tiles):
    lane = lax.broadcasted_iota(jnp.int32, tiles[0].shape, 1)
    step = 2**level
    keep = lane & (2 * step - 1) < step
    half = len(tiles) // 2
    return [jnp.where(keep, tiles[i], pltpu.roll(tiles[i + half], step, 1)) for i in range(half)]


def unpack_tiles(level, tiles, inner):
    lane = lax.broadcasted_iota(jnp.int32, tiles[0].shape, 1)
    step = 2**level
    keep = lane & (2 * step - 1) < step
    inner = list(inner) + [pltpu.roll(tile, LANES - step, 1) for tile in inner]
    return [jnp.where(keep, new, old) for new, old in zip(inner, tiles)]


def lift_lanes(tiles, ext, weights):
    first = lax.broadcasted_iota(jnp.int32, tiles[0].shape, 1) < LANES // 2
    blocks = [(tiles, ext)]
    if len(tiles) == 4:
        blocks = [(tiles[:2], jnp.where(first, tiles[2], ext)), (tiles[2:], jnp.where(first, ext, tiles[1]))]
    out = []
    for main, beside in blocks:
        main_top, main_low = parts_of(jnp.concatenate(main, axis=1))
        side_top, side_low = parts_of(beside)
        stacked = jnp.concatenate([main_top, main_low, main_top, side_top, side_low, side_top], axis=1)
        result = jnp.dot(stacked, weights[...], preferred_element_type=f32)
        out += [result[:, i * LANES : (i + 1) * LANES] for i in range(len(main))]
    return out


def loop(count, unroll, body, carry=0):
    unroll = min(unroll, count)

    def turns(number, carried):
        for inner in range(unroll):
            carried = body(number * unroll + inner, carried)
        return carried

    return lax.fori_loop(0, count // unroll, turns, carry)


NAMES = ("zs", "zr", "ze", "xs", "xr", "xe", "xl", "es", "er", "ys", "yr", "yp", "zys", "zyr", "xys", "xyr", "cr")
GROUPS = {"y": 0, "x": 1, "e": 1, "c": 1, "xy": 1, "zy": 2, "z": 3, "zlow": 4}
FIRST_NAMES = ("zl", "zc", "zlow", "zlowr")


def kernel(shape, field_ref, out_ref, inner_ref, *scratch):
    depth, rows, _ = shape
    refs = list(scratch)
    take = lambda: refs.pop(0)
    bodies = [out_ref, inner_ref, take()]
    load_sem, send_sem, recv_sem = take(), take(), take()
    y_weights, far_weights, z_weights = [[take() for _ in range(LEVELS)] for _ in range(3)]
    held = [{name: take() for name in NAMES} for _ in range(LEVELS)]
    held[0].update({name: take() for name in FIRST_NAMES})

    here = {name: lax.axis_index(name) for name in ("gx", "gy", "gz")}
    count = {name: lax.axis_size(name) for name in ("gx", "gy", "gz")}

    near = {
        name: {-1: lax.rem(at + count[name] - 1, count[name]), 0: at, 1: lax.rem(at + 1, count[name])}
        for name, at in here.items()
    }

    def beside(**by):
        return {name: near[name][way] for name, way in by.items()}

    loads = [
        [
            pltpu.make_async_copy(
                field_ref.at[pl.ds(first, size), :, pl.ds(tile * LANES, LANES)],
                out_ref.at[pl.ds(first, size), tile],
                load_sem.at[number, tile],
            )
            for tile in range(TILES)
        ]
        for number, (first, size) in enumerate(((0, 4), (depth - 4, 4), (4, depth - 8)))
    ]
    for part in loads[:2]:
        for load in part:
            load.start()
    barrier = pltpu.get_barrier_semaphore()
    for x in (-1, 0, 1):
        for y in (-1, 0, 1):
            for z in (-1, 0, 1):
                if (x, y, z) != (0, 0, 0):
                    pl.semaphore_signal(barrier, inc=1, device_id=beside(gx=x, gy=y, gz=z), device_id_type=MESH)
    for load in loads[2]:
        load.start()

    def fill(ref, blocks):
        start = 0
        for values in blocks:
            top, low = parts_of(values)
            size = values.shape[0]
            for part in (top, top, low):
                ref[start : start + size] = part
                start += size

    def make_weights(level):
        window = 4 << level
        tiles = TILES >> level
        cells = (TILES * LANES) >> level
        width = min(tiles, 2) * LANES
        row = lax.broadcasted_iota(jnp.int32, (2 * LANES, width), 0)
        col = lax.broadcasted_iota(jnp.int32, (2 * LANES, width), 1)
        target = cell_of(level, col >> 7, col & 127)
        main = row[:width]
        side = row[:LANES]
        after, before = (2 * LANES, -LANES) if level == 0 else (cells, -cells)
        right = cell_of(level, 0, side) + after
        left = cell_of(level, 0 if level == 0 else tiles - 1, side) + before
        position = jnp.where(side < LANES // 2, right, left)
        fill(
            y_weights[level],
            [
                tap_weights(cell_of(level, main >> 7, main & 127), target[:width]),
                tap_weights(position, target[:LANES]),
            ],
        )
        inside = row & (window - 1)
        left = cell_of(level, tiles - 1, LANES - window + inside) - cells
        right = cell_of(level, 0, inside) + cells
        position = jnp.where(row < LANES, left, right)
        last = cell_of(level, tiles - 1, col & 127)
        target = jnp.where(col < LANES, cell_of(level, 0, col & 127), last)
        fill(far_weights[level], [tap_weights(position, target)])
        shift = 2 + level
        row, col = row[:LANES, :LANES], col[:LANES, :LANES]
        taps = tap_weights(row >> shift, col >> shift)
        fill(z_weights[level], [jnp.where((row & (window - 1)) == (col & (window - 1)), taps, 0.0)])

    make_weights(0)
    for part in loads[:2]:
        for load in part:
            load.wait()

    sent = [0] * LEVELS
    arriving = [[0] * 5 for _ in range(LEVELS)]
    way = (1, -1)
    sub = lax.broadcasted_iota(jnp.int32, (8, LANES), 0)
    lane8 = lax.broadcasted_iota(jnp.int32, (8, LANES), 1)
    last_half = lane8 >= LANES // 2
    none8 = jnp.zeros((8, LANES), f32)

    def extent(level):
        return depth >> level, TILES >> level, rows >> level, 4 << level

    def flat_of(ref):
        size = 1
        for extent_of_dim in ref.shape[:-1]:
            size *= extent_of_dim
        return ref.reshape(size, LANES)

    def wait_rows(sem, count):
        held_rows = flat_of(out_ref).at[pl.ds(0, count)]
        pltpu.make_async_copy(held_rows, held_rows, sem).wait()

    def wait_for(level, key):
        wait_rows(recv_sem.at[level, GROUPS[key]], arriving[level][GROUPS[key]])

    def lift_layers(layers, low):
        _, tiles, height, _ = extent(0)
        layers_flat = flat_of(layers)

        def along_x(layer, _):
            for tile in range(tiles):
                lift_rows(layers_flat, (layer * tiles + tile) * height, height)
            return 0

        loop(4, 4, along_x)
        values = [layers[:, :, tile].reshape(4 * height, LANES) for tile in range(tiles)]
        lifted = lift_lanes(values, jnp.zeros((4 * height, LANES), f32), y_weights[0])
        for tile in range(tiles):
            layers[:, :, tile] = lifted[tile].reshape(2, 2, height, LANES)
        for layer in range(4):
            for tile, packed in enumerate(pack_tiles(0, low_tiles(layers_flat, layer))):
                low[layer // 2, layer % 2, tile] = packed

    def low_tiles(layers_flat, layer):
        _, tiles, height, _ = extent(0)
        return [
            layers_flat[pl.ds((layer * tiles + tile) * height, height // 2, stride=2), :] for tile in range(tiles)
        ]

    def start(level):
        planes, tiles, height, window = extent(level)
        body, flat, r = bodies[level], flat_of(bodies[level]), held[level]
        shift = 2 + level

        def send(key, source, target, **by):
            copy = pltpu.make_async_remote_copy(
                src_ref=source,
                dst_ref=target,
                send_sem=send_sem.at[level],
                recv_sem=recv_sem.at[level, GROUPS[key]],
                device_id=beside(**by),
                device_id_type=MESH,
            )
            if level == 0 and not sent[0]:
                pl.semaphore_wait(barrier, 26)
            copy.start()
            size = 1
            for extent_of_dim in source.shape[:-1]:
                size *= extent_of_dim
            sent[level] += size
            arriving[level][GROUPS[key]] += size

        zs, xs, es = r["zs"], r["xs"], r["es"]
        for tile in range(tiles):
            end = encode_end(*[body[planes - 4 + number, tile] for number in range(4)])
            begin = encode_start(*[body[number, tile] for number in range(3)])
            for k in range(2):
                zs[0, k, tile] = end[k]
                zs[1, k, tile] = begin[k]
                if level == 0:
                    r["zl"][0, k, tile] = end[k]
                    r["zl"][1, k, tile] = begin[k]
        if level == 0:
            lift_layers(r["zl"], r["zlow"])
            for side in SIDES:
                send("zlow", r["zlow"].at[side], r["zlowr"].at[side], gz=way[side])
            for load in loads[2]:
                load.wait()
        else:
            for side in SIDES:
                send("z", zs.at[side], r["zr"].at[side], gz=way[side])

        xs_flat = flat_of(xs)
        for tile in range(tiles):
            def at(number):
                return flat[pl.ds(tile * height + number, planes, stride=tiles * height), :]

            end = encode_end(*[at(height - 4 + number) for number in range(4)])
            begin = encode_start(*[at(number) for number in range(3)])
            for k in range(2):
                xs_flat[pl.ds(k * tiles + tile, planes, stride=8), :] = end[k]
                xs_flat[pl.ds(planes * 8 + k * tiles + tile, planes, stride=8), :] = begin[k]
        for side in SIDES:
            send("x", xs.at[side], r["xr"].at[side], gx=way[side])

        for side in SIDES:
            end = encode_end(*[xs[side, planes - 4 + number] for number in range(4)])
            begin = encode_start(*[xs[side, number] for number in range(3)])
            for k in range(2):
                es[side, 0, k] = end[k]
                es[side, 1, k] = begin[k]
        for sx in SIDES:
            for sz in SIDES:
                send("e", es.at[sx, sz], r["er"].at[sx, sz], gx=way[sx], gz=way[sz])
                for sy in SIDES:
                    send("c", es.at[sx, sz], r["cr"].at[sx, sz, sy], gx=way[sx], gz=way[sz], gy=way[sy])

        lane = lax.broadcasted_iota(jnp.int32, (height, LANES), 1)

        def pack(plane, carried):
            to_right, to_left, x_right, x_left = carried
            tail_by = lax.rem(plane * window + window, LANES)
            head_by = plane * window
            mine = lane >> shift == plane
            to_right = jnp.where(mine, pltpu.roll(body[plane, tiles - 1], tail_by, 1), to_right)
            to_left = jnp.where(mine, pltpu.roll(body[plane, 0], head_by, 1), to_left)
            mine = lane8 >> shift == plane
            x_right = tuple(jnp.where(mine, pltpu.roll(xs[sx, plane], tail_by, 1), x_right[sx]) for sx in SIDES)
            x_left = tuple(jnp.where(mine, pltpu.roll(xs[sx, plane], head_by, 1), x_left[sx]) for sx in SIDES)
            return to_right, to_left, x_right, x_left

        none = jnp.zeros((height, LANES), f32)
        to_right, to_left, x_right, x_left = loop(
            planes, 4, pack, (none, none, (none8, none8), (none8, none8))
        )
        r["ys"][0], r["ys"][1] = to_right, to_left
        for sx in SIDES:
            r["xys"][0, sx], r["xys"][1, sx] = x_right[sx], x_left[sx]
        groups = height // 8
        for sz in SIDES:
            tail = head = none8
            for k in range(2):
                for group in range(groups):
                    slot = k * groups + group
                    mine = lane8 >> shift == slot
                    part = pl.ds(group * 8, 8)
                    by = (slot * window + window) % LANES
                    tail = jnp.where(mine, pltpu.roll(zs[sz, k, tiles - 1, part, :], by, 1), tail)
                    head = jnp.where(mine, pltpu.roll(zs[sz, k, 0, part, :], slot * window, 1), head)
            r["zys"][0, sz], r["zys"][1, sz] = tail, head
        for sy in SIDES:
            send("y", r["ys"].at[sy], r["yr"].at[sy], gy=way[sy])
            for s in SIDES:
                send("xy", r["xys"].at[sy, s], r["xyr"].at[sy, s], gy=way[sy], gx=way[s])
                send("zy", r["zys"].at[sy, s], r["zyr"].at[sy, s], gy=way[sy], gz=way[s])
        if level == 0:
            for side in SIDES:
                send("z", r["zl"].at[side], r["zr"].at[side], gz=way[side])

    def own_x(level):
        planes, tiles, height, _ = extent(level)
        flat = flat_of(bodies[level])

        def along_x(plane, _):
            for tile in range(tiles):
                lift_rows(flat, (plane * tiles + tile) * height, height)
            return 0

        loop(planes, 4, along_x)

    def own_z(level, parity=None):
        planes, tiles, height, _ = extent(level)
        flat = flat_of(bodies[level])
        every = 1 if parity is None else 2
        groups = height // (8 * every)

        def along_z(block, _):
            tile, group = block // groups, block % groups
            first = tile * height + group * 8 * every
            if parity is None:
                first = pl.multiple_of(first, 8)
                where = [pl.ds(first + plane * tiles * height, 8) for plane in range(planes)]
            else:
                where = [pl.ds(first + parity + plane * tiles * height, 8, stride=2) for plane in range(planes)]
            lifted = lift_list([flat[at, :] for at in where])
            for at, values in zip(where, lifted):
                flat[at, :] = values
            return 0

        loop(tiles * groups, 1 if level == 0 else 2, along_z)

    def own_y(level, start=0, stop=None, with_halos=False):
        planes, tiles, height, _ = extent(level)
        body = bodies[level]
        chunk = min(planes, 512 // height)

        def halos(plane):
            yp = held[level]["yp"]
            window = 4 << level
            left = pltpu.roll(yp[0, 0] + yp[1, 0], lax.rem(2 * LANES - window - plane * window, LANES), 1)
            right = pltpu.roll(yp[0, 1] + yp[1, 1], lax.rem(LANES - plane * window, LANES), 1)
            return jnp.where(lax.broadcasted_iota(jnp.int32, (height, LANES), 1) >= LANES // 2, left, right)

        def along_y(number, _):
            where = pl.ds(number * chunk, chunk)
            values = [body[where, tile].reshape(chunk * height, LANES) for tile in range(tiles)]
            if with_halos:
                ext = jnp.concatenate([halos(number * chunk + inner) for inner in range(chunk)], axis=0)
            else:
                ext = jnp.zeros((chunk * height, LANES), f32)
            lifted = lift_lanes(values, ext, y_weights[level])
            for tile in range(tiles):
                body[where, tile] = lifted[tile].reshape(chunk, height, LANES)
            return 0

        lax.fori_loop(start, planes // chunk if stop is None else stop, along_y, 0)

    def prepare_y(level):
        height = extent(level)[2]
        r = held[level]
        for sy in SIDES:
            lift_rows(r["yr"].at[sy], 0, height)
            top, low = parts_of(r["yr"][sy])
            stacked = jnp.concatenate([top, low, top], axis=1)
            values = jnp.dot(stacked, z_weights[level][...], preferred_element_type=f32)
            top = values.astype(bf16).astype(f32)
            r["yp"][0, sy] = top
            r["yp"][1, sy] = values - top

    def spread_y(level, planes, pick):
        height = extent(level)[2]
        shift = 2 + level
        yp = held[level]["yp"]
        parts = [[pick(yp.at[part, sy]) for sy in SIDES] for part in range(2)]
        lane = lax.broadcasted_iota(jnp.int32, parts[0][0].shape, 1)
        stacks = []
        for plane in planes:
            mine = lane >> shift == plane
            top, low = [[jnp.where(mine, values, 0.0).astype(bf16) for values in part] for part in parts]
            stacks.append(jnp.concatenate(top + low + top, axis=1))
        return jnp.dot(jnp.concatenate(stacks, axis=0), far_weights[level][...], preferred_element_type=f32)

    def prepare_x(level):
        planes, tiles, height, window = extent(level)
        r = held[level]
        xr, xe, xl = r["xr"], r["xe"], r["xl"]

        def aligned(values):
            return pltpu.roll(values, 9 - tiles, 0) if tiles > 1 else values

        lefts = [aligned(r["xyr"][0, sx]) for sx in SIDES]
        rights = [r["xyr"][1, sx] for sx in SIDES]

        def unpack(plane, _):
            left_by = lax.rem(2 * LANES - window - plane * window, LANES)
            right_by = lax.rem(LANES - plane * window, LANES)
            for sx in SIDES:
                xe[sx, plane] = jnp.where(
                    last_half, pltpu.roll(lefts[sx], left_by, 1), pltpu.roll(rights[sx], right_by, 1)
                )
            return 0

        loop(planes, 8, unpack)
        for sx in SIDES:
            halo = [r["er"][sx, sz, k] for sz in SIDES for k in range(2)]
            lifted = lift_list([xr[sx, plane] for plane in range(planes)], halo)
            for plane in range(planes):
                xr[sx, plane] = lifted[plane]
            halo = [
                jnp.where(last_half, aligned(r["cr"][sx, sz, 0, k]), r["cr"][sx, sz, 1, k])
                for sz in SIDES
                for k in range(2)
            ]
            lifted = lift_list([xe[sx, plane] for plane in range(planes)], halo)
            for plane in range(planes):
                xe[sx, plane] = lifted[plane]
        xr_flat, xe_flat = flat_of(xr), flat_of(xe)

        def strip(ref, start):
            return ref[pl.ds(start, 2 * planes, stride=8), :]

        values = [
            jnp.concatenate([strip(xr_flat, k * tiles + tile) for k in range(2)], axis=0) for tile in range(tiles)
        ]
        ext = jnp.concatenate([strip(xe_flat, k * tiles) for k in range(2)], axis=0)
        lifted = lift_lanes(values, ext, y_weights[level])
        for tile in range(tiles):
            xl[tile] = lifted[tile]

    def prepare_z(level):
        planes, tiles, height, window = extent(level)
        r = held[level]
        zr, ze = r["zr"], r["ze"]
        zr_flat, ze_flat = flat_of(zr), flat_of(ze)
        groups = height // 8
        wait_for(level, "zy")
        for sz in SIDES:
            for k in range(2):
                for group in range(groups):
                    slot = k * groups + group
                    left = pltpu.roll(r["zyr"][0, sz], (2 * LANES - window - slot * window) % LANES, 1)
                    right = pltpu.roll(r["zyr"][1, sz], (LANES - slot * window) % LANES, 1)
                    ze[sz, k, pl.ds(group * 8, 8), :] = jnp.where(last_half, left, right)
        if level == 0:
            for layer in range(4):
                lift_rows(ze_flat, layer * height, height)
            ext = ze[...].reshape(4 * height, LANES)
            first = lax.broadcasted_iota(jnp.int32, ext.shape, 1) < LANES // 2
            side_weights = y_weights[0][6 * LANES :]
            for block in range(2):
                top, low = parts_of(jnp.where(first, 0.0, ext) if block == 0 else jnp.where(first, ext, 0.0))
                stacked = jnp.concatenate([top, low, top], axis=1)
                added = jnp.dot(stacked, side_weights, preferred_element_type=f32)
                for tile in range(2):
                    part = added[:, tile * LANES : (tile + 1) * LANES]
                    r["zc"][:, :, 2 * block + tile] = part.reshape(2, 2, height, LANES)
            return
        wait_for(level, "z")

        def along_x(layer, _):
            for tile in range(tiles):
                lift_rows(zr_flat, (layer * tiles + tile) * height, height)
            lift_rows(ze_flat, layer * height, height)
            return 0

        loop(4, 4, along_x)
        values = [zr[:, :, tile].reshape(4 * height, LANES) for tile in range(tiles)]
        lifted = lift_lanes(values, ze[...].reshape(4 * height, LANES), y_weights[level])
        for tile in range(tiles):
            zr[:, :, tile] = lifted[tile].reshape(2, 2, height, LANES)

    def row_weights(table, layer, at):
        values = none8
        for number, weights in table.items():
            place = at(number)
            if place is not None and weights[layer] != 0.0:
                values = jnp.where(sub == place, weights[layer], values)
        return values

    def add_y(level):
        planes, tiles, height, _ = extent(level)
        body = bodies[level]
        chunk = min(planes, 512 // height)

        def add(number, _):
            where = pl.ds(number * chunk, chunk)
            added = spread_y(level, [number * chunk + inner for inner in range(chunk)], lambda ref: ref[...])
            body[where, 0] = body[where, 0] + added[:, :LANES].reshape(chunk, height, LANES)
            if tiles > 1:
                body[where, tiles - 1] = body[where, tiles - 1] + added[:, LANES:].reshape(chunk, height, LANES)
            return 0

        lax.fori_loop(0, planes // chunk, add, 0)

    def add_x_rows(body, planes, every, height, strips, at):
        tables = ((FROM_LEFT, 0), (FROM_RIGHT, height - 8))
        weigh = [[row_weights(table, layer, at) for layer in range(2)] for table, _ in tables]

        def add(number, _):
            for tile in range(body.shape[1]):
                strip = strips(tile)
                for side in SIDES:
                    part = pl.ds(tables[side][1], 8)
                    first = side * planes + number * every
                    added = weigh[side][0] * strip[pl.ds(first, 1), :]
                    added = added + weigh[side][1] * strip[pl.ds(2 * planes + first, 1), :]
                    body[number, tile, part, :] = body[number, tile, part, :] + added
            return 0

        loop(planes // every, 4, add)

    def add_x(level):
        planes, _, height, _ = extent(level)
        xl = held[level]["xl"]
        add_x_rows(bodies[level], planes, 1, height, lambda tile: xl.at[tile], lambda number: number % 8)

    def add_z(level):
        planes, tiles, _, _ = extent(level)
        body, zr = bodies[level], held[level]["zr"]
        if level == 0:
            wait_for(0, "z")
            for side in SIDES:
                for k in range(2):
                    for tile in range(tiles):
                        zr[side, k, tile] = zr[side, k, tile] + held[0]["zc"][side, k, tile]
        for side, table in ((0, FROM_LEFT), (1, FROM_RIGHT)):
            for number, (one, two) in table.items():
                plane = number % planes
                for tile in range(tiles):
                    added = one * zr[side, 0, tile]
                    if two != 0.0:
                        added = added + two * zr[side, 1, tile]
                    body[plane, tile] = body[plane, tile] + added

    start(0)
    own_x(0)
    own_z(0, 0)
    planes, tiles, height, _ = extent(0)
    half, deep = height // 2, planes // 2
    inner, inner_tiles = bodies[1], tiles // 2
    flat = flat_of(bodies[0])
    tops = list(range(0, planes, 2))

    def low_rows(ref_flat, start_of):
        return ref_flat[pl.ds(start_of, half, stride=2), :]

    values = [
        jnp.concatenate([low_rows(flat, (plane * tiles + tile) * height) for plane in tops], axis=0)
        for tile in range(tiles)
    ]
    lifted = lift_lanes(values, jnp.zeros((deep * half, LANES), f32), y_weights[0])
    for tile, packed in enumerate(pack_tiles(0, lifted)):
        inner[:, tile] = packed.reshape(deep, half, LANES)

    wait_for(0, "y")
    prepare_y(0)
    added = spread_y(0, tops, lambda ref: ref[pl.ds(0, half, stride=2), :])
    keep = (lax.broadcasted_iota(jnp.int32, (deep * half, LANES), 1) & 1) == 0
    first = jnp.where(keep, added[:, :LANES], 0.0)
    last = jnp.where(keep, 0.0, pltpu.roll(added[:, LANES:], 1, 1))
    inner[:, 0] = inner[:, 0] + first.reshape(deep, half, LANES)
    inner[:, inner_tiles - 1] = inner[:, inner_tiles - 1] + last.reshape(deep, half, LANES)

    wait_for(0, "x")
    prepare_x(0)
    xl, xp = held[0]["xl"], take()
    for tile, packed in enumerate(pack_tiles(0, [xl[tile] for tile in range(tiles)])):
        xp[tile] = packed

    def even_row(number):
        return (number % 16) // 2 % 8 if number % 2 == 0 else None

    add_x_rows(inner, planes, 2, half, lambda tile: xp.at[tile], even_row)
    prepare_z(0)
    zc_flat = flat_of(held[0]["zc"])
    packed_layers = [pack_tiles(0, low_tiles(zc_flat, layer)) for layer in range(4)]
    wait_for(0, "zlow")
    for side, table in ((0, FROM_LEFT), (1, FROM_RIGHT)):
        packed = [
            [held[0]["zlowr"][side, k, tile] + packed_layers[2 * side + k][tile] for tile in range(inner_tiles)]
            for k in range(2)
        ]
        for number, (one, two) in table.items():
            if number % 2 == 0:
                plane = (number % planes) // 2
                for tile in range(inner_tiles):
                    added = one * packed[0][tile]
                    if two != 0.0:
                        added = added + two * packed[1][tile]
                    inner[plane, tile] = inner[plane, tile] + added

    start(1)
    make_weights(1)
    own_x(1)
    own_z(1)
    own_y(1)
    own_z(0, 1)
    own_y(0, 0, 1, True)
    wait_for(1, "y")
    prepare_y(1)
    add_y(1)
    wait_for(1, "x")
    prepare_x(1)
    add_x(1)
    prepare_z(1)
    add_z(1)
    planes, tiles, height, _ = extent(1)
    half = height // 2
    flat = flat_of(bodies[1])

    def pick(plane, _):
        values = [flat[pl.ds((2 * plane * tiles + tile) * height, half, stride=2), :] for tile in range(tiles)]
        for tile, packed in enumerate(pack_tiles(1, values)):
            bodies[2][plane, tile] = packed
        return 0

    loop(planes // 2, 4, pick)

    start(2)
    make_weights(2)
    own_x(2)
    own_z(2)
    own_y(2)
    own_y(0, 1, None, True)
    add_x(0)
    add_z(0)
    wait_for(2, "y")
    prepare_y(2)
    add_y(2)
    wait_for(2, "x")
    prepare_x(2)
    add_x(2)
    prepare_z(2)
    add_z(2)

    planes, tiles, height, _ = extent(1)
    half = height // 2

    def place(plane, _):
        where = [pl.ds((2 * plane * tiles + tile) * height, half, stride=2) for tile in range(tiles)]
        inner = [bodies[2][plane, tile] for tile in range(tiles // 2)]
        for at, values in zip(where, unpack_tiles(1, [flat[at, :] for at in where], inner)):
            flat[at, :] = values
        return 0

    loop(planes // 2, 4, place)

    for level in range(LEVELS):
        wait_rows(send_sem.at[level], sent[level])


def write_out(held_ref, inner_ref, out_ref, merged, sem):
    depth, tiles, rows, _ = held_ref.shape
    planes, half = depth // 2, rows // 2
    pairs = held_ref.reshape(planes, 2, tiles, rows, LANES)
    target = out_ref.reshape(planes, 2, rows, tiles * LANES)
    parts = sem.shape[0] - 1
    size = planes // parts

    def copy(source, odd, tile, slot, where):
        return pltpu.make_async_copy(
            source, target.at[where, odd, :, pl.ds(tile * LANES, LANES)], sem.at[slot, tile]
        )

    copies = [copy(pairs.at[:, 1, tile], 1, tile, parts, pl.ds(0, planes)) for tile in range(tiles)]
    for one in copies:
        one.start()
    held_flat = held_ref.reshape(depth * tiles * rows, LANES)
    merged_flat = merged.reshape(planes * tiles * rows, LANES)

    def place(plane, _):
        source = [2 * plane * tiles * rows + tile * rows for tile in range(tiles)]
        target = [plane * tiles * rows + tile * rows for tile in range(tiles)]
        low = [held_flat[pl.ds(start, half, stride=2), :] for start in source]
        inner = [inner_ref[plane, tile] for tile in range(tiles // 2)]
        for tile, values in enumerate(unpack_tiles(0, low, inner)):
            merged_flat[pl.ds(target[tile], half, stride=2), :] = values
            odd = held_flat[pl.ds(source[tile] + 1, half, stride=2), :]
            merged_flat[pl.ds(target[tile] + 1, half, stride=2), :] = odd
        return 0

    for part in range(parts):
        loop(size, 4, lambda number, _: place(part * size + number, _))
        for tile in range(tiles):
            where = pl.ds(part * size, size)
            copies.append(copy(merged.at[where, tile], 0, tile, part, where))
            copies[-1].start()
    for one in copies:
        one.wait()


def local(field):
    depth, rows, lanes = field.shape
    vmem = pltpu.VMEM
    sizes = [(depth >> level, TILES >> level, rows >> level) for level in range(LEVELS)]
    scratch = [vmem((planes, tiles, height, LANES), f32) for planes, tiles, height in sizes[2:]]
    scratch += [
        pltpu.SemaphoreType.DMA((3, TILES)),
        pltpu.SemaphoreType.DMA((LEVELS,)),
        pltpu.SemaphoreType.DMA((LEVELS, 5)),
    ]
    widths = [min(tiles, 2) * LANES for _, tiles, _ in sizes]
    scratch += [vmem((3 * (width + LANES), width), bf16) for width in widths]
    scratch += [vmem((6 * LANES, width), bf16) for width in widths]
    scratch += [vmem((3 * LANES, LANES), bf16) for _ in sizes]
    for planes, tiles, height in sizes:
        shapes = [(2, 2, tiles, height)] * 2 + [(2, 2, height)]
        shapes += [(2, planes, 8)] * 3 + [(tiles, 4 * planes)]
        shapes += [(2, 2, 2, 8)] * 2 + [(2, height)] * 2 + [(2, 2, height)]
        shapes += [(2, 2, 8)] * 4 + [(2, 2, 2, 2, 8)]
        scratch += [vmem((*shape, LANES), f32) for shape in shapes]
    scratch += [vmem((2, 2, TILES, rows, LANES), f32)] * 2 + [vmem((2, 2, TILES // 2, rows // 2, LANES), f32)] * 2
    scratch += [vmem((TILES // 2, 4 * depth, LANES), f32)]
    lifted = pl.pallas_call(
        functools.partial(kernel, field.shape),
        out_shape=[jax.ShapeDtypeStruct((size[0], size[1], size[2], LANES), f32) for size in sizes[:2]],
        in_specs=[pl.BlockSpec(memory_space=pltpu.HBM)],
        out_specs=[pl.BlockSpec(memory_space=pltpu.VMEM)] * 2,
        scratch_shapes=scratch,
        compiler_params=pltpu.CompilerParams(
            collective_id=0, has_side_effects=True, vmem_limit_bytes=48 * 2**20
        ),
        name="lift",
    )(field)
    return pl.pallas_call(
        write_out,
        out_shape=jax.ShapeDtypeStruct(field.shape, f32),
        in_specs=[pl.BlockSpec(memory_space=pltpu.VMEM)] * 2,
        out_specs=pl.BlockSpec(memory_space=pltpu.HBM),
        scratch_shapes=[
            vmem((depth // 2, TILES, rows, LANES), f32),
            pltpu.SemaphoreType.DMA((3, TILES)),
        ],
        compiler_params=pltpu.CompilerParams(vmem_limit_bytes=8 * 2**20),
        name="write_out",
    )(*lifted)


def solution(mesh):
    placed = (P("gz", "gx", "gy"),)
    return jax.shard_map(
        local, mesh=mesh, in_specs=placed, out_specs=P("gz", "gx", "gy"), check_vma=False
    )
```

```python
import functools

import jax
import jax.numpy as jnp
import numpy as np
from jax import lax
from jax.experimental import pallas as pl
from jax.experimental.pallas import tpu as pltpu
from jax.sharding import PartitionSpec as P

A = -1.586134342
B = -0.05298011854
G = 0.8829110762
E = 0.4435068522
Z = 1.149604398
MESH = pl.DeviceIdType.MESH
LANES = 128
TILES = 4
LEVELS = 3
SIDES = (0, 1)
f32, bf16 = jnp.float32, jnp.bfloat16


def filter_taps():
    u = np.eye(64)
    s, d = u[0::2].copy(), u[1::2].copy()
    d += A * (s + np.roll(s, -1, 0))
    s += B * (np.roll(d, 1, 0) + d)
    d += G * (s + np.roll(s, -1, 0))
    s += E * (np.roll(d, 1, 0) + d)
    low, high = s[16] * Z, d[16] / Z
    return [float(low[32 + o]) for o in range(5)], [float(high[33 + o]) for o in range(5)]


LOW, HIGH = filter_taps()

FROM_LEFT = {
    0: (Z * (B + E * (1 + 3 * G * B)), Z * E * G),
    1: (G * B / Z, 0.0),
    2: (Z * E * G * B, 0.0),
}
FROM_RIGHT = {
    -4: (Z * E * G * B * A, 0.0),
    -3: (G * B * A / Z, 0.0),
    -2: (Z * (B * A + E * (G * B * A + A * (1 + 2 * G * B))), Z * E * G),
    -1: (A * (1 + 2 * G * B) / Z, G / Z),
}


def cell_of(level, tile, lane):
    if level == 0:
        return tile * LANES + lane
    if level == 1:
        turn = lane & 1
        return ((tile + 2 * turn) * LANES + lane - turn) >> 1
    turn = lane & 3
    return (((turn >> 1) + 2 * (turn & 1)) * LANES + lane - turn) >> 2


def tap_weights(position, target):
    apart = jnp.abs(position - target)
    low = jnp.zeros(position.shape, f32)
    high = jnp.zeros(position.shape, f32)
    for o in range(5):
        low = jnp.where(apart == o, LOW[o], low)
        if o < 4:
            high = jnp.where(apart == o, HIGH[o], high)
    return jnp.where((target & 1) == 0, low, high)


def parts_of(values):
    top = values.astype(bf16)
    return top, (values - top.astype(f32)).astype(bf16)


def encode_end(s2, d2, s1, d1):
    return d1 + A * s1, s1 + B * (d2 + A * (s2 + s1))


def encode_start(s0, d0, s1):
    return s0, s0 + B * (d0 + A * (s0 + s1))


def lift_list(u, halo=None):
    s, d = list(u[0::2]), list(u[1::2])
    count = len(s)
    d_before = A * s[0]
    if halo is not None:
        d_before = d_before + halo[0]
    s_before = B * d_before
    if halo is not None:
        s_before = s_before + halo[1]
    for i in range(count - 1):
        d[i] = d[i] + A * (s[i] + s[i + 1])
    last = s[-1] if halo is None else s[-1] + halo[2]
    d[-1] = d[-1] + A * last
    s_after = B * d[-1]
    if halo is not None:
        s_after = s_after + halo[3]
    around = [d_before] + d
    s = [s[i] + B * (around[i] + around[i + 1]) for i in range(count)]
    d_before = d_before + G * (s_before + s[0])
    around = s + [s_after]
    d = [d[i] + G * (around[i] + around[i + 1]) for i in range(count)]
    around = [d_before] + d
    s = [s[i] + E * (around[i] + around[i + 1]) for i in range(count)]
    out = []
    for i in range(count):
        out += [s[i] * Z, d[i] * (1.0 / Z)]
    return out


def lift_rows(flat, start, height):
    half = height // 2
    pair = lax.broadcasted_iota(jnp.int32, (half, LANES), 0)
    even, odd = pl.ds(start, half, stride=2), pl.ds(start + 1, half, stride=2)
    s, d = flat[even, :], flat[odd, :]

    def after(values, last):
        return jnp.where(pair == half - 1, last, pltpu.roll(values, half - 1, 0))

    def before(values, first):
        return jnp.where(pair == 0, first, pltpu.roll(values, 1, 0))

    d_before = A * s[:1]
    d = d + A * (s + after(s, 0.0))
    s_after = B * d[half - 1 :]
    s_before = B * d_before
    s = s + B * (before(d, d_before) + d)
    d_before = d_before + G * (s_before + s[:1])
    d = d + G * (s + after(s, s_after))
    s = s + E * (before(d, d_before) + d)
    flat[even, :] = s * Z
    flat[odd, :] = d * (1.0 / Z)


def pack_tiles(level, tiles):
    lane = lax.broadcasted_iota(jnp.int32, tiles[0].shape, 1)
    step = 2**level
    keep = lane & (2 * step - 1) < step
    half = len(tiles) // 2
    return [jnp.where(keep, tiles[i], pltpu.roll(tiles[i + half], step, 1)) for i in range(half)]


def unpack_tiles(level, tiles, inner):
    lane = lax.broadcasted_iota(jnp.int32, tiles[0].shape, 1)
    step = 2**level
    keep = lane & (2 * step - 1) < step
    inner = list(inner) + [pltpu.roll(tile, LANES - step, 1) for tile in inner]
    return [jnp.where(keep, new, old) for new, old in zip(inner, tiles)]


def lift_lanes(tiles, ext, weights):
    first = lax.broadcasted_iota(jnp.int32, tiles[0].shape, 1) < LANES // 2
    blocks = [(tiles, ext)]
    if len(tiles) == 4:
        blocks = [(tiles[:2], jnp.where(first, tiles[2], ext)), (tiles[2:], jnp.where(first, ext, tiles[1]))]
    out = []
    for main, beside in blocks:
        main_top, main_low = parts_of(jnp.concatenate(main, axis=1))
        side_top, side_low = parts_of(beside)
        stacked = jnp.concatenate([main_top, main_low, main_top, side_top, side_low, side_top], axis=1)
        result = jnp.dot(stacked, weights[...], preferred_element_type=f32)
        out += [result[:, i * LANES : (i + 1) * LANES] for i in range(len(main))]
    return out


def loop(count, unroll, body, carry=0):
    unroll = min(unroll, count)

    def turns(number, carried):
        for inner in range(unroll):
            carried = body(number * unroll + inner, carried)
        return carried

    return lax.fori_loop(0, count // unroll, turns, carry)


NAMES = ("zs", "zr", "ze", "xs", "xr", "xe", "xl", "es", "er", "ys", "yr", "yp", "zys", "zyr", "xys", "xyr", "cr")
GROUPS = {"y": 0, "x": 1, "e": 1, "c": 1, "xy": 1, "zy": 2, "z": 3, "zlow": 4}
FIRST_NAMES = ("zl", "zc", "zlow", "zlowr")


def kernel(shape, field_ref, out_ref, inner_ref, *scratch):
    depth, rows, _ = shape
    refs = list(scratch)
    take = lambda: refs.pop(0)
    bodies = [out_ref, inner_ref, take()]
    load_sem, send_sem, recv_sem = take(), take(), take()
    y_weights, far_weights, z_weights = [[take() for _ in range(LEVELS)] for _ in range(3)]
    held = [{name: take() for name in NAMES} for _ in range(LEVELS)]
    held[0].update({name: take() for name in FIRST_NAMES})

    here = {name: lax.axis_index(name) for name in ("gx", "gy", "gz")}
    count = {name: lax.axis_size(name) for name in ("gx", "gy", "gz")}

    near = {
        name: {-1: lax.rem(at + count[name] - 1, count[name]), 0: at, 1: lax.rem(at + 1, count[name])}
        for name, at in here.items()
    }

    def beside(**by):
        return {name: near[name][way] for name, way in by.items()}

    loads = [
        [
            pltpu.make_async_copy(
                field_ref.at[pl.ds(first, size), :, pl.ds(tile * LANES, LANES)],
                out_ref.at[pl.ds(first, size), tile],
                load_sem.at[number, tile],
            )
            for tile in range(TILES)
        ]
        for number, (first, size) in enumerate(((0, 4), (depth - 4, 4), (4, depth - 8)))
    ]
    for part in loads[:2]:
        for load in part:
            load.start()
    barrier = pltpu.get_barrier_semaphore()
    for x in (-1, 0, 1):
        for y in (-1, 0, 1):
            for z in (-1, 0, 1):
                if (x, y, z) != (0, 0, 0):
                    pl.semaphore_signal(barrier, inc=1, device_id=beside(gx=x, gy=y, gz=z), device_id_type=MESH)
    for load in loads[2]:
        load.start()

    def fill(ref, blocks):
        start = 0
        for values in blocks:
            top, low = parts_of(values)
            size = values.shape[0]
            for part in (top, top, low):
                ref[start : start + size] = part
                start += size

    def make_weights(level):
        window = 4 << level
        tiles = TILES >> level
        cells = (TILES * LANES) >> level
        width = min(tiles, 2) * LANES
        row = lax.broadcasted_iota(jnp.int32, (2 * LANES, width), 0)
        col = lax.broadcasted_iota(jnp.int32, (2 * LANES, width), 1)
        target = cell_of(level, col >> 7, col & 127)
        main = row[:width]
        side = row[:LANES]
        after, before = (2 * LANES, -LANES) if level == 0 else (cells, -cells)
        right = cell_of(level, 0, side) + after
        left = cell_of(level, 0 if level == 0 else tiles - 1, side) + before
        position = jnp.where(side < LANES // 2, right, left)
        fill(
            y_weights[level],
            [
                tap_weights(cell_of(level, main >> 7, main & 127), target[:width]),
                tap_weights(position, target[:LANES]),
            ],
        )
        inside = row & (window - 1)
        left = cell_of(level, tiles - 1, LANES - window + inside) - cells
        right = cell_of(level, 0, inside) + cells
        position = jnp.where(row < LANES, left, right)
        last = cell_of(level, tiles - 1, col & 127)
        target = jnp.where(col < LANES, cell_of(level, 0, col & 127), last)
        fill(far_weights[level], [tap_weights(position, target)])
        shift = 2 + level
        row, col = row[:LANES, :LANES], col[:LANES, :LANES]
        taps = tap_weights(row >> shift, col >> shift)
        fill(z_weights[level], [jnp.where((row & (window - 1)) == (col & (window - 1)), taps, 0.0)])

    make_weights(0)
    for part in loads[:2]:
        for load in part:
            load.wait()

    sent = [0] * LEVELS
    arriving = [[0] * 5 for _ in range(LEVELS)]
    way = (1, -1)
    sub = lax.broadcasted_iota(jnp.int32, (8, LANES), 0)
    lane8 = lax.broadcasted_iota(jnp.int32, (8, LANES), 1)
    last_half = lane8 >= LANES // 2
    none8 = jnp.zeros((8, LANES), f32)

    def extent(level):
        return depth >> level, TILES >> level, rows >> level, 4 << level

    def flat_of(ref):
        size = 1
        for extent_of_dim in ref.shape[:-1]:
            size *= extent_of_dim
        return ref.reshape(size, LANES)

    def wait_rows(sem, count):
        held_rows = flat_of(out_ref).at[pl.ds(0, count)]
        pltpu.make_async_copy(held_rows, held_rows, sem).wait()

    def wait_for(level, key):
        wait_rows(recv_sem.at[level, GROUPS[key]], arriving[level][GROUPS[key]])

    def lift_layers(layers, low):
        _, tiles, height, _ = extent(0)
        layers_flat = flat_of(layers)

        def along_x(layer, _):
            for tile in range(tiles):
                lift_rows(layers_flat, (layer * tiles + tile) * height, height)
            return 0

        loop(4, 4, along_x)
        values = [layers[:, :, tile].reshape(4 * height, LANES) for tile in range(tiles)]
        lifted = lift_lanes(values, jnp.zeros((4 * height, LANES), f32), y_weights[0])
        for tile in range(tiles):
            layers[:, :, tile] = lifted[tile].reshape(2, 2, height, LANES)
        for layer in range(4):
            for tile, packed in enumerate(pack_tiles(0, low_tiles(layers_flat, layer))):
                low[layer // 2, layer % 2, tile] = packed

    def low_tiles(layers_flat, layer):
        _, tiles, height, _ = extent(0)
        return [
            layers_flat[pl.ds((layer * tiles + tile) * height, height // 2, stride=2), :] for tile in range(tiles)
        ]

    def start(level):
        planes, tiles, height, window = extent(level)
        body, flat, r = bodies[level], flat_of(bodies[level]), held[level]
        shift = 2 + level

        def send(key, source, target, **by):
            copy = pltpu.make_async_remote_copy(
                src_ref=source,
                dst_ref=target,
                send_sem=send_sem.at[level],
                recv_sem=recv_sem.at[level, GROUPS[key]],
                device_id=beside(**by),
                device_id_type=MESH,
            )
            if level == 0 and not sent[0]:
                pl.semaphore_wait(barrier, 26)
            copy.start()
            size = 1
            for extent_of_dim in source.shape[:-1]:
                size *= extent_of_dim
            sent[level] += size
            arriving[level][GROUPS[key]] += size

        zs, xs, es = r["zs"], r["xs"], r["es"]
        for tile in range(tiles):
            end = encode_end(*[body[planes - 4 + number, tile] for number in range(4)])
            begin = encode_start(*[body[number, tile] for number in range(3)])
            for k in range(2):
                zs[0, k, tile] = end[k]
                zs[1, k, tile] = begin[k]
                if level == 0:
                    r["zl"][0, k, tile] = end[k]
                    r["zl"][1, k, tile] = begin[k]
        if level == 0:
            lift_layers(r["zl"], r["zlow"])
            for side in SIDES:
                send("zlow", r["zlow"].at[side], r["zlowr"].at[side], gz=way[side])
            for load in loads[2]:
                load.wait()
        else:
            for side in SIDES:
                send("z", zs.at[side], r["zr"].at[side], gz=way[side])

        xs_flat = flat_of(xs)
        for tile in range(tiles):
            def at(number):
                return flat[pl.ds(tile * height + number, planes, stride=tiles * height), :]

            end = encode_end(*[at(height - 4 + number) for number in range(4)])
            begin = encode_start(*[at(number) for number in range(3)])
            for k in range(2):
                xs_flat[pl.ds(k * tiles + tile, planes, stride=8), :] = end[k]
                xs_flat[pl.ds(planes * 8 + k * tiles + tile, planes, stride=8), :] = begin[k]
        for side in SIDES:
            send("x", xs.at[side], r["xr"].at[side], gx=way[side])

        for side in SIDES:
            end = encode_end(*[xs[side, planes - 4 + number] for number in range(4)])
            begin = encode_start(*[xs[side, number] for number in range(3)])
            for k in range(2):
                es[side, 0, k] = end[k]
                es[side, 1, k] = begin[k]
        for sx in SIDES:
            for sz in SIDES:
                send("e", es.at[sx, sz], r["er"].at[sx, sz], gx=way[sx], gz=way[sz])
                for sy in SIDES:
                    send("c", es.at[sx, sz], r["cr"].at[sx, sz, sy], gx=way[sx], gz=way[sz], gy=way[sy])

        lane = lax.broadcasted_iota(jnp.int32, (height, LANES), 1)

        def pack(plane, carried):
            to_right, to_left, x_right, x_left = carried
            tail_by = lax.rem(plane * window + window, LANES)
            head_by = plane * window
            mine = lane >> shift == plane
            to_right = jnp.where(mine, pltpu.roll(body[plane, tiles - 1], tail_by, 1), to_right)
            to_left = jnp.where(mine, pltpu.roll(body[plane, 0], head_by, 1), to_left)
            mine = lane8 >> shift == plane
            x_right = tuple(jnp.where(mine, pltpu.roll(xs[sx, plane], tail_by, 1), x_right[sx]) for sx in SIDES)
            x_left = tuple(jnp.where(mine, pltpu.roll(xs[sx, plane], head_by, 1), x_left[sx]) for sx in SIDES)
            return to_right, to_left, x_right, x_left

        none = jnp.zeros((height, LANES), f32)
        to_right, to_left, x_right, x_left = loop(
            planes, 4, pack, (none, none, (none8, none8), (none8, none8))
        )
        r["ys"][0], r["ys"][1] = to_right, to_left
        for sx in SIDES:
            r["xys"][0, sx], r["xys"][1, sx] = x_right[sx], x_left[sx]
        groups = height // 8
        for sz in SIDES:
            tail = head = none8
            for k in range(2):
                for group in range(groups):
                    slot = k * groups + group
                    mine = lane8 >> shift == slot
                    part = pl.ds(group * 8, 8)
                    by = (slot * window + window) % LANES
                    tail = jnp.where(mine, pltpu.roll(zs[sz, k, tiles - 1, part, :], by, 1), tail)
                    head = jnp.where(mine, pltpu.roll(zs[sz, k, 0, part, :], slot * window, 1), head)
            r["zys"][0, sz], r["zys"][1, sz] = tail, head
        for sy in SIDES:
            send("y", r["ys"].at[sy], r["yr"].at[sy], gy=way[sy])
            for s in SIDES:
                send("xy", r["xys"].at[sy, s], r["xyr"].at[sy, s], gy=way[sy], gx=way[s])
                send("zy", r["zys"].at[sy, s], r["zyr"].at[sy, s], gy=way[sy], gz=way[s])
        if level == 0:
            for side in SIDES:
                send("z", r["zl"].at[side], r["zr"].at[side], gz=way[side])

    def own_x(level):
        planes, tiles, height, _ = extent(level)
        flat = flat_of(bodies[level])

        def along_x(plane, _):
            for tile in range(tiles):
                lift_rows(flat, (plane * tiles + tile) * height, height)
            return 0

        loop(planes, 4, along_x)

    def own_z(level, parity=None):
        planes, tiles, height, _ = extent(level)
        flat = flat_of(bodies[level])
        every = 1 if parity is None else 2
        groups = height // (8 * every)

        def along_z(block, _):
            tile, group = block // groups, block % groups
            first = tile * height + group * 8 * every
            if parity is None:
                first = pl.multiple_of(first, 8)
                where = [pl.ds(first + plane * tiles * height, 8) for plane in range(planes)]
            else:
                where = [pl.ds(first + parity + plane * tiles * height, 8, stride=2) for plane in range(planes)]
            lifted = lift_list([flat[at, :] for at in where])
            for at, values in zip(where, lifted):
                flat[at, :] = values
            return 0

        loop(tiles * groups, 1 if level == 0 else 2, along_z)

    def own_y(level, start=0, stop=None):
        planes, tiles, height, _ = extent(level)
        body = bodies[level]
        chunk = min(planes, 512 // height)

        def halos(plane):
            yp = held[level]["yp"]
            window = 4 << level
            left = pltpu.roll(yp[0, 0] + yp[1, 0], lax.rem(2 * LANES - window - plane * window, LANES), 1)
            right = pltpu.roll(yp[0, 1] + yp[1, 1], lax.rem(LANES - plane * window, LANES), 1)
            return jnp.where(lax.broadcasted_iota(jnp.int32, (height, LANES), 1) >= LANES // 2, left, right)

        def along_y(number, _):
            where = pl.ds(number * chunk, chunk)
            values = [body[where, tile].reshape(chunk * height, LANES) for tile in range(tiles)]
            ext = jnp.concatenate([halos(number * chunk + inner) for inner in range(chunk)], axis=0)
            lifted = lift_lanes(values, ext, y_weights[level])
            for tile in range(tiles):
                body[where, tile] = lifted[tile].reshape(chunk, height, LANES)
            return 0

        lax.fori_loop(start, planes // chunk if stop is None else stop, along_y, 0)

    def prepare_y(level):
        height = extent(level)[2]
        r = held[level]
        for sy in SIDES:
            lift_rows(r["yr"].at[sy], 0, height)
            top, low = parts_of(r["yr"][sy])
            stacked = jnp.concatenate([top, low, top], axis=1)
            values = jnp.dot(stacked, z_weights[level][...], preferred_element_type=f32)
            top = values.astype(bf16).astype(f32)
            r["yp"][0, sy] = top
            r["yp"][1, sy] = values - top

    def spread_y(level, planes, pick):
        height = extent(level)[2]
        shift = 2 + level
        yp = held[level]["yp"]
        parts = [[pick(yp.at[part, sy]) for sy in SIDES] for part in range(2)]
        lane = lax.broadcasted_iota(jnp.int32, parts[0][0].shape, 1)
        stacks = []
        for plane in planes:
            mine = lane >> shift == plane
            top, low = [[jnp.where(mine, values, 0.0).astype(bf16) for values in part] for part in parts]
            stacks.append(jnp.concatenate(top + low + top, axis=1))
        return jnp.dot(jnp.concatenate(stacks, axis=0), far_weights[level][...], preferred_element_type=f32)

    def prepare_x(level):
        planes, tiles, height, window = extent(level)
        r = held[level]
        xr, xe, xl = r["xr"], r["xe"], r["xl"]

        def aligned(values):
            return pltpu.roll(values, 9 - tiles, 0) if tiles > 1 else values

        lefts = [aligned(r["xyr"][0, sx]) for sx in SIDES]
        rights = [r["xyr"][1, sx] for sx in SIDES]

        def unpack(plane, _):
            left_by = lax.rem(2 * LANES - window - plane * window, LANES)
            right_by = lax.rem(LANES - plane * window, LANES)
            for sx in SIDES:
                xe[sx, plane] = jnp.where(
                    last_half, pltpu.roll(lefts[sx], left_by, 1), pltpu.roll(rights[sx], right_by, 1)
                )
            return 0

        loop(planes, 8, unpack)
        for sx in SIDES:
            halo = [r["er"][sx, sz, k] for sz in SIDES for k in range(2)]
            lifted = lift_list([xr[sx, plane] for plane in range(planes)], halo)
            for plane in range(planes):
                xr[sx, plane] = lifted[plane]
            halo = [
                jnp.where(last_half, aligned(r["cr"][sx, sz, 0, k]), r["cr"][sx, sz, 1, k])
                for sz in SIDES
                for k in range(2)
            ]
            lifted = lift_list([xe[sx, plane] for plane in range(planes)], halo)
            for plane in range(planes):
                xe[sx, plane] = lifted[plane]
        xr_flat, xe_flat = flat_of(xr), flat_of(xe)

        def strip(ref, start):
            return ref[pl.ds(start, 2 * planes, stride=8), :]

        values = [
            jnp.concatenate([strip(xr_flat, k * tiles + tile) for k in range(2)], axis=0) for tile in range(tiles)
        ]
        ext = jnp.concatenate([strip(xe_flat, k * tiles) for k in range(2)], axis=0)
        lifted = lift_lanes(values, ext, y_weights[level])
        for tile in range(tiles):
            xl[tile] = lifted[tile]

    def prepare_z(level):
        planes, tiles, height, window = extent(level)
        r = held[level]
        zr, ze = r["zr"], r["ze"]
        zr_flat, ze_flat = flat_of(zr), flat_of(ze)
        groups = height // 8
        wait_for(level, "zy")
        for sz in SIDES:
            for k in range(2):
                for group in range(groups):
                    slot = k * groups + group
                    left = pltpu.roll(r["zyr"][0, sz], (2 * LANES - window - slot * window) % LANES, 1)
                    right = pltpu.roll(r["zyr"][1, sz], (LANES - slot * window) % LANES, 1)
                    ze[sz, k, pl.ds(group * 8, 8), :] = jnp.where(last_half, left, right)
        if level == 0:
            for layer in range(4):
                lift_rows(ze_flat, layer * height, height)
            ext = ze[...].reshape(4 * height, LANES)
            first = lax.broadcasted_iota(jnp.int32, ext.shape, 1) < LANES // 2
            side_weights = y_weights[0][6 * LANES :]
            for block in range(2):
                top, low = parts_of(jnp.where(first, 0.0, ext) if block == 0 else jnp.where(first, ext, 0.0))
                stacked = jnp.concatenate([top, low, top], axis=1)
                added = jnp.dot(stacked, side_weights, preferred_element_type=f32)
                for tile in range(2):
                    part = added[:, tile * LANES : (tile + 1) * LANES]
                    r["zc"][:, :, 2 * block + tile] = part.reshape(2, 2, height, LANES)
            return
        wait_for(level, "z")

        def along_x(layer, _):
            for tile in range(tiles):
                lift_rows(zr_flat, (layer * tiles + tile) * height, height)
            lift_rows(ze_flat, layer * height, height)
            return 0

        loop(4, 4, along_x)
        values = [zr[:, :, tile].reshape(4 * height, LANES) for tile in range(tiles)]
        lifted = lift_lanes(values, ze[...].reshape(4 * height, LANES), y_weights[level])
        for tile in range(tiles):
            zr[:, :, tile] = lifted[tile].reshape(2, 2, height, LANES)

    def row_weights(table, layer, at):
        values = none8
        for number, weights in table.items():
            place = at(number)
            if place is not None and weights[layer] != 0.0:
                values = jnp.where(sub == place, weights[layer], values)
        return values

    def add_x_rows(body, planes, every, height, strips, at):
        tables = ((FROM_LEFT, 0), (FROM_RIGHT, height - 8))
        weigh = [[row_weights(table, layer, at) for layer in range(2)] for table, _ in tables]

        def add(number, _):
            for tile in range(body.shape[1]):
                strip = strips(tile)
                for side in SIDES:
                    part = pl.ds(tables[side][1], 8)
                    first = side * planes + number * every
                    added = weigh[side][0] * strip[pl.ds(first, 1), :]
                    added = added + weigh[side][1] * strip[pl.ds(2 * planes + first, 1), :]
                    body[number, tile, part, :] = body[number, tile, part, :] + added
            return 0

        loop(planes // every, 4, add)

    def add_x(level):
        planes, _, height, _ = extent(level)
        xl = held[level]["xl"]
        add_x_rows(bodies[level], planes, 1, height, lambda tile: xl.at[tile], lambda number: number % 8)

    def add_z(level):
        planes, tiles, _, _ = extent(level)
        body, zr = bodies[level], held[level]["zr"]
        if level == 0:
            wait_for(0, "z")
            for side in SIDES:
                for k in range(2):
                    for tile in range(tiles):
                        zr[side, k, tile] = zr[side, k, tile] + held[0]["zc"][side, k, tile]
        for side, table in ((0, FROM_LEFT), (1, FROM_RIGHT)):
            for number, (one, two) in table.items():
                plane = number % planes
                for tile in range(tiles):
                    added = one * zr[side, 0, tile]
                    if two != 0.0:
                        added = added + two * zr[side, 1, tile]
                    body[plane, tile] = body[plane, tile] + added

    start(0)
    own_x(0)
    own_z(0, 0)
    planes, tiles, height, _ = extent(0)
    half, deep = height // 2, planes // 2
    inner, inner_tiles = bodies[1], tiles // 2
    flat = flat_of(bodies[0])
    tops = list(range(0, planes, 2))

    def low_rows(ref_flat, start_of):
        return ref_flat[pl.ds(start_of, half, stride=2), :]

    values = [
        jnp.concatenate([low_rows(flat, (plane * tiles + tile) * height) for plane in tops], axis=0)
        for tile in range(tiles)
    ]
    lifted = lift_lanes(values, jnp.zeros((deep * half, LANES), f32), y_weights[0])
    for tile, packed in enumerate(pack_tiles(0, lifted)):
        inner[:, tile] = packed.reshape(deep, half, LANES)

    wait_for(0, "y")
    prepare_y(0)
    added = spread_y(0, tops, lambda ref: ref[pl.ds(0, half, stride=2), :])
    keep = (lax.broadcasted_iota(jnp.int32, (deep * half, LANES), 1) & 1) == 0
    first = jnp.where(keep, added[:, :LANES], 0.0)
    last = jnp.where(keep, 0.0, pltpu.roll(added[:, LANES:], 1, 1))
    inner[:, 0] = inner[:, 0] + first.reshape(deep, half, LANES)
    inner[:, inner_tiles - 1] = inner[:, inner_tiles - 1] + last.reshape(deep, half, LANES)

    wait_for(0, "x")
    prepare_x(0)
    xl, xp = held[0]["xl"], take()
    for tile, packed in enumerate(pack_tiles(0, [xl[tile] for tile in range(tiles)])):
        xp[tile] = packed

    def even_row(number):
        return (number % 16) // 2 % 8 if number % 2 == 0 else None

    add_x_rows(inner, planes, 2, half, lambda tile: xp.at[tile], even_row)
    prepare_z(0)
    zc_flat = flat_of(held[0]["zc"])
    packed_layers = [pack_tiles(0, low_tiles(zc_flat, layer)) for layer in range(4)]
    wait_for(0, "zlow")
    for side, table in ((0, FROM_LEFT), (1, FROM_RIGHT)):
        packed = [
            [held[0]["zlowr"][side, k, tile] + packed_layers[2 * side + k][tile] for tile in range(inner_tiles)]
            for k in range(2)
        ]
        for number, (one, two) in table.items():
            if number % 2 == 0:
                plane = (number % planes) // 2
                for tile in range(inner_tiles):
                    added = one * packed[0][tile]
                    if two != 0.0:
                        added = added + two * packed[1][tile]
                    inner[plane, tile] = inner[plane, tile] + added

    start(1)
    make_weights(1)
    own_x(1)
    own_z(1)
    own_z(0, 1)
    own_y(0, 0, 1)
    wait_for(1, "y")
    prepare_y(1)
    own_y(1)
    wait_for(1, "x")
    prepare_x(1)
    add_x(1)
    prepare_z(1)
    add_z(1)
    planes, tiles, height, _ = extent(1)
    half = height // 2
    flat = flat_of(bodies[1])

    def pick(plane, _):
        values = [flat[pl.ds((2 * plane * tiles + tile) * height, half, stride=2), :] for tile in range(tiles)]
        for tile, packed in enumerate(pack_tiles(1, values)):
            bodies[2][plane, tile] = packed
        return 0

    loop(planes // 2, 4, pick)

    start(2)
    make_weights(2)
    own_x(2)
    own_z(2)
    own_y(0, 1)
    add_x(0)
    add_z(0)
    wait_for(2, "y")
    prepare_y(2)
    own_y(2)
    wait_for(2, "x")
    prepare_x(2)
    add_x(2)
    prepare_z(2)
    add_z(2)

    planes, tiles, height, _ = extent(1)
    half = height // 2

    def place(plane, _):
        where = [pl.ds((2 * plane * tiles + tile) * height, half, stride=2) for tile in range(tiles)]
        inner = [bodies[2][plane, tile] for tile in range(tiles // 2)]
        for at, values in zip(where, unpack_tiles(1, [flat[at, :] for at in where], inner)):
            flat[at, :] = values
        return 0

    loop(planes // 2, 4, place)

    for level in range(LEVELS):
        wait_rows(send_sem.at[level], sent[level])


def write_out(held_ref, inner_ref, out_ref, merged, sem):
    depth, tiles, rows, _ = held_ref.shape
    planes, half = depth // 2, rows // 2
    pairs = held_ref.reshape(planes, 2, tiles, rows, LANES)
    target = out_ref.reshape(planes, 2, rows, tiles * LANES)
    parts = sem.shape[0] - 1
    size = planes // parts

    def copy(source, odd, tile, slot, where):
        return pltpu.make_async_copy(
            source, target.at[where, odd, :, pl.ds(tile * LANES, LANES)], sem.at[slot, tile]
        )

    copies = [copy(pairs.at[:, 1, tile], 1, tile, parts, pl.ds(0, planes)) for tile in range(tiles)]
    for one in copies:
        one.start()
    held_flat = held_ref.reshape(depth * tiles * rows, LANES)
    merged_flat = merged.reshape(planes * tiles * rows, LANES)

    def place(plane, _):
        source = [2 * plane * tiles * rows + tile * rows for tile in range(tiles)]
        target = [plane * tiles * rows + tile * rows for tile in range(tiles)]
        low = [held_flat[pl.ds(start, half, stride=2), :] for start in source]
        inner = [inner_ref[plane, tile] for tile in range(tiles // 2)]
        for tile, values in enumerate(unpack_tiles(0, low, inner)):
            merged_flat[pl.ds(target[tile], half, stride=2), :] = values
            odd = held_flat[pl.ds(source[tile] + 1, half, stride=2), :]
            merged_flat[pl.ds(target[tile] + 1, half, stride=2), :] = odd
        return 0

    for part in range(parts):
        loop(size, 4, lambda number, _: place(part * size + number, _))
        for tile in range(tiles):
            where = pl.ds(part * size, size)
            copies.append(copy(merged.at[where, tile], 0, tile, part, where))
            copies[-1].start()
    for one in copies:
        one.wait()


def local(field):
    depth, rows, lanes = field.shape
    vmem = pltpu.VMEM
    sizes = [(depth >> level, TILES >> level, rows >> level) for level in range(LEVELS)]
    scratch = [vmem((planes, tiles, height, LANES), f32) for planes, tiles, height in sizes[2:]]
    scratch += [
        pltpu.SemaphoreType.DMA((3, TILES)),
        pltpu.SemaphoreType.DMA((LEVELS,)),
        pltpu.SemaphoreType.DMA((LEVELS, 5)),
    ]
    widths = [min(tiles, 2) * LANES for _, tiles, _ in sizes]
    scratch += [vmem((3 * (width + LANES), width), bf16) for width in widths]
    scratch += [vmem((6 * LANES, width), bf16) for width in widths]
    scratch += [vmem((3 * LANES, LANES), bf16) for _ in sizes]
    for planes, tiles, height in sizes:
        shapes = [(2, 2, tiles, height)] * 2 + [(2, 2, height)]
        shapes += [(2, planes, 8)] * 3 + [(tiles, 4 * planes)]
        shapes += [(2, 2, 2, 8)] * 2 + [(2, height)] * 2 + [(2, 2, height)]
        shapes += [(2, 2, 8)] * 4 + [(2, 2, 2, 2, 8)]
        scratch += [vmem((*shape, LANES), f32) for shape in shapes]
    scratch += [vmem((2, 2, TILES, rows, LANES), f32)] * 2 + [vmem((2, 2, TILES // 2, rows // 2, LANES), f32)] * 2
    scratch += [vmem((TILES // 2, 4 * depth, LANES), f32)]
    lifted = pl.pallas_call(
        functools.partial(kernel, field.shape),
        out_shape=[jax.ShapeDtypeStruct((size[0], size[1], size[2], LANES), f32) for size in sizes[:2]],
        in_specs=[pl.BlockSpec(memory_space=pltpu.HBM)],
        out_specs=[pl.BlockSpec(memory_space=pltpu.VMEM)] * 2,
        scratch_shapes=scratch,
        compiler_params=pltpu.CompilerParams(
            collective_id=0, has_side_effects=True, vmem_limit_bytes=48 * 2**20
        ),
        name="lift",
    )(field)
    return pl.pallas_call(
        write_out,
        out_shape=jax.ShapeDtypeStruct(field.shape, f32),
        in_specs=[pl.BlockSpec(memory_space=pltpu.VMEM)] * 2,
        out_specs=pl.BlockSpec(memory_space=pltpu.HBM),
        scratch_shapes=[
            vmem((depth // 2, TILES, rows, LANES), f32),
            pltpu.SemaphoreType.DMA((3, TILES)),
        ],
        compiler_params=pltpu.CompilerParams(vmem_limit_bytes=8 * 2**20),
        name="write_out",
    )(*lifted)


def solution(mesh):
    placed = (P("gz", "gx", "gy"),)
    return jax.shard_map(
        local, mesh=mesh, in_specs=placed, out_specs=P("gz", "gx", "gy"), check_vma=False
    )
```
